256 devices in a mesh: cast: 8 (over x, core), span: 32 (over z, y).
Axes of the slice: x: 4, y: 4, z: 8, core: 2. Of those that a mesh axis runs over, the one named last changes fastest.
Arguments:
- phase: int32 [16, 128, 4096], P(None, 'cast', 'span'), may hold values from 0 to 2
- viscosity_table: float32 [3], replicated, may hold values from 0.25 to 4
- pressure_source: float32 [16, 128, 4096], P(None, 'cast', 'span'), may hold values from -6 to 6
Outputs:
- solution_field: float32 [16, 128, 4096], P(None, 'cast', 'span')
- residual: float32 [16, 128, 4096], P(None, 'cast', 'span')
The draws below stay inside these ranges and needn't reach their ends.
All inputs are finite; a program needn't handle non-finite values.
Results may differ from the reference program's by a relative error of at most 0.0003.
Values sent between devices are 32-bit elements; how exact they have to be, the bound alone decides.
No kernel may reach another device: no remote copies, remote signals or barrier semaphores. Data moves between devices by JAX's collectives and lax.ppermute only.
A program may use at most 64 MiB of HBM per device.

```python
import math
import jax
import jax.numpy as jnp

HZ = 16
LEVELS = 3
PRE = 2
POST = 2
COARSE = 8
NC = 128
NS = 4096


def draw_pressure_source(key, part):
    return jnp.clip(jax.random.normal(key, (HZ, NC, NS), jnp.float32), -6.0, 6.0)


def with_ends(entries, own_key, least, high):
    place = [jax.random.randint(jax.random.fold_in(own_key, axis), (), 0, length) for axis, length in enumerate(entries.shape)]
    longest = entries.shape.index(max(entries.shape))
    beside = place[:longest] + [(place[longest] + 1) % entries.shape[longest]] + place[longest + 1:]
    return entries.at[tuple(place)].set(least).at[tuple(beside)].set(high)


def setup_inputs(seed: int = 0) -> dict:
    arg_keys = jax.random.split(jax.random.key(seed), 4)
    phase = with_ends(jax.random.randint(arg_keys[0], (HZ, NC, NS), 0, 3), jax.random.fold_in(arg_keys[0], 1), 0, 2).astype(jnp.int32)
    viscosity_table = jnp.clip(jnp.exp(jax.random.uniform(arg_keys[1], (3,), jnp.float32, math.log(0.25), math.log(4.0))), 0.25, 4.0)
    pressure_source = draw_pressure_source(jax.random.fold_in(arg_keys[3], 71), 0)
    return dict(phase=phase, viscosity_table=viscosity_table, pressure_source=pressure_source)


relax_weight = 0.8


def harmonic(lower, upper):
    return 2.0 * lower * upper / (lower + upper)


def coarsen(values):
    height, length, width = values.shape
    return jnp.mean(values.reshape(height // 2, 2, length // 2, 2, width // 2, 2), axis=(1, 3, 5))


def refine(values):
    return jnp.repeat(jnp.repeat(jnp.repeat(values, 2, axis=0), 2, axis=1), 2, axis=2)


def face_table(coeff):
    padded = jnp.concatenate([coeff[:, :1], coeff, coeff[:, -1:]], axis=1)
    cast_faces = harmonic(padded[:, :-1], padded[:, 1:])
    span_faces = harmonic(jnp.roll(coeff, 1, axis=2), coeff)
    span_upper = jnp.roll(span_faces, -1, axis=2)
    flat = jnp.zeros_like(coeff[:1])
    height_faces = jnp.concatenate([flat, harmonic(coeff[:-1], coeff[1:]), flat], axis=0)
    diagonal = cast_faces[:, :-1] + cast_faces[:, 1:] + span_faces + span_upper + height_faces[:-1] + height_faces[1:]
    return cast_faces, span_faces, span_upper, height_faces, diagonal


def operate(values, table, scale):
    cast_faces, span_faces, span_upper, height_faces, diagonal = table
    zero_cast = jnp.zeros_like(values[:, :1])
    zero_height = jnp.zeros_like(values[:1])
    cast_below = jnp.concatenate([zero_cast, values[:, :-1]], axis=1)
    cast_above = jnp.concatenate([values[:, 1:], zero_cast], axis=1)
    below = jnp.concatenate([zero_height, values[:-1]], axis=0)
    above = jnp.concatenate([values[1:], zero_height], axis=0)
    near = (cast_faces[:, :-1] * cast_below + cast_faces[:, 1:] * cast_above
            + span_faces * jnp.roll(values, 1, axis=2) + span_upper * jnp.roll(values, -1, axis=2)
            + height_faces[:-1] * below + height_faces[1:] * above)
    return scale * (diagonal * values - near)


def relax(values, source, table, scale):
    return values + relax_weight * (source - operate(values, table, scale)) / (scale * table[4])


def reference(phase, viscosity_table, pressure_source):
    viscosity = jnp.where(phase == 0, viscosity_table[0], jnp.where(phase == 1, viscosity_table[1], viscosity_table[2]))
    coeff = 1.0 / viscosity
    tables = []
    for level in range(LEVELS + 1):
        tables.append(face_table(coeff))
        if level < LEVELS:
            coeff = coarsen(coeff)
    sources = [pressure_source]
    kept = []
    for level in range(LEVELS):
        scale = 0.25 ** level
        values = jnp.zeros_like(sources[level])
        for sweep in range(PRE):
            values = relax(values, sources[level], tables[level], scale)
        remainder = sources[level] - operate(values, tables[level], scale)
        kept.append(values)
        sources.append(coarsen(remainder))
    scale = 0.25 ** LEVELS
    values = jnp.zeros_like(sources[LEVELS])
    for sweep in range(COARSE):
        values = relax(values, sources[LEVELS], tables[LEVELS], scale)
    for level in reversed(range(LEVELS)):
        scale = 0.25 ** level
        values = kept[level] + refine(values)
        for sweep in range(POST):
            values = relax(values, sources[level], tables[level], scale)
    residual = pressure_source - operate(values, tables[0], 1.0)
    return values, residual
```

```python
import jax
import jax.numpy as jnp
from jax import lax
from jax.experimental import pallas as pl
from jax.experimental.pallas import tpu as pltpu
from jax.sharding import PartitionSpec as P

HZ, BC, BS = 16, 16, 128
HALO = 16
ROWS = BC + 2 * HALO
LANES = 256
SWEEPS_COARSE = 8
WEIGHT = 0.8
F32 = jnp.float32
HIGH = lax.Precision.HIGHEST


def shift(x, step, axis):
    return pltpu.roll(x, step % x.shape[axis], axis)


def iota(shape, axis):
    return lax.broadcasted_iota(jnp.int32, shape, axis)


def product(a, b):
    return jnp.dot(a, b, precision=HIGH, preferred_element_type=F32)


def harmonic(a, b):
    return 2.0 * a * b / (a + b)


def near(x, below, above, cast, span, low, high):
    return (
        cast * shift(x, 1, 0)
        + shift(cast * x, -1, 0)
        + span * shift(x, 1, 1)
        + shift(span * x, -1, 1)
        + low * below
        + high * above
    )


def diagonal_of(cast, span, low, high):
    return cast + shift(cast, -1, 0) + span + shift(span, -1, 1) + low + high


class Level:
    def __init__(self, cast, span, height, diag, relax, source):
        self.cast, self.span, self.height = cast, span, height
        self.diag, self.relax, self.source = diag, relax, source
        self.depth = len(cast)

    def near(self, x, z):
        depth = self.depth
        return near(
            x[z],
            x[max(z - 1, 0)],
            x[min(z + 1, depth - 1)],
            self.cast[z],
            self.span[z],
            self.height[z],
            self.height[z + 1],
        )

    def start(self):
        return [self.relax[z] * self.source[z] for z in range(self.depth)]

    def sweep(self, x):
        return [
            (1.0 - WEIGHT) * x[z] + self.relax[z] * (self.near(x, z) + self.source[z])
            for z in range(self.depth)
        ]

    def residual(self, x):
        return [self.source[z] - self.diag[z] * x[z] + self.near(x, z) for z in range(self.depth)]


def height_faces(coeff):
    flat = jnp.zeros_like(coeff[0])
    inner = [harmonic(a, b) for a, b in zip(coeff[:-1], coeff[1:])]
    return [flat] + inner + [flat]


def whole_level(coeff, source):
    shape = coeff[0].shape
    row = iota(shape, 0)
    height = height_faces(coeff)
    cast, span, diag, relax = [], [], [], []
    for z, c in enumerate(coeff):
        lower = jnp.where(row == 0, 0.0, harmonic(shift(c, 1, 0), c))
        ends = jnp.where((row == 0) | (row == shape[0] - 1), c, 0.0)
        side = harmonic(shift(c, 1, 1), c)
        total = diagonal_of(lower, side, height[z], height[z + 1]) + ends
        cast.append(lower)
        span.append(side)
        diag.append(total)
        relax.append(WEIGHT / total)
    return Level(cast, span, height, diag, relax, source)


def pair_rows(value, scratch):
    rows = value.shape[0]
    scratch[...] = value
    return scratch[pl.ds(0, rows // 2, stride=2), :] + scratch[pl.ds(1, rows // 2, stride=2), :]


def stage_kernel(table, phase, source, out):
    for z in range(HZ):
        p = phase[z]
        out[0, z] = jnp.where(p == 0, table[0], jnp.where(p == 1, table[1], table[2]))
        out[1, z] = source[z]


def margin_kernel(own, before, after, first, last):
    lane = iota((ROWS, BS), 1)
    for a in range(2):
        for group in range(2):
            head = tail = None
            for k in range(8):
                z = group * 8 + k
                slab = jnp.concatenate([before[a, z], own[a, z], after[a, z]], axis=0)
                h = shift(slab, HALO * k, 1)
                t = shift(slab, HALO * k + HALO, 1)
                inside = (lane >= HALO * k) & (lane < HALO * k + HALO)
                head = h if head is None else jnp.where(inside, h, head)
                tail = t if tail is None else jnp.where(inside, t, tail)
            first[a, group] = head
            last[a, group] = tail


def descent_kernel(
    place,
    own,
    before,
    after,
    right,
    left,
    x0,
    b0,
    cast0,
    span0,
    height0,
    diag0,
    relax0,
    x1,
    b1,
    cast1,
    span1,
    height1,
    relax1,
    slots,
    visc,
    xa,
    pair,
    cpair,
    rows24,
    rows8,
):
    index, count = place[0], place[1]
    first, last = index == 0, index == count - 1
    lane = iota((ROWS, BS), 1)

    for z in range(HZ):
        for a, target in ((0, visc), (1, b0)):
            low, mid, high = before[a, z], own[a, z], after[a, z]
            if a == 0:
                low = jnp.where(first, jnp.broadcast_to(mid[:1], low.shape), low)
                high = jnp.where(last, jnp.broadcast_to(mid[-1:], high.shape), high)
            target[z, :, :BS] = jnp.concatenate([low, mid, high], axis=0)
            group, k = divmod(z, 8)
            r = shift(right[a, group], -HALO * k, 1)
            l = shift(left[a, group], BS - HALO - HALO * k, 1)
            fill = 1.0 if a == 0 else 0.0
            edge = jnp.where(lane < HALO, r, jnp.where(lane >= BS - HALO, l, fill))
            if a == 0:
                edge = jnp.concatenate(
                    [
                        jnp.where(first, jnp.broadcast_to(edge[HALO : HALO + 1], (HALO, BS)), edge[:HALO]),
                        edge[HALO : HALO + BC],
                        jnp.where(last, jnp.broadcast_to(edge[HALO + BC - 1 : HALO + BC], (HALO, BS)), edge[HALO + BC :]),
                    ],
                    axis=0,
                )
            target[z, :, BS:] = edge

    height0[0] = jnp.zeros((ROWS, LANES), F32)
    height0[HZ] = jnp.zeros((ROWS, LANES), F32)

    def faces(z, _):
        v = visc[z]
        cast0[z] = 2.0 / (v + shift(v, 1, 0))
        span0[z] = 2.0 / (v + shift(v, 1, 1))

        @pl.when(z > 0)
        def _():
            height0[z] = 2.0 / (v + visc[jnp.maximum(z - 1, 0)])

        return 0

    lax.fori_loop(0, HZ, faces, 0)

    row = iota((ROWS, LANES), 0)
    outside = (first & (row < HALO)) | (last & (row >= HALO + BC))
    weight = jnp.where(outside, 0.0, WEIGHT)

    def begin(z, _):
        total = diagonal_of(cast0[z], span0[z], height0[z], height0[z + 1])
        diag0[z] = total
        relax = weight / total
        relax0[z] = relax
        xa[z] = relax * b0[z]
        return 0

    lax.fori_loop(0, HZ, begin, 0)

    def near0(x, z):
        return near(
            x[z],
            x[jnp.maximum(z - 1, 0)],
            x[jnp.minimum(z + 1, HZ - 1)],
            cast0[z],
            span0[z],
            height0[z],
            height0[z + 1],
        )

    def sweep(z, _):
        x0[z] = (1.0 - WEIGHT) * xa[z] + relax0[z] * (near0(xa, z) + b0[z])
        return 0

    lax.fori_loop(0, HZ, sweep, 0)

    def remainder(k, _):
        total = None
        for z in (2 * k, 2 * k + 1):
            r = b0[z] - diag0[z] * x0[z] + near0(x0, z)
            total = r if total is None else total + r
        pair[k] = total
        cpair[k] = 1.0 / visc[2 * k] + 1.0 / visc[2 * k + 1]
        return 0

    lax.fori_loop(0, HZ // 2, remainder, 0)

    half = ROWS // 2
    merge = jnp.where(iota((LANES, BS), 0) // 2 == iota((LANES, BS), 1), 1.0, 0.0)
    depth = HZ // 2
    edge = HALO // 2
    for a, source in enumerate((cpair, pair)):
        for k in range(depth):
            rows24[a * depth + k] = product(source[k], merge)

    def halved(k):
        return rows24[k, pl.ds(0, half, stride=2), :] + rows24[k, pl.ds(1, half, stride=2), :]

    row = iota((half, BS), 0)
    coeff, sources = [], []
    for k in range(depth):
        c = 0.125 * halved(k)
        low = jnp.where(first, jnp.broadcast_to(c[edge : edge + 1], (edge, BS)), c[:edge])
        high = jnp.where(last, jnp.broadcast_to(c[half - edge - 1 : half - edge], (edge, BS)), c[half - edge :])
        coeff.append(jnp.concatenate([low, c[edge : half - edge], high], axis=0))
        sources.append(0.5 * halved(depth + k))
    outside = (first & (row < edge)) | (last & (row >= half - edge))
    weight = jnp.where(outside, 0.0, WEIGHT)
    height = height_faces(coeff)
    cast = [harmonic(shift(c, 1, 0), c) for c in coeff]
    span = [harmonic(shift(c, 1, 1), c) for c in coeff]
    diag = [diagonal_of(cast[z], span[z], height[z], height[z + 1]) for z in range(depth)]
    relax = [weight / d for d in diag]
    level = Level(cast, span, height, diag, relax, sources)
    x = level.sweep(level.start())
    for z in range(depth):
        x1[z] = x[z]
        b1[z] = sources[z]
        cast1[z] = cast[z]
        span1[z] = span[z]
        relax1[z] = relax[z]
    for z in range(depth + 1):
        height1[z] = height[z]
    remains = level.residual(x)

    total_c = total_b = None
    for k in range(depth // 2):
        source, target = iota((BS, BS), 0), iota((BS, BS), 1)
        place_k = jnp.where((source < BS // 2) & (source // 2 + 32 * k == target), 1.0, 0.0)
        c = coeff[2 * k][edge : edge + 8] + coeff[2 * k + 1][edge : edge + 8]
        r = remains[2 * k][edge : edge + 8] + remains[2 * k + 1][edge : edge + 8]
        part = product(jnp.concatenate([c, r], axis=0), place_k)
        total_c = part if total_c is None else total_c + part
    rows8[...] = total_c
    c = 0.125 * (rows8[pl.ds(0, 4, stride=2), :] + rows8[pl.ds(1, 4, stride=2), :])
    r = 0.5 * (rows8[pl.ds(8, 4, stride=2), :] + rows8[pl.ds(9, 4, stride=2), :])
    for d in range(slots.shape[0]):
        slots[d, 0:4] = c
        slots[d, 4:8] = r


def ascent_kernel(
    place,
    own,
    right,
    left,
    x0,
    b0,
    cast0,
    span0,
    height0,
    diag0,
    relax0,
    x1,
    b1,
    cast1,
    span1,
    height1,
    relax1,
    solution_out,
    residual_out,
    tiles,
    pairs,
    wide2,
    padded2,
    wide1,
    wide0,
    xa,
    xb,
):
    count = own.shape[0]
    rows = 4 * count
    lane = iota((rows, 128), 1)
    index = place[0]

    fields = []
    for part in range(2):
        for s, block in enumerate((own, right, left)):
            for d in range(count):
                tiles[s, 4 * d : 4 * d + 4] = block[d, 4 * part : 4 * part + 4]
        slabs = []
        for z in range(4):
            o = shift(tiles[0], -32 * z, 1)
            r = shift(tiles[1], 32 - 32 * z, 1)
            l = shift(tiles[2], 96 - 32 * z, 1)
            fill = 1.0 if part == 0 else 0.0
            slabs.append(jnp.where(lane < 32, o, jnp.where(lane < 64, r, jnp.where(lane >= 96, l, fill))))
        fields.append(slabs)
    coeff2, source2 = fields
    level2 = whole_level(coeff2, source2)
    x2 = level2.sweep(level2.start())
    remains = level2.residual(x2)

    a, b = iota((128, 128), 0), iota((128, 128), 1)
    narrow = jnp.where(((a < 64) & (a // 2 == b)) | ((a >= 96) & (a // 2 + 64 == b)), 1.0, 0.0)
    widen = jnp.where(((b < 64) & (b // 2 == a)) | ((b >= 96) & (b // 2 + 64 == a)), 1.0, 0.0)
    gathered = []
    for field in (coeff2, remains):
        for k in range(2):
            gathered.append(pair_rows(field[2 * k] + field[2 * k + 1], pairs))
    merged = product(jnp.concatenate(gathered, axis=0), narrow)
    half = rows // 2
    lane3 = iota((half, 128), 1)
    known = (lane3 < 32) | (lane3 >= 112)
    coeff3 = [jnp.where(known, 0.125 * merged[half * k : half * (k + 1)], 1.0) for k in range(2)]
    source3 = [0.5 * merged[half * (2 + k) : half * (3 + k)] for k in range(2)]
    level3 = whole_level(coeff3, source3)
    x3 = level3.start()
    for _ in range(SWEEPS_COARSE - 1):
        x3 = level3.sweep(x3)

    spread = product(jnp.concatenate(x3, axis=0), widen)
    for k in range(2):
        wide2[k, pl.ds(0, half, stride=2), :] = spread[half * k : half * (k + 1)]
        wide2[k, pl.ds(1, half, stride=2), :] = spread[half * k : half * (k + 1)]
    x2 = [x2[z] + wide2[z // 2] for z in range(4)]
    x2 = level2.sweep(level2.sweep(x2))

    for z in range(4):
        padded2[z, 0:8] = jnp.zeros((8, 128), F32)
        padded2[z, 8 : 8 + rows] = x2[z]
        padded2[z, 8 + rows : 16 + rows] = jnp.zeros((8, 128), F32)
    grow = jnp.where(((b < 96) & (b // 2 == a)) | ((b >= 96) & (b // 2 + 64 == a)), 1.0, 0.0)
    local = [padded2[z, pl.ds(4 * index + 4, 16), :] for z in range(4)]
    spread = product(jnp.concatenate(local, axis=0), grow)
    for z in range(4):
        wide1[z, pl.ds(0, 16, stride=2), :] = spread[16 * z : 16 * z + 16]
        wide1[z, pl.ds(1, 16, stride=2), :] = spread[16 * z : 16 * z + 16]
    depth = HZ // 2
    half = ROWS // 2
    level1 = Level(
        [cast1[z] for z in range(depth)],
        [span1[z] for z in range(depth)],
        [height1[z] for z in range(depth + 1)],
        None,
        [relax1[z] for z in range(depth)],
        [b1[z] for z in range(depth)],
    )
    x = [x1[z] + wide1[z // 2, 0:half] for z in range(depth)]
    x = level1.sweep(level1.sweep(x))

    double = jnp.where(iota((BS, LANES), 1) // 2 == iota((BS, LANES), 0), 1.0, 0.0)
    spread = product(jnp.concatenate(x, axis=0), double)
    for z in range(depth):
        for s in range(2):
            part = spread[half * z : half * (z + 1), BS * s : BS * (s + 1)]
            wide0[s, z, pl.ds(0, half, stride=2), :] = part
            wide0[s, z, pl.ds(1, half, stride=2), :] = part
    top, bottom = 8, ROWS - 8
    cut = slice(top, bottom)

    def correct(z, _):
        k = lax.div(z, 2)
        for s in range(2):
            lanes = slice(BS * s, BS * (s + 1))
            xa[z, :, lanes] = x0[z, cut, lanes] + wide0[s, k, cut]
        return 0

    lax.fori_loop(0, HZ, correct, 0)

    def near0(x, z):
        return near(
            x[z],
            x[jnp.maximum(z - 1, 0)],
            x[jnp.minimum(z + 1, HZ - 1)],
            cast0[z, cut],
            span0[z, cut],
            height0[z, cut],
            height0[z + 1, cut],
        )

    def sweep(source, target):
        def body(z, _):
            target[z] = (1.0 - WEIGHT) * source[z] + relax0[z, cut] * (near0(source, z) + b0[z, cut])
            return 0

        lax.fori_loop(0, HZ, body, 0)

    sweep(xa, xb)
    sweep(xb, xa)

    def finish(z, _):
        r = b0[z, cut] - diag0[z, cut] * xa[z] + near0(xa, z)
        solution_out[z] = xa[z, HALO - top : HALO - top + BC, :BS]
        residual_out[z] = r[HALO - top : HALO - top + BC, :BS]
        return 0

    lax.fori_loop(0, HZ, finish, 0)


VMEM = pl.BlockSpec(memory_space=pltpu.VMEM)
SMEM = pl.BlockSpec(memory_space=pltpu.SMEM)
PARAMS = pltpu.CompilerParams(vmem_limit_bytes=48 * 1024 * 1024)
INTERPRET = False


def call(kernel, in_specs, outs, scratch=()):
    single = not isinstance(outs, list)
    shapes = [outs] if single else outs
    shapes = [jax.ShapeDtypeStruct(s, F32) for s in shapes]
    run = pl.pallas_call(
        kernel,
        in_specs=in_specs,
        out_specs=VMEM if single else [VMEM] * len(shapes),
        out_shape=shapes[0] if single else shapes,
        scratch_shapes=[pltpu.VMEM(s, F32) for s in scratch],
        compiler_params=PARAMS,
        interpret=INTERPRET,
    )
    return run


def ring(value, axis, step):
    size = lax.axis_size(axis)
    return lax.ppermute(value, axis, [(i, (i + step) % size) for i in range(size)])


def shards(phase, viscosity_table, pressure_source):
    count = lax.axis_size("cast")
    place = jnp.stack([lax.axis_index("cast"), count]).astype(jnp.int32)
    block = (2, HZ, BC, BS)
    fine = (HZ, ROWS, LANES)
    mid = (HZ // 2, ROWS // 2, BS)
    packed = (2, 2, ROWS, BS)

    own = call(stage_kernel, [SMEM, VMEM, VMEM], block)(viscosity_table, phase, pressure_source)
    before = ring(own, "cast", 1)
    after = ring(own, "cast", -1)
    first, last = call(margin_kernel, [VMEM] * 3, [packed, packed])(own, before, after)
    right = ring(first, "span", -1)
    left = ring(last, "span", 1)

    state_shapes = [fine, fine, fine, fine, (HZ + 1, ROWS, LANES), fine, fine]
    state_shapes += [mid, mid, mid, mid, (HZ // 2 + 1, ROWS // 2, BS), mid]
    scratch = [fine, fine, (HZ // 2, ROWS, LANES), (HZ // 2, ROWS, LANES), (HZ, ROWS, BS), (16, BS)]
    *state, slots = call(
        descent_kernel,
        [SMEM] + [VMEM] * 5,
        state_shapes + [(count, 8, 128)],
        scratch,
    )(place, own, before, after, right, left)

    column = lax.all_to_all(slots, "cast", 0, 0)
    column_left = ring(column, "span", 1)
    column_right = ring(column, "span", -1)
    rows = 4 * count
    scratch = [
        (3, rows, 128),
        (rows, 128),
        (2, rows, 128),
        (4, rows + 16, 128),
        (4, 32, 128),
        (2, HZ // 2, ROWS, BS),
        (HZ, ROWS - 16, LANES),
        (HZ, ROWS - 16, LANES),
    ]
    out = (HZ, BC, BS)
    return tuple(
        call(ascent_kernel, [SMEM] + [VMEM] * (3 + len(state)), [out, out], scratch)(
            place, column, column_right, column_left, *state
        )
    )


def solution(mesh):
    blocks = P(None, "cast", "span")
    return jax.shard_map(
        shards,
        mesh=mesh,
        in_specs=(blocks, P(), blocks),
        out_specs=(blocks, blocks),
        check_vma=False,
    )
```

```python
import jax
import jax.numpy as jnp
from jax import lax
from jax.experimental import pallas as pl
from jax.experimental.pallas import tpu as pltpu
from jax.sharding import PartitionSpec as P

HZ, BC, BS = 16, 16, 128
HALO = 16
ROWS = BC + 2 * HALO
CUT = slice(HALO - 4, HALO + BC + 4)
KEPT = BC + 8
HALF = ROWS // 2
PACK = HZ // 2
SWEEPS_COARSE = 8
WEIGHT = 0.8
F32 = jnp.float32
HIGH = lax.Precision.HIGHEST


def shift(x, step, axis):
    return pltpu.roll(x, step % x.shape[axis], axis)


def iota(shape, axis):
    return lax.broadcasted_iota(jnp.int32, shape, axis)


def product(a, b):
    return jnp.dot(a, b, precision=HIGH, preferred_element_type=F32)


def harmonic(a, b):
    return 2.0 * a * b / (a + b)


def near(x, below, above, cast, span, low, high):
    return (
        cast * shift(x, 1, 0)
        + shift(cast * x, -1, 0)
        + span * shift(x, 1, 1)
        + shift(span * x, -1, 1)
        + low * below
        + high * above
    )


def diagonal_of(cast, span, low, high):
    return cast + shift(cast, -1, 0) + span + shift(span, -1, 1) + low + high


class Level:
    def __init__(self, cast, span, height, diag, relax, source, depth, packed=False):
        self.cast, self.span, self.height = cast, span, height
        self.diag, self.relax, self.source = diag, relax, source
        self.depth, self.packed = depth, packed

    def near(self, x, z):
        last = self.depth - 1
        below, above = x[max(z - 1, 0)], x[min(z + 1, last)]
        if self.packed and z == 0:
            below = shift(x[last], 64, 1)
        if self.packed and z == last:
            above = shift(x[0], 64, 1)
        return near(x[z], below, above, self.cast[z], self.span[z], self.height[z], self.height[z + 1])

    def start(self):
        return [self.relax[z] * self.source[z] for z in range(self.depth)]

    def sweep(self, x):
        return [
            (1.0 - WEIGHT) * x[z] + self.relax[z] * (self.near(x, z) + self.source[z])
            for z in range(self.depth)
        ]

    def residual(self, x):
        return [self.source[z] - self.diag[z] * x[z] + self.near(x, z) for z in range(self.depth)]


def fine_level(visc, source, outside, packed):
    depth = len(visc)
    shape = visc[0].shape
    weight = jnp.where(outside, 0.0, WEIGHT)
    cast = [2.0 / (v + shift(v, 1, 0)) for v in visc]
    span = [2.0 / (v + shift(v, 1, 1)) for v in visc]
    inner = [2.0 / (a + b) for a, b in zip(visc[:-1], visc[1:])]
    if packed:
        bottom = jnp.where(iota(shape, 1) < 64, 0.0, 2.0 / (visc[0] + shift(visc[-1], 64, 1)))
        top = shift(bottom, 64, 1)
    else:
        bottom = top = jnp.zeros(shape, F32)
    height = [bottom] + inner + [top]
    diag = [diagonal_of(cast[z], span[z], height[z], height[z + 1]) for z in range(depth)]
    relax = [weight / d for d in diag]
    return Level(cast, span, height, diag, relax, source, depth, packed)


def keep(level, x, refs):
    for ref, values in zip(refs, (x, level.source, level.cast, level.span, level.height, level.diag, level.relax)):
        for z, value in enumerate(values):
            ref[z] = value[CUT]


def coarse_parts(visc, remains, scratch):
    parts = []
    count = len(visc) // 2
    for a, values in enumerate(([1.0 / v for v in visc], remains)):
        for k in range(count):
            scratch[a * count + k] = values[2 * k] + values[2 * k + 1]
            ref = scratch.at[a * count + k]
            parts.append(ref[pl.ds(0, HALF, stride=2), :] + ref[pl.ds(1, HALF, stride=2), :])
    return jnp.concatenate(parts, axis=0)


def ends(value, first, last, edge):
    rows = value.shape[0]
    low = jnp.where(first, jnp.broadcast_to(value[edge : edge + 1], (edge, BS)), value[:edge])
    high = jnp.where(last, jnp.broadcast_to(value[rows - edge - 1 : rows - edge], (edge, BS)), value[rows - edge :])
    return jnp.concatenate([low, value[edge : rows - edge], high], axis=0)


def beyond(place, rows, edge):
    row = iota((rows, BS), 0)
    first, last = place[0] == 0, place[0] == place[1] - 1
    return first, last, (first & (row < edge)) | (last & (row >= rows - edge))


def height_faces(coeff):
    flat = jnp.zeros_like(coeff[0])
    inner = [harmonic(a, b) for a, b in zip(coeff[:-1], coeff[1:])]
    return [flat] + inner + [flat]


def whole_level(coeff, source):
    shape = coeff[0].shape
    row = iota(shape, 0)
    height = height_faces(coeff)
    cast, span, diag, relax = [], [], [], []
    for z, c in enumerate(coeff):
        lower = jnp.where(row == 0, 0.0, harmonic(shift(c, 1, 0), c))
        ends = jnp.where((row == 0) | (row == shape[0] - 1), c, 0.0)
        side = harmonic(shift(c, 1, 1), c)
        total = diagonal_of(lower, side, height[z], height[z + 1]) + ends
        cast.append(lower)
        span.append(side)
        diag.append(total)
        relax.append(WEIGHT / total)
    return Level(cast, span, height, diag, relax, source, len(coeff))


def pair_rows(value, scratch):
    rows = value.shape[0]
    scratch[...] = value
    return scratch[pl.ds(0, rows // 2, stride=2), :] + scratch[pl.ds(1, rows // 2, stride=2), :]


def stage_kernel(table_in, phase_in, source_in, out, table, phase, sems):
    copies = [
        pltpu.make_async_copy(table_in, table, sems.at[0]),
        pltpu.make_async_copy(phase_in, phase, sems.at[1]),
        pltpu.make_async_copy(source_in, out.at[1], sems.at[2]),
    ]
    for copy in copies:
        copy.start()
    copies[0].wait()
    copies[1].wait()
    for z in range(HZ):
        p = phase[z]
        out[0, z] = jnp.where(p == 0, table[0], jnp.where(p == 1, table[1], table[2]))
    copies[2].wait()


def margin_kernel(own, before, after, first, last):
    lane = iota((ROWS, BS), 1)
    for a in range(2):
        for group in range(2):
            head = tail = None
            for sub in range(4):
                for half in range(2):
                    z = group * 4 + sub + 8 * half
                    start = 16 * sub + 64 * half
                    slab = jnp.concatenate([before[a, z], own[a, z], after[a, z]], axis=0)
                    h = shift(slab, start, 1)
                    t = shift(slab, start + HALO, 1)
                    inside = (lane >= start) & (lane < start + HALO)
                    head = h if head is None else jnp.where(inside, h, head)
                    tail = t if tail is None else jnp.where(inside, t, tail)
            first[a, group] = head
            last[a, group] = tail


def own_kernel(place, own, before, after, x, b, cast, span, height, diag, relax, merged, inner, scratch):
    first, last, outside = beyond(place, ROWS, HALO)
    visc, source = [], []
    for z in range(HZ):
        v, s = (jnp.concatenate([before[a, z], own[a, z], after[a, z]], axis=0) for a in range(2))
        visc.append(ends(v, first, last, HALO))
        source.append(s)
    lane = iota((ROWS, BS), 1)
    for a, field in enumerate((visc, source)):
        for k in range(PACK):
            low, high = field[k], field[k + PACK]
            inner[a, k] = jnp.where(
                lane < 32,
                shift(low, 16, 1),
                jnp.where(lane < 64, shift(low, 48, 1), jnp.where(lane < 96, shift(high, 80, 1), shift(high, 112, 1))),
            )
    level = fine_level(visc, source, outside, False)
    values = level.sweep(level.start())
    keep(level, values, (x, b, cast, span, height, diag, relax))
    parts = coarse_parts(visc, level.residual(values), scratch)
    i, j = iota((BS, BS), 0), iota((BS, BS), 1)
    merge = jnp.where((i // 2 == j) & (i >= 8) & (i < 120), 1.0, 0.0)
    total = product(parts, merge)
    for k in range(HZ):
        merged[k] = total[HALF * k : HALF * (k + 1)]


def edge_kernel(
    place, right, left, inner, merged, x, b, cast, span, height, diag, relax,
    x1, b1, cast1, span1, height1, relax1, slots, scratch, rows8,
):
    first, last, outside = beyond(place, ROWS, HALO)
    lane = iota((ROWS, BS), 1) % 64
    fields = []
    for a in range(2):
        slabs = []
        for k in range(PACK):
            group, sub = divmod(k, 4)
            l = shift(left[a, group], -16 * sub, 1)
            r = shift(right[a, group], 48 - 16 * sub, 1)
            value = jnp.where(lane < 16, l, jnp.where(lane >= 48, r, inner[a, k]))
            slabs.append(ends(value, first, last, HALO) if a == 0 else value)
        fields.append(slabs)
    visc, source = fields
    level = fine_level(visc, source, outside, True)
    values = level.sweep(level.start())
    keep(level, values, (x, b, cast, span, height, diag, relax))
    parts = coarse_parts(visc, level.residual(values), scratch)
    i, j = iota((BS, 2 * BS), 0), iota((BS, 2 * BS), 1)
    m, ring_lane = i % 64, j % BS
    target = jnp.where(m < 24, (m // 2 + 120) % BS, m // 2 + 40)
    used = (m < 24) | (m >= 40)
    merge = jnp.where(used & (target == ring_lane) & (i // 64 == j // BS), 1.0, 0.0)
    total = product(parts, merge)

    edge = HALO // 2
    first, last, outside = beyond(place, HALF, edge)
    weight = jnp.where(outside, 0.0, WEIGHT)
    coarse = []
    for k in range(HZ):
        a, z = divmod(k, 8)
        side, pos = divmod(z, 4)
        row = HALF * (4 * a + pos)
        coarse.append(merged[k] + total[row : row + HALF, BS * side : BS * (side + 1)])
    lane = iota((HALF, BS), 1)
    known = (lane < 72) | (lane >= 120)
    coeff = [jnp.where(known, 0.125 * ends(c, first, last, edge), 1.0) for c in coarse[:8]]
    source = [0.5 * c for c in coarse[8:]]
    height = height_faces(coeff)
    cast_faces = [harmonic(shift(c, 1, 0), c) for c in coeff]
    span_faces = [harmonic(shift(c, 1, 1), c) for c in coeff]
    diagonal = [diagonal_of(cast_faces[z], span_faces[z], height[z], height[z + 1]) for z in range(8)]
    level = Level(cast_faces, span_faces, height, diagonal, [weight / d for d in diagonal], source, 8)
    values = level.sweep(level.start())
    for ref, items in ((x1, values), (b1, source), (cast1, cast_faces), (span1, span_faces), (height1, height), (relax1, level.relax)):
        for z, item in enumerate(items):
            ref[z] = item
    remains = level.residual(values)

    total = None
    i, j = iota((BS, BS), 0), iota((BS, BS), 1)
    for k in range(4):
        move = jnp.where((i < 64) & (i // 2 + 32 * k == j), 1.0, 0.0)
        c = coeff[2 * k][edge : edge + 8] + coeff[2 * k + 1][edge : edge + 8]
        r = remains[2 * k][edge : edge + 8] + remains[2 * k + 1][edge : edge + 8]
        part = product(jnp.concatenate([c, r], axis=0), move)
        total = part if total is None else total + part
    rows8[...] = total
    c = 0.125 * (rows8[pl.ds(0, 4, stride=2), :] + rows8[pl.ds(1, 4, stride=2), :])
    r = 0.5 * (rows8[pl.ds(8, 4, stride=2), :] + rows8[pl.ds(9, 4, stride=2), :])
    for d in range(slots.shape[0]):
        slots[d, 0:4] = c
        slots[d, 4:8] = r


def ascent_kernel(
    place, own, right, left,
    xo, bo, casto, spano, heighto, diago, relaxo,
    xe, be, caste, spane, heighte, diage, relaxe,
    x1, b1, cast1, span1, height1, relax1,
    solution_out, residual_out, tiles, pairs, wide2, padded2, wide1, wide_own, wide_edge,
):
    count = own.shape[0]
    rows = 4 * count
    lane = iota((rows, 128), 1)
    index = place[0]

    fields = []
    for part in range(2):
        for s, block in enumerate((own, right, left)):
            for d in range(count):
                tiles[s, 4 * d : 4 * d + 4] = block[d, 4 * part : 4 * part + 4]
        slabs = []
        for z in range(4):
            o = shift(tiles[0], -32 * z, 1)
            r = shift(tiles[1], 32 - 32 * z, 1)
            l = shift(tiles[2], 96 - 32 * z, 1)
            fill = 1.0 if part == 0 else 0.0
            slabs.append(jnp.where(lane < 32, o, jnp.where(lane < 64, r, jnp.where(lane >= 96, l, fill))))
        fields.append(slabs)
    coeff2, source2 = fields
    level2 = whole_level(coeff2, source2)
    x2 = level2.sweep(level2.start())
    remains = level2.residual(x2)

    a, b = iota((128, 128), 0), iota((128, 128), 1)
    narrow = jnp.where(((a < 64) & (a // 2 == b)) | ((a >= 96) & (a // 2 + 64 == b)), 1.0, 0.0)
    widen = jnp.where(((b < 64) & (b // 2 == a)) | ((b >= 96) & (b // 2 + 64 == a)), 1.0, 0.0)
    gathered = []
    for field in (coeff2, remains):
        for k in range(2):
            gathered.append(pair_rows(field[2 * k] + field[2 * k + 1], pairs))
    merged = product(jnp.concatenate(gathered, axis=0), narrow)
    half = rows // 2
    lane3 = iota((half, 128), 1)
    known = (lane3 < 32) | (lane3 >= 112)
    coeff3 = [jnp.where(known, 0.125 * merged[half * k : half * (k + 1)], 1.0) for k in range(2)]
    source3 = [0.5 * merged[half * (2 + k) : half * (3 + k)] for k in range(2)]
    level3 = whole_level(coeff3, source3)
    x3 = level3.start()
    for _ in range(SWEEPS_COARSE - 1):
        x3 = level3.sweep(x3)

    spread = product(jnp.concatenate(x3, axis=0), widen)
    for k in range(2):
        wide2[k, pl.ds(0, half, stride=2), :] = spread[half * k : half * (k + 1)]
        wide2[k, pl.ds(1, half, stride=2), :] = spread[half * k : half * (k + 1)]
    x2 = [x2[z] + wide2[z // 2] for z in range(4)]
    x2 = level2.sweep(level2.sweep(x2))

    for z in range(4):
        padded2[z, 0:8] = jnp.zeros((8, 128), F32)
        padded2[z, 8 : 8 + rows] = x2[z]
        padded2[z, 8 + rows : 16 + rows] = jnp.zeros((8, 128), F32)
    grow = jnp.where(((b < 96) & (b // 2 == a)) | ((b >= 96) & (b // 2 + 64 == a)), 1.0, 0.0)
    local = [padded2[z, pl.ds(4 * index + 4, 16), :] for z in range(4)]
    spread = product(jnp.concatenate(local, axis=0), grow)
    for z in range(4):
        wide1[z, pl.ds(0, 16, stride=2), :] = spread[16 * z : 16 * z + 16]
        wide1[z, pl.ds(1, 16, stride=2), :] = spread[16 * z : 16 * z + 16]
    level1 = Level(cast1, span1, height1, None, relax1, b1, 8)
    x = [x1[z] + wide1[z // 2, 0:HALF] for z in range(8)]
    x = level1.sweep(level1.sweep(x))

    i, j = iota((BS, BS), 0), iota((BS, BS), 1)
    spread = product(jnp.concatenate(x, axis=0), jnp.where(j // 2 == i, 1.0, 0.0))
    for z in range(8):
        for s in range(2):
            wide_own[z, pl.ds(s, HALF, stride=2), :] = spread[HALF * z : HALF * (z + 1)]
    i, j = iota((2 * BS, BS), 0), iota((2 * BS, BS), 1)
    m = j % 64
    origin = jnp.where(m < 32, (m // 2 + 120) % BS, m // 2 + 40)
    expand = jnp.where((origin == i % BS) & (i // BS == j // 64), 1.0, 0.0)
    sides = [jnp.concatenate([x[k], x[k + 4]], axis=1) for k in range(4)]
    spread = product(jnp.concatenate(sides, axis=0), expand)
    for k in range(4):
        for s in range(2):
            wide_edge[k, pl.ds(s, HALF, stride=2), :] = spread[HALF * k : HALF * (k + 1)]
    level_own = Level(casto, spano, heighto, diago, relaxo, bo, HZ)
    level_edge = Level(caste, spane, heighte, diage, relaxe, be, PACK, True)
    own_x = [xo[z] + wide_own[z // 2, CUT] for z in range(HZ)]
    edge_x = [xe[k] + wide_edge[k // 2, CUT] for k in range(PACK)]
    edge_x = level_edge.sweep(level_edge.sweep(edge_x))
    edge_r = level_edge.residual(edge_x)
    own_x = level_own.sweep(level_own.sweep(own_x))
    own_r = level_own.residual(own_x)
    lane = iota((BC, BS), 1)
    rows = slice(4, 4 + BC)
    for out, mid, side in ((solution_out, own_x, edge_x), (residual_out, own_r, edge_r)):
        for z in range(HZ):
            half, k = divmod(z, PACK)
            low = shift(side[k][rows], -16 - 64 * half, 1)
            high = shift(side[k][rows], 80 - 64 * half, 1)
            out[z] = jnp.where(lane < 8, low, jnp.where(lane >= 120, high, mid[z][rows]))


VMEM = pl.BlockSpec(memory_space=pltpu.VMEM)
SMEM = pl.BlockSpec(memory_space=pltpu.SMEM)
HBM = pl.BlockSpec(memory_space=pltpu.HBM)
PARAMS = pltpu.CompilerParams(vmem_limit_bytes=16 * 1024 * 1024)
INTERPRET = False


def call(kernel, in_specs, outs, scratch=()):
    return pl.pallas_call(
        kernel,
        in_specs=in_specs,
        out_specs=[VMEM] * len(outs),
        out_shape=[jax.ShapeDtypeStruct(s, F32) for s in outs],
        scratch_shapes=[pltpu.VMEM(s, F32) if isinstance(s, tuple) else s for s in scratch],
        compiler_params=PARAMS,
        interpret=INTERPRET,
    )


def ring(value, axis, step):
    size = lax.axis_size(axis)
    return lax.ppermute(value, axis, [(i, (i + step) % size) for i in range(size)])


def shards(phase, viscosity_table, pressure_source):
    count = lax.axis_size("cast")
    place = jnp.stack([lax.axis_index("cast"), count]).astype(jnp.int32)
    packed = (2, 2, ROWS, BS)
    own_state = [(HZ, KEPT, BS)] * 4 + [(HZ + 1, KEPT, BS)] + [(HZ, KEPT, BS)] * 2
    edge_state = [(PACK, KEPT, BS)] * 4 + [(PACK + 1, KEPT, BS)] + [(PACK, KEPT, BS)] * 2
    level1_state = [(8, HALF, BS)] * 4 + [(9, HALF, BS), (8, HALF, BS)]

    stage_scratch = [pltpu.SMEM((3,), F32), pltpu.VMEM((HZ, BC, BS), jnp.int32), pltpu.SemaphoreType.DMA((3,))]
    (own,) = call(stage_kernel, [HBM] * 3, [(2, HZ, BC, BS)], stage_scratch)(viscosity_table, phase, pressure_source)
    before = ring(own, "cast", 1)
    after = ring(own, "cast", -1)
    first, last = call(margin_kernel, [VMEM] * 3, [packed, packed])(own, before, after)
    right = ring(first, "span", -1)
    left = ring(last, "span", 1)
    *kept_own, merged, inner = call(
        own_kernel,
        [SMEM] + [VMEM] * 3,
        own_state + [(HZ, HALF, BS), (2, PACK, ROWS, BS)],
        [(HZ, ROWS, BS)],
    )(place, own, before, after)
    *kept_edge, slots = call(
        edge_kernel,
        [SMEM] + [VMEM] * 4,
        edge_state + level1_state + [(count, 8, BS)],
        [(8, ROWS, BS), (16, BS)],
    )(place, right, left, inner, merged)

    column = lax.all_to_all(slots, "cast", 0, 0)
    column_left = ring(column, "span", 1)
    column_right = ring(column, "span", -1)
    rows = 4 * count
    scratch = [
        (3, rows, BS),
        (rows, BS),
        (2, rows, BS),
        (4, rows + 16, BS),
        (4, 32, BS),
        (8, ROWS, BS),
        (4, ROWS, BS),
    ]
    state = kept_own + kept_edge
    return tuple(
        call(ascent_kernel, [SMEM] + [VMEM] * (3 + len(state)), [(HZ, BC, BS)] * 2, scratch)(
            place, column, column_right, column_left, *state
        )
    )


def solution(mesh):
    blocks = P(None, "cast", "span")
    return jax.shard_map(
        shards,
        mesh=mesh,
        in_specs=(blocks, P(), blocks),
        out_specs=(blocks, blocks),
        check_vma=False,
    )
```

```python
import jax
import jax.numpy as jnp
from jax import lax
from jax.experimental import pallas as pl
from jax.experimental.pallas import tpu as pltpu
from jax.sharding import PartitionSpec as P

HZ, BC, BS = 16, 16, 128
HALO = 16
ROWS = BC + 2 * HALO
CUT = slice(HALO - 4, HALO + BC + 4)
KEPT = BC + 8
HALF = ROWS // 2
PACK = HZ // 2
SWEEPS_COARSE = 8
WEIGHT = 0.8
F32 = jnp.float32
BF16 = jnp.bfloat16


def shift(x, step, axis):
    return pltpu.roll(x, step % x.shape[axis], axis)


def iota(shape, axis):
    return lax.broadcasted_iota(jnp.int32, shape, axis)


def product(a, where):
    b = jnp.where(where, 1.0, 0.0).astype(BF16)
    high = a.astype(BF16)
    low = (a - high.astype(F32)).astype(BF16)
    return jnp.dot(high, b, preferred_element_type=F32) + jnp.dot(low, b, preferred_element_type=F32)


def harmonic(a, b):
    return 2.0 * a * b / (a + b)


def near(x, below, above, cast, span, low, high):
    return (
        cast * shift(x, 1, 0)
        + shift(cast * x, -1, 0)
        + span * shift(x, 1, 1)
        + shift(span * x, -1, 1)
        + low * below
        + high * above
    )


def diagonal_of(cast, span, low, high):
    return cast + shift(cast, -1, 0) + span + shift(span, -1, 1) + low + high


class Level:
    def __init__(self, cast, span, height, diag, relax, source, depth, packed=False):
        self.cast, self.span, self.height = cast, span, height
        self.diag, self.relax, self.source = diag, relax, source
        self.depth, self.packed = depth, packed

    def near(self, x, z):
        last = self.depth - 1
        below, above = x[max(z - 1, 0)], x[min(z + 1, last)]
        if self.packed and z == 0:
            below = shift(x[last], 64, 1)
        if self.packed and z == last:
            above = shift(x[0], 64, 1)
        return near(x[z], below, above, self.cast[z], self.span[z], self.height[z], self.height[z + 1])

    def start(self):
        return [self.relax[z] * self.source[z] for z in range(self.depth)]

    def sweep(self, x):
        return [
            (1.0 - WEIGHT) * x[z] + self.relax[z] * (self.near(x, z) + self.source[z])
            for z in range(self.depth)
        ]

    def residual(self, x):
        return [self.source[z] - self.diag[z] * x[z] + self.near(x, z) for z in range(self.depth)]


def fine_level(visc, source, outside, packed):
    depth = len(visc)
    shape = visc[0].shape
    weight = jnp.where(outside, 0.0, WEIGHT)
    cast = [2.0 / (v + shift(v, 1, 0)) for v in visc]
    span = [2.0 / (v + shift(v, 1, 1)) for v in visc]
    inner = [2.0 / (a + b) for a, b in zip(visc[:-1], visc[1:])]
    if packed:
        bottom = jnp.where(iota(shape, 1) < 64, 0.0, 2.0 / (visc[0] + shift(visc[-1], 64, 1)))
        top = shift(bottom, 64, 1)
    else:
        bottom = top = jnp.zeros(shape, F32)
    height = [bottom] + inner + [top]
    diag = [diagonal_of(cast[z], span[z], height[z], height[z + 1]) for z in range(depth)]
    relax = [weight / d for d in diag]
    return Level(cast, span, height, diag, relax, source, depth, packed)


def keep(level, x, refs):
    for ref, values in zip(refs, (x, level.source, level.cast, level.span, level.height, level.diag, level.relax)):
        for z, value in enumerate(values):
            ref[z] = value[CUT]


def coarse_parts(visc, remains, scratch):
    parts = []
    count = len(visc) // 2
    for a, values in enumerate(([1.0 / v for v in visc], remains)):
        for k in range(count):
            scratch[a * count + k] = values[2 * k] + values[2 * k + 1]
            ref = scratch.at[a * count + k]
            parts.append(ref[pl.ds(0, HALF, stride=2), :] + ref[pl.ds(1, HALF, stride=2), :])
    return jnp.concatenate(parts, axis=0)


def ends(value, first, last, edge):
    rows = value.shape[0]
    low = jnp.where(first, jnp.broadcast_to(value[edge : edge + 1], (edge, BS)), value[:edge])
    high = jnp.where(last, jnp.broadcast_to(value[rows - edge - 1 : rows - edge], (edge, BS)), value[rows - edge :])
    return jnp.concatenate([low, value[edge : rows - edge], high], axis=0)


def beyond(rows, edge):
    row = iota((rows, BS), 0)
    index = lax.axis_index("cast")
    first, last = index == 0, index == lax.axis_size("cast") - 1
    return first, last, (first & (row < edge)) | (last & (row >= rows - edge))


def height_faces(coeff):
    flat = jnp.zeros_like(coeff[0])
    inner = [harmonic(a, b) for a, b in zip(coeff[:-1], coeff[1:])]
    return [flat] + inner + [flat]


def whole_level(coeff, source):
    shape = coeff[0].shape
    row = iota(shape, 0)
    height = height_faces(coeff)
    cast, span, diag, relax = [], [], [], []
    for z, c in enumerate(coeff):
        lower = jnp.where(row == 0, 0.0, harmonic(shift(c, 1, 0), c))
        ends = jnp.where((row == 0) | (row == shape[0] - 1), c, 0.0)
        side = harmonic(shift(c, 1, 1), c)
        total = diagonal_of(lower, side, height[z], height[z + 1]) + ends
        cast.append(lower)
        span.append(side)
        diag.append(total)
        relax.append(WEIGHT / total)
    return Level(cast, span, height, diag, relax, source, len(coeff))


def pair_rows(value, scratch):
    rows = value.shape[0]
    scratch[...] = value
    return scratch[pl.ds(0, rows // 2, stride=2), :] + scratch[pl.ds(1, rows // 2, stride=2), :]


def stage_kernel(table_in, phase_in, source_in, out, table, phase, sems):
    copies = [
        pltpu.make_async_copy(table_in, table, sems.at[0]),
        pltpu.make_async_copy(phase_in, phase, sems.at[1]),
        pltpu.make_async_copy(source_in, out.at[1], sems.at[2]),
    ]
    for copy in copies:
        copy.start()
    copies[0].wait()
    copies[1].wait()
    for z in range(HZ):
        p = phase[z]
        out[0, z] = jnp.where(p == 0, table[0], jnp.where(p == 1, table[1], table[2]))
    copies[2].wait()


def margin_kernel(own, before, after, first, last):
    lane = iota((ROWS, BS), 1)
    for a in range(2):
        for group in range(2):
            head = tail = None
            for sub in range(4):
                for half in range(2):
                    z = group * 4 + sub + 8 * half
                    start = 16 * sub + 64 * half
                    slab = jnp.concatenate([before[a, z], own[a, z], after[a, z]], axis=0)
                    h = shift(slab, start, 1)
                    t = shift(slab, start + HALO, 1)
                    inside = (lane >= start) & (lane < start + HALO)
                    head = h if head is None else jnp.where(inside, h, head)
                    tail = t if tail is None else jnp.where(inside, t, tail)
            first[a, group] = head
            last[a, group] = tail


def own_kernel(own, before, after, x, b, cast, span, height, diag, relax, merged, inner, scratch):
    first, last, outside = beyond(ROWS, HALO)
    visc, source = [], []
    for z in range(HZ):
        v, s = (jnp.concatenate([before[a, z], own[a, z], after[a, z]], axis=0) for a in range(2))
        visc.append(ends(v, first, last, HALO))
        source.append(s)
    lane = iota((ROWS, BS), 1)
    for a, field in enumerate((visc, source)):
        for k in range(PACK):
            low, high = field[k], field[k + PACK]
            inner[a, k] = jnp.where(
                lane < 32,
                shift(low, 16, 1),
                jnp.where(lane < 64, shift(low, 48, 1), jnp.where(lane < 96, shift(high, 80, 1), shift(high, 112, 1))),
            )
    level = fine_level(visc, source, outside, False)
    values = level.sweep(level.start())
    keep(level, values, (x, b, cast, span, height, diag, relax))
    parts = coarse_parts(visc, level.residual(values), scratch)
    i, j = iota((BS, BS), 0), iota((BS, BS), 1)
    merge = (i // 2 == j) & (i >= 8) & (i < 120)
    total = product(parts, merge)
    for k in range(HZ):
        merged[k] = total[HALF * k : HALF * (k + 1)]


def edge_kernel(
    right, left, inner, merged, x, b, cast, span, height, diag, relax,
    x1, b1, cast1, span1, height1, relax1, slots, scratch, rows8,
):
    first, last, outside = beyond(ROWS, HALO)
    lane = iota((ROWS, BS), 1) % 64
    fields = []
    for a in range(2):
        slabs = []
        for k in range(PACK):
            group, sub = divmod(k, 4)
            l = shift(left[a, group], -16 * sub, 1)
            r = shift(right[a, group], 48 - 16 * sub, 1)
            value = jnp.where(lane < 16, l, jnp.where(lane >= 48, r, inner[a, k]))
            slabs.append(ends(value, first, last, HALO) if a == 0 else value)
        fields.append(slabs)
    visc, source = fields
    level = fine_level(visc, source, outside, True)
    values = level.sweep(level.start())
    keep(level, values, (x, b, cast, span, height, diag, relax))
    parts = coarse_parts(visc, level.residual(values), scratch)
    i, j = iota((BS, 2 * BS), 0), iota((BS, 2 * BS), 1)
    m, ring_lane = i % 64, j % BS
    target = jnp.where(m < 24, (m // 2 + 120) % BS, m // 2 + 40)
    used = (m < 24) | (m >= 40)
    merge = used & (target == ring_lane) & (i // 64 == j // BS)
    total = product(parts, merge)

    edge = HALO // 2
    first, last, outside = beyond(HALF, edge)
    weight = jnp.where(outside, 0.0, WEIGHT)
    coarse = []
    for k in range(HZ):
        a, z = divmod(k, 8)
        side, pos = divmod(z, 4)
        row = HALF * (4 * a + pos)
        coarse.append(merged[k] + total[row : row + HALF, BS * side : BS * (side + 1)])
    lane = iota((HALF, BS), 1)
    known = (lane < 72) | (lane >= 120)
    coeff = [jnp.where(known, 0.125 * ends(c, first, last, edge), 1.0) for c in coarse[:8]]
    source = [0.5 * c for c in coarse[8:]]
    height = height_faces(coeff)
    cast_faces = [harmonic(shift(c, 1, 0), c) for c in coeff]
    span_faces = [harmonic(shift(c, 1, 1), c) for c in coeff]
    diagonal = [diagonal_of(cast_faces[z], span_faces[z], height[z], height[z + 1]) for z in range(8)]
    level = Level(cast_faces, span_faces, height, diagonal, [weight / d for d in diagonal], source, 8)
    values = level.sweep(level.start())
    for ref, items in ((x1, values), (b1, source), (cast1, cast_faces), (span1, span_faces), (height1, height), (relax1, level.relax)):
        for z, item in enumerate(items):
            ref[z] = item
    remains = level.residual(values)

    i, j = iota((4 * BS, BS), 0), iota((4 * BS, BS), 1)
    move = (i % BS < 64) & (i % BS // 2 + 32 * (i // BS) == j)
    fields = []
    for k in range(4):
        rows = slice(edge, edge + 8)
        c = coeff[2 * k][rows] + coeff[2 * k + 1][rows]
        r = remains[2 * k][rows] + remains[2 * k + 1][rows]
        rows8[k] = jnp.concatenate([0.125 * c, 0.5 * r], axis=0)
        fields.append(rows8[k, pl.ds(0, 8, stride=2), :] + rows8[k, pl.ds(1, 8, stride=2), :])
    total = product(jnp.concatenate(fields, axis=1), move)
    for d in range(slots.shape[0]):
        slots[d] = total


def ascent_kernel(
    own, right, left,
    xo, bo, casto, spano, heighto, diago, relaxo,
    xe, be, caste, spane, heighte, diage, relaxe,
    x1, b1, cast1, span1, height1, relax1,
    solution_out, residual_out, tiles, pairs, wide2, padded2, wide1, wide_own, wide_edge, results, sems,
):
    count = own.shape[0]
    rows = 4 * count
    lane = iota((rows, 128), 1)
    index = lax.axis_index("cast")

    fields = []
    for part in range(2):
        for s, block in enumerate((own, right, left)):
            for d in range(count):
                tiles[s, 4 * d : 4 * d + 4] = block[d, 4 * part : 4 * part + 4]
        slabs = []
        for z in range(4):
            o = shift(tiles[0], -32 * z, 1)
            r = shift(tiles[1], 32 - 32 * z, 1)
            l = shift(tiles[2], 96 - 32 * z, 1)
            fill = 1.0 if part == 0 else 0.0
            slabs.append(jnp.where(lane < 32, o, jnp.where(lane < 64, r, jnp.where(lane >= 96, l, fill))))
        fields.append(slabs)
    coeff2, source2 = fields
    level2 = whole_level(coeff2, source2)
    x2 = level2.sweep(level2.start())
    remains = level2.residual(x2)

    a, b = iota((128, 128), 0), iota((128, 128), 1)
    narrow = ((a < 64) & (a // 2 == b)) | ((a >= 96) & (a // 2 + 64 == b))
    widen = ((b < 64) & (b // 2 == a)) | ((b >= 96) & (b // 2 + 64 == a))
    gathered = []
    for field in (coeff2, remains):
        for k in range(2):
            gathered.append(pair_rows(field[2 * k] + field[2 * k + 1], pairs))
    merged = product(jnp.concatenate(gathered, axis=0), narrow)
    half = rows // 2
    lane3 = iota((half, 128), 1)
    known = (lane3 < 32) | (lane3 >= 112)
    coeff3 = [jnp.where(known, 0.125 * merged[half * k : half * (k + 1)], 1.0) for k in range(2)]
    source3 = [0.5 * merged[half * (2 + k) : half * (3 + k)] for k in range(2)]
    level3 = whole_level(coeff3, source3)
    x3 = level3.start()
    for _ in range(SWEEPS_COARSE - 1):
        x3 = level3.sweep(x3)

    spread = product(jnp.concatenate(x3, axis=0), widen)
    for k in range(2):
        wide2[k, pl.ds(0, half, stride=2), :] = spread[half * k : half * (k + 1)]
        wide2[k, pl.ds(1, half, stride=2), :] = spread[half * k : half * (k + 1)]
    x2 = [x2[z] + wide2[z // 2] for z in range(4)]
    x2 = level2.sweep(level2.sweep(x2))

    for z in range(4):
        padded2[z, 0:8] = jnp.zeros((8, 128), F32)
        padded2[z, 8 : 8 + rows] = x2[z]
        padded2[z, 8 + rows : 16 + rows] = jnp.zeros((8, 128), F32)
    grow = ((b < 96) & (b // 2 == a)) | ((b >= 96) & (b // 2 + 64 == a))
    local = [padded2[z, pl.ds(4 * index + 4, 16), :] for z in range(4)]
    spread = product(jnp.concatenate(local, axis=0), grow)
    for z in range(4):
        wide1[z, pl.ds(0, 16, stride=2), :] = spread[16 * z : 16 * z + 16]
        wide1[z, pl.ds(1, 16, stride=2), :] = spread[16 * z : 16 * z + 16]
    level1 = Level(cast1, span1, height1, None, relax1, b1, 8)
    x = [x1[z] + wide1[z // 2, 0:HALF] for z in range(8)]
    x = level1.sweep(level1.sweep(x))

    i, j = iota((BS, BS), 0), iota((BS, BS), 1)
    spread = product(jnp.concatenate(x, axis=0), j // 2 == i)
    for z in range(8):
        for s in range(2):
            wide_own[z, pl.ds(s, HALF, stride=2), :] = spread[HALF * z : HALF * (z + 1)]
    i, j = iota((2 * BS, BS), 0), iota((2 * BS, BS), 1)
    m = j % 64
    origin = jnp.where(m < 32, (m // 2 + 120) % BS, m // 2 + 40)
    expand = (origin == i % BS) & (i // BS == j // 64)
    sides = [jnp.concatenate([x[k], x[k + 4]], axis=1) for k in range(4)]
    spread = product(jnp.concatenate(sides, axis=0), expand)
    for k in range(4):
        for s in range(2):
            wide_edge[k, pl.ds(s, HALF, stride=2), :] = spread[HALF * k : HALF * (k + 1)]
    level_own = Level(casto, spano, heighto, diago, relaxo, bo, HZ)
    level_edge = Level(caste, spane, heighte, diage, relaxe, be, PACK, True)
    own_x = [xo[z] + wide_own[z // 2, CUT] for z in range(HZ)]
    edge_x = [xe[k] + wide_edge[k // 2, CUT] for k in range(PACK)]
    edge_x = level_edge.sweep(level_edge.sweep(edge_x))
    own_x = level_own.sweep(level_own.sweep(own_x))
    lane = iota((BC, BS), 1)
    rows = slice(4, 4 + BC)

    def give(number, out, mid, side):
        for z in range(HZ):
            half, k = divmod(z, PACK)
            low = shift(side[k][rows], -16 - 64 * half, 1)
            high = shift(side[k][rows], 80 - 64 * half, 1)
            results[number, z] = jnp.where(lane < 8, low, jnp.where(lane >= 120, high, mid[z][rows]))
        copy = pltpu.make_async_copy(results.at[number], out, sems.at[number])
        copy.start()
        return copy

    first = give(0, solution_out, own_x, edge_x)
    second = give(1, residual_out, level_own.residual(own_x), level_edge.residual(edge_x))
    first.wait()
    second.wait()


VMEM = pl.BlockSpec(memory_space=pltpu.VMEM)
HBM = pl.BlockSpec(memory_space=pltpu.HBM)
PARAMS = pltpu.CompilerParams(vmem_limit_bytes=16 * 1024 * 1024)
INTERPRET = False


def call(kernel, in_specs, outs, scratch=(), out_spec=VMEM):
    return pl.pallas_call(
        kernel,
        in_specs=in_specs,
        out_specs=[out_spec] * len(outs),
        out_shape=[jax.ShapeDtypeStruct(s, F32) for s in outs],
        scratch_shapes=[pltpu.VMEM(s, F32) if isinstance(s, tuple) else s for s in scratch],
        compiler_params=PARAMS,
        interpret=INTERPRET,
    )


def ring(value, axis, step):
    size = lax.axis_size(axis)
    return lax.ppermute(value, axis, [(i, (i + step) % size) for i in range(size)])


def shards(phase, viscosity_table, pressure_source):
    count = lax.axis_size("cast")
    packed = (2, 2, ROWS, BS)
    own_state = [(HZ, KEPT, BS)] * 4 + [(HZ + 1, KEPT, BS)] + [(HZ, KEPT, BS)] * 2
    edge_state = [(PACK, KEPT, BS)] * 4 + [(PACK + 1, KEPT, BS)] + [(PACK, KEPT, BS)] * 2
    level1_state = [(8, HALF, BS)] * 4 + [(9, HALF, BS), (8, HALF, BS)]

    arguments = (pltpu.with_memory_space_constraint(a, pltpu.HBM) for a in (viscosity_table, phase, pressure_source))
    stage_scratch = [pltpu.SMEM((3,), F32), pltpu.VMEM((HZ, BC, BS), jnp.int32), pltpu.SemaphoreType.DMA((3,))]
    (own,) = call(stage_kernel, [HBM] * 3, [(2, HZ, BC, BS)], stage_scratch)(*arguments)
    before = ring(own, "cast", 1)
    after = ring(own, "cast", -1)
    first, last = call(margin_kernel, [VMEM] * 3, [packed, packed])(own, before, after)
    right = ring(first, "span", -1)
    left = ring(last, "span", 1)
    *kept_own, merged, inner = call(
        own_kernel,
        [VMEM] * 3,
        own_state + [(HZ, HALF, BS), (2, PACK, ROWS, BS)],
        [(HZ, ROWS, BS)],
    )(own, before, after)
    *kept_edge, slots = call(
        edge_kernel,
        [VMEM] * 4,
        edge_state + level1_state + [(count, 8, BS)],
        [(8, ROWS, BS), (4, 16, BS)],
    )(right, left, inner, merged)

    column = lax.all_to_all(slots, "cast", 0, 0)
    column_left = ring(column, "span", 1)
    column_right = ring(column, "span", -1)
    rows = 4 * count
    scratch = [
        (3, rows, BS),
        (rows, BS),
        (2, rows, BS),
        (4, rows + 16, BS),
        (4, 32, BS),
        (8, ROWS, BS),
        (4, ROWS, BS),
        (2, HZ, BC, BS),
        pltpu.SemaphoreType.DMA((2,)),
    ]
    state = kept_own + kept_edge
    return tuple(
        call(ascent_kernel, [VMEM] * (3 + len(state)), [(HZ, BC, BS)] * 2, scratch, HBM)(
            column, column_right, column_left, *state
        )
    )


def solution(mesh):
    blocks = P(None, "cast", "span")
    return jax.shard_map(
        shards,
        mesh=mesh,
        in_specs=(blocks, P(), blocks),
        out_specs=(blocks, blocks),
        check_vma=False,
    )
```

```python
import jax
import jax.numpy as jnp
from jax import lax
from jax.experimental import pallas as pl
from jax.experimental.pallas import tpu as pltpu
from jax.sharding import PartitionSpec as P

HZ, BC, BS = 16, 16, 128
HALO = 16
ROWS = BC + 2 * HALO
CUT = slice(HALO - 4, HALO + BC + 4)
KEPT = BC + 8
HALF = ROWS // 2
PACK = HZ // 2
SWEEPS_COARSE = 8
WEIGHT = 0.8
F32 = jnp.float32
BF16 = jnp.bfloat16


def shift(x, step, axis):
    return pltpu.roll(x, step % x.shape[axis], axis)


def iota(shape, axis):
    return lax.broadcasted_iota(jnp.int32, shape, axis)


def product(a, where):
    b = jnp.where(where, 1.0, 0.0).astype(BF16)
    high = a.astype(BF16)
    low = (a - high.astype(F32)).astype(BF16)
    return jnp.dot(high, b, preferred_element_type=F32) + jnp.dot(low, b, preferred_element_type=F32)


def harmonic(a, b):
    return 2.0 * a * b / (a + b)


def near(x, below, above, cast, span, low, high):
    return (
        cast * shift(x, 1, 0)
        + shift(cast * x, -1, 0)
        + span * shift(x, 1, 1)
        + shift(span * x, -1, 1)
        + low * below
        + high * above
    )


def diagonal_of(cast, span, low, high):
    return cast + shift(cast, -1, 0) + span + shift(span, -1, 1) + low + high


class Level:
    def __init__(self, cast, span, height, diag, relax, source, depth, packed=False):
        self.cast, self.span, self.height = cast, span, height
        self.diag, self.relax, self.source = diag, relax, source
        self.depth, self.packed = depth, packed

    def near(self, x, z):
        last = self.depth - 1
        below, above = x[max(z - 1, 0)], x[min(z + 1, last)]
        if self.packed and z == 0:
            below = shift(x[last], 64, 1)
        if self.packed and z == last:
            above = shift(x[0], 64, 1)
        return near(x[z], below, above, self.cast[z], self.span[z], self.height[z], self.height[z + 1])

    def start(self):
        return [self.relax[z] * self.source[z] for z in range(self.depth)]

    def sweep(self, x):
        return [
            (1.0 - WEIGHT) * x[z] + self.relax[z] * (self.near(x, z) + self.source[z])
            for z in range(self.depth)
        ]

    def residual(self, x):
        return [self.source[z] - self.diag[z] * x[z] + self.near(x, z) for z in range(self.depth)]


def fine_level(visc, source, outside, packed):
    depth = len(visc)
    shape = visc[0].shape
    weight = jnp.where(outside, 0.0, WEIGHT)
    cast = [2.0 / (v + shift(v, 1, 0)) for v in visc]
    span = [2.0 / (v + shift(v, 1, 1)) for v in visc]
    inner = [2.0 / (a + b) for a, b in zip(visc[:-1], visc[1:])]
    if packed:
        bottom = jnp.where(iota(shape, 1) < 64, 0.0, 2.0 / (visc[0] + shift(visc[-1], 64, 1)))
        top = shift(bottom, 64, 1)
    else:
        bottom = top = jnp.zeros(shape, F32)
    height = [bottom] + inner + [top]
    diag = [diagonal_of(cast[z], span[z], height[z], height[z + 1]) for z in range(depth)]
    relax = [weight / d for d in diag]
    return Level(cast, span, height, diag, relax, source, depth, packed)


def keep(level, x, refs):
    for ref, values in zip(refs, (x, level.source, level.cast, level.span, level.height, level.diag, level.relax)):
        for z, value in enumerate(values):
            ref[z] = value[CUT]


def coarse_parts(visc, remains, scratch):
    parts = []
    count = len(visc) // 2
    for a, values in enumerate(([1.0 / v for v in visc], remains)):
        for k in range(count):
            scratch[a * count + k] = values[2 * k] + values[2 * k + 1]
            ref = scratch.at[a * count + k]
            parts.append(ref[pl.ds(0, HALF, stride=2), :] + ref[pl.ds(1, HALF, stride=2), :])
    return jnp.concatenate(parts, axis=0)


def ends(value, first, last, edge):
    rows = value.shape[0]
    low = jnp.where(first, jnp.broadcast_to(value[edge : edge + 1], (edge, BS)), value[:edge])
    high = jnp.where(last, jnp.broadcast_to(value[rows - edge - 1 : rows - edge], (edge, BS)), value[rows - edge :])
    return jnp.concatenate([low, value[edge : rows - edge], high], axis=0)


def beyond(rows, edge):
    row = iota((rows, BS), 0)
    index = lax.axis_index("cast")
    first, last = index == 0, index == lax.axis_size("cast") - 1
    return first, last, (first & (row < edge)) | (last & (row >= rows - edge))


def height_faces(coeff):
    flat = jnp.zeros_like(coeff[0])
    inner = [harmonic(a, b) for a, b in zip(coeff[:-1], coeff[1:])]
    return [flat] + inner + [flat]


def whole_level(coeff, source):
    shape = coeff[0].shape
    row = iota(shape, 0)
    height = height_faces(coeff)
    cast, span, diag, relax = [], [], [], []
    for z, c in enumerate(coeff):
        lower = jnp.where(row == 0, 0.0, harmonic(shift(c, 1, 0), c))
        ends = jnp.where((row == 0) | (row == shape[0] - 1), c, 0.0)
        side = harmonic(shift(c, 1, 1), c)
        total = diagonal_of(lower, side, height[z], height[z + 1]) + ends
        cast.append(lower)
        span.append(side)
        diag.append(total)
        relax.append(WEIGHT / total)
    return Level(cast, span, height, diag, relax, source, len(coeff))


def pair_rows(value, scratch):
    rows = value.shape[0]
    scratch[...] = value
    return scratch[pl.ds(0, rows // 2, stride=2), :] + scratch[pl.ds(1, rows // 2, stride=2), :]


def by_side(axis, near_pair, far_pair):
    even = lax.rem(lax.axis_index(axis), 2) == 0
    return jnp.where(even, far_pair, near_pair), jnp.where(even, near_pair, far_pair)


def extended(own, near_pair, far_pair, a, z):
    before, after = by_side("cast", near_pair[a, z], far_pair[a, z])
    return jnp.concatenate([before, own[a, z], after], axis=0)


def stage_kernel(table_in, phase_in, source_in, out, table, phase, sems):
    copies = [
        pltpu.make_async_copy(table_in, table, sems.at[0]),
        pltpu.make_async_copy(phase_in, phase, sems.at[1]),
        pltpu.make_async_copy(source_in, out.at[1], sems.at[2]),
    ]
    for copy in copies:
        copy.start()
    copies[0].wait()
    copies[1].wait()
    for z in range(HZ):
        p = phase[z]
        out[0, z] = jnp.where(p == 0, table[0], jnp.where(p == 1, table[1], table[2]))
    copies[2].wait()


def margin_kernel(own, near_cast, far_cast, far_span, near_span):
    lane = iota((ROWS, BS), 1)
    for a in range(2):
        for group in range(2):
            head = tail = None
            for sub in range(4):
                for half in range(2):
                    z = group * 4 + sub + 8 * half
                    start = 16 * sub + 64 * half
                    slab = extended(own, near_cast, far_cast, a, z)
                    h = shift(slab, start, 1)
                    t = shift(slab, start + HALO, 1)
                    inside = (lane >= start) & (lane < start + HALO)
                    head = h if head is None else jnp.where(inside, h, head)
                    tail = t if tail is None else jnp.where(inside, t, tail)
            far_span[a, group], near_span[a, group] = by_side("span", tail, head)


def own_kernel(own, near_cast, far_cast, x, b, cast, span, height, diag, relax, merged, inner, scratch):
    first, last, outside = beyond(ROWS, HALO)
    visc, source = [], []
    for z in range(HZ):
        v, s = (extended(own, near_cast, far_cast, a, z) for a in range(2))
        visc.append(ends(v, first, last, HALO))
        source.append(s)
    lane = iota((ROWS, BS), 1)
    for a, field in enumerate((visc, source)):
        for k in range(PACK):
            low, high = field[k], field[k + PACK]
            inner[a, k] = jnp.where(
                lane < 32,
                shift(low, 16, 1),
                jnp.where(lane < 64, shift(low, 48, 1), jnp.where(lane < 96, shift(high, 80, 1), shift(high, 112, 1))),
            )
    level = fine_level(visc, source, outside, False)
    values = level.sweep(level.start())
    keep(level, values, (x, b, cast, span, height, diag, relax))
    parts = coarse_parts(visc, level.residual(values), scratch)
    i, j = iota((BS, BS), 0), iota((BS, BS), 1)
    merge = (i // 2 == j) & (i >= 8) & (i < 120)
    total = product(parts, merge)
    for k in range(HZ):
        merged[k] = total[HALF * k : HALF * (k + 1)]


def edge_kernel(
    far_span, near_span, inner, merged, x, b, cast, span, height, diag, relax,
    x1, b1, cast1, span1, height1, relax1, slots, scratch, rows8,
):
    first, last, outside = beyond(ROWS, HALO)
    lane = iota((ROWS, BS), 1) % 64
    fields = []
    for a in range(2):
        slabs = []
        for k in range(PACK):
            group, sub = divmod(k, 4)
            left, right = by_side("span", near_span[a, group], far_span[a, group])
            l = shift(left, -16 * sub, 1)
            r = shift(right, 48 - 16 * sub, 1)
            value = jnp.where(lane < 16, l, jnp.where(lane >= 48, r, inner[a, k]))
            slabs.append(ends(value, first, last, HALO) if a == 0 else value)
        fields.append(slabs)
    visc, source = fields
    level = fine_level(visc, source, outside, True)
    values = level.sweep(level.start())
    keep(level, values, (x, b, cast, span, height, diag, relax))
    parts = coarse_parts(visc, level.residual(values), scratch)
    i, j = iota((BS, 2 * BS), 0), iota((BS, 2 * BS), 1)
    m, ring_lane = i % 64, j % BS
    target = jnp.where(m < 24, (m // 2 + 120) % BS, m // 2 + 40)
    used = (m < 24) | (m >= 40)
    merge = used & (target == ring_lane) & (i // 64 == j // BS)
    total = product(parts, merge)

    edge = HALO // 2
    first, last, outside = beyond(HALF, edge)
    weight = jnp.where(outside, 0.0, WEIGHT)
    coarse = []
    for k in range(HZ):
        a, z = divmod(k, 8)
        side, pos = divmod(z, 4)
        row = HALF * (4 * a + pos)
        coarse.append(merged[k] + total[row : row + HALF, BS * side : BS * (side + 1)])
    lane = iota((HALF, BS), 1)
    known = (lane < 72) | (lane >= 120)
    coeff = [jnp.where(known, 0.125 * ends(c, first, last, edge), 1.0) for c in coarse[:8]]
    source = [0.5 * c for c in coarse[8:]]
    height = height_faces(coeff)
    cast_faces = [harmonic(shift(c, 1, 0), c) for c in coeff]
    span_faces = [harmonic(shift(c, 1, 1), c) for c in coeff]
    diagonal = [diagonal_of(cast_faces[z], span_faces[z], height[z], height[z + 1]) for z in range(8)]
    level = Level(cast_faces, span_faces, height, diagonal, [weight / d for d in diagonal], source, 8)
    values = level.sweep(level.start())
    for ref, items in ((x1, values), (b1, source), (cast1, cast_faces), (span1, span_faces), (height1, height), (relax1, level.relax)):
        for z, item in enumerate(items):
            ref[z] = item
    remains = level.residual(values)

    i, j = iota((4 * BS, BS), 0), iota((4 * BS, BS), 1)
    move = (i % BS < 64) & (i % BS // 2 + 32 * (i // BS) == j)
    fields = []
    for k in range(4):
        rows = slice(edge, edge + 8)
        c = coeff[2 * k][rows] + coeff[2 * k + 1][rows]
        r = remains[2 * k][rows] + remains[2 * k + 1][rows]
        rows8[k] = jnp.concatenate([0.125 * c, 0.5 * r], axis=0)
        fields.append(rows8[k, pl.ds(0, 8, stride=2), :] + rows8[k, pl.ds(1, 8, stride=2), :])
    total = product(jnp.concatenate(fields, axis=1), move)
    for d in range(slots.shape[0]):
        slots[d] = total


def ascent_kernel(
    own, near_column, far_column,
    xo, bo, casto, spano, heighto, diago, relaxo,
    xe, be, caste, spane, heighte, diage, relaxe,
    x1, b1, cast1, span1, height1, relax1,
    solution_out, residual_out, tiles, pairs, wide2, padded2, wide1, wide_own, wide_edge, results, sems,
):
    count = own.shape[0]
    rows = 4 * count
    lane = iota((rows, 128), 1)
    index = lax.axis_index("cast")

    fields = []
    for part in range(2):
        for d in range(count):
            rows_d = slice(4 * part, 4 * part + 4)
            left, right = by_side("span", near_column[d, rows_d], far_column[d, rows_d])
            for s, block in enumerate((own[d, rows_d], right, left)):
                tiles[s, 4 * d : 4 * d + 4] = block
        slabs = []
        for z in range(4):
            o = shift(tiles[0], -32 * z, 1)
            r = shift(tiles[1], 32 - 32 * z, 1)
            l = shift(tiles[2], 96 - 32 * z, 1)
            fill = 1.0 if part == 0 else 0.0
            slabs.append(jnp.where(lane < 32, o, jnp.where(lane < 64, r, jnp.where(lane >= 96, l, fill))))
        fields.append(slabs)
    coeff2, source2 = fields
    level2 = whole_level(coeff2, source2)
    x2 = level2.sweep(level2.start())
    remains = level2.residual(x2)

    a, b = iota((128, 128), 0), iota((128, 128), 1)
    narrow = ((a < 64) & (a // 2 == b)) | ((a >= 96) & (a // 2 + 64 == b))
    widen = ((b < 64) & (b // 2 == a)) | ((b >= 96) & (b // 2 + 64 == a))
    gathered = []
    for field in (coeff2, remains):
        for k in range(2):
            gathered.append(pair_rows(field[2 * k] + field[2 * k + 1], pairs))
    merged = product(jnp.concatenate(gathered, axis=0), narrow)
    half = rows // 2
    lane3 = iota((half, 128), 1)
    known = (lane3 < 32) | (lane3 >= 112)
    coeff3 = [jnp.where(known, 0.125 * merged[half * k : half * (k + 1)], 1.0) for k in range(2)]
    source3 = [0.5 * merged[half * (2 + k) : half * (3 + k)] for k in range(2)]
    level3 = whole_level(coeff3, source3)
    x3 = level3.start()
    for _ in range(SWEEPS_COARSE - 1):
        x3 = level3.sweep(x3)

    spread = product(jnp.concatenate(x3, axis=0), widen)
    for k in range(2):
        wide2[k, pl.ds(0, half, stride=2), :] = spread[half * k : half * (k + 1)]
        wide2[k, pl.ds(1, half, stride=2), :] = spread[half * k : half * (k + 1)]
    x2 = [x2[z] + wide2[z // 2] for z in range(4)]
    x2 = level2.sweep(level2.sweep(x2))

    for z in range(4):
        padded2[z, 0:8] = jnp.zeros((8, 128), F32)
        padded2[z, 8 : 8 + rows] = x2[z]
        padded2[z, 8 + rows : 16 + rows] = jnp.zeros((8, 128), F32)
    grow = ((b < 96) & (b // 2 == a)) | ((b >= 96) & (b // 2 + 64 == a))
    local = [padded2[z, pl.ds(4 * index + 4, 16), :] for z in range(4)]
    spread = product(jnp.concatenate(local, axis=0), grow)
    for z in range(4):
        wide1[z, pl.ds(0, 16, stride=2), :] = spread[16 * z : 16 * z + 16]
        wide1[z, pl.ds(1, 16, stride=2), :] = spread[16 * z : 16 * z + 16]
    level1 = Level(cast1, span1, height1, None, relax1, b1, 8)
    x = [x1[z] + wide1[z // 2, 0:HALF] for z in range(8)]
    x = level1.sweep(level1.sweep(x))

    i, j = iota((BS, BS), 0), iota((BS, BS), 1)
    spread = product(jnp.concatenate(x, axis=0), j // 2 == i)
    for z in range(8):
        for s in range(2):
            wide_own[z, pl.ds(s, HALF, stride=2), :] = spread[HALF * z : HALF * (z + 1)]
    i, j = iota((2 * BS, BS), 0), iota((2 * BS, BS), 1)
    m = j % 64
    origin = jnp.where(m < 32, (m // 2 + 120) % BS, m // 2 + 40)
    expand = (origin == i % BS) & (i // BS == j // 64)
    sides = [jnp.concatenate([x[k], x[k + 4]], axis=1) for k in range(4)]
    spread = product(jnp.concatenate(sides, axis=0), expand)
    for k in range(4):
        for s in range(2):
            wide_edge[k, pl.ds(s, HALF, stride=2), :] = spread[HALF * k : HALF * (k + 1)]
    level_own = Level(casto, spano, heighto, diago, relaxo, bo, HZ)
    level_edge = Level(caste, spane, heighte, diage, relaxe, be, PACK, True)
    own_x = [xo[z] + wide_own[z // 2, CUT] for z in range(HZ)]
    edge_x = [xe[k] + wide_edge[k // 2, CUT] for k in range(PACK)]
    edge_x = level_edge.sweep(level_edge.sweep(edge_x))
    own_x = level_own.sweep(level_own.sweep(own_x))
    lane = iota((BC, BS), 1)
    rows = slice(4, 4 + BC)

    def give(number, out, mid, side):
        for z in range(HZ):
            half, k = divmod(z, PACK)
            low = shift(side[k][rows], -16 - 64 * half, 1)
            high = shift(side[k][rows], 80 - 64 * half, 1)
            results[number, z] = jnp.where(lane < 8, low, jnp.where(lane >= 120, high, mid[z][rows]))
        copy = pltpu.make_async_copy(results.at[number], out, sems.at[number])
        copy.start()
        return copy

    first = give(0, solution_out, own_x, edge_x)
    second = give(1, residual_out, level_own.residual(own_x), level_edge.residual(edge_x))
    first.wait()
    second.wait()


VMEM = pl.BlockSpec(memory_space=pltpu.VMEM)
HBM = pl.BlockSpec(memory_space=pltpu.HBM)
PARAMS = pltpu.CompilerParams(vmem_limit_bytes=16 * 1024 * 1024)
INTERPRET = False


def call(kernel, in_specs, outs, scratch=(), out_spec=VMEM):
    return pl.pallas_call(
        kernel,
        in_specs=in_specs,
        out_specs=[out_spec] * len(outs),
        out_shape=[jax.ShapeDtypeStruct(s, F32) for s in outs],
        scratch_shapes=[pltpu.VMEM(s, F32) if isinstance(s, tuple) else s for s in scratch],
        compiler_params=PARAMS,
        interpret=INTERPRET,
    )


def swap(value, axis, far, periodic):
    size = lax.axis_size(axis)
    partner = [i ^ 1 for i in range(size)]
    if far:
        partner = [((i - 1) ^ 1) + 1 for i in range(size)]
        partner = [p % size if periodic or 0 <= p < size else i for i, p in enumerate(partner)]
        if not periodic:
            partner[0], partner[-1] = 0, size - 1
    return lax.ppermute(value, axis, list(enumerate(partner)))


def shards(phase, viscosity_table, pressure_source):
    count = lax.axis_size("cast")
    packed = (2, 2, ROWS, BS)
    own_state = [(HZ, KEPT, BS)] * 4 + [(HZ + 1, KEPT, BS)] + [(HZ, KEPT, BS)] * 2
    edge_state = [(PACK, KEPT, BS)] * 4 + [(PACK + 1, KEPT, BS)] + [(PACK, KEPT, BS)] * 2
    level1_state = [(8, HALF, BS)] * 4 + [(9, HALF, BS), (8, HALF, BS)]

    arguments = (pltpu.with_memory_space_constraint(a, pltpu.HBM) for a in (viscosity_table, phase, pressure_source))
    stage_scratch = [pltpu.SMEM((3,), F32), pltpu.VMEM((HZ, BC, BS), jnp.int32), pltpu.SemaphoreType.DMA((3,))]
    (own,) = call(stage_kernel, [HBM] * 3, [(2, HZ, BC, BS)], stage_scratch)(*arguments)
    far_cast = swap(own, "cast", True, False)
    near_cast = swap(own, "cast", False, False)
    far_span, near_span = call(margin_kernel, [VMEM] * 3, [packed, packed])(own, near_cast, far_cast)
    far_span = swap(far_span, "span", True, True)
    near_span = swap(near_span, "span", False, True)
    *kept_own, merged, inner = call(
        own_kernel,
        [VMEM] * 3,
        own_state + [(HZ, HALF, BS), (2, PACK, ROWS, BS)],
        [(HZ, ROWS, BS)],
    )(own, near_cast, far_cast)
    *kept_edge, slots = call(
        edge_kernel,
        [VMEM] * 4,
        edge_state + level1_state + [(count, 8, BS)],
        [(8, ROWS, BS), (4, 16, BS)],
    )(far_span, near_span, inner, merged)

    column = lax.all_to_all(slots, "cast", 0, 0)
    far_column = swap(column, "span", True, True)
    near_column = swap(column, "span", False, True)
    rows = 4 * count
    scratch = [
        (3, rows, BS),
        (rows, BS),
        (2, rows, BS),
        (4, rows + 16, BS),
        (4, 32, BS),
        (8, ROWS, BS),
        (4, ROWS, BS),
        (2, HZ, BC, BS),
        pltpu.SemaphoreType.DMA((2,)),
    ]
    state = kept_own + kept_edge
    return tuple(
        call(ascent_kernel, [VMEM] * (3 + len(state)), [(HZ, BC, BS)] * 2, scratch, HBM)(
            column, near_column, far_column, *state
        )
    )


def solution(mesh):
    blocks = P(None, "cast", "span")
    return jax.shard_map(
        shards,
        mesh=mesh,
        in_specs=(blocks, P(), blocks),
        out_specs=(blocks, blocks),
        check_vma=False,
    )
```

```python
import jax
import jax.numpy as jnp
from jax import lax
from jax.experimental import pallas as pl
from jax.experimental.pallas import tpu as pltpu
from jax.sharding import PartitionSpec as P

HZ, BC, BS = 16, 16, 128
HALO = 16
ROWS = BC + 2 * HALO
CUT = slice(HALO - 4, HALO + BC + 4)
KEPT = BC + 8
HALF = ROWS // 2
SENT = BC + 16
PACK = HZ // 2
SWEEPS_COARSE = 8
WEIGHT = 0.8
F32 = jnp.float32
BF16 = jnp.bfloat16


def shift(x, step, axis):
    return pltpu.roll(x, step % x.shape[axis], axis)


def iota(shape, axis):
    return lax.broadcasted_iota(jnp.int32, shape, axis)


def product(a, where):
    b = jnp.where(where, 1.0, 0.0).astype(BF16)
    high = a.astype(BF16)
    low = (a - high.astype(F32)).astype(BF16)
    return jnp.dot(high, b, preferred_element_type=F32) + jnp.dot(low, b, preferred_element_type=F32)


def harmonic(a, b):
    return 2.0 * a * b / (a + b)


def near(x, below, above, cast, span, low, high):
    return (
        cast * shift(x, 1, 0)
        + shift(cast * x, -1, 0)
        + span * shift(x, 1, 1)
        + shift(span * x, -1, 1)
        + low * below
        + high * above
    )


def diagonal_of(cast, span, low, high):
    return cast + shift(cast, -1, 0) + span + shift(span, -1, 1) + low + high


class Level:
    def __init__(self, cast, span, height, diag, relax, source, depth, packed=False):
        self.cast, self.span, self.height = cast, span, height
        self.diag, self.relax, self.source = diag, relax, source
        self.depth, self.packed = depth, packed

    def near(self, x, z):
        last = self.depth - 1
        below, above = x[max(z - 1, 0)], x[min(z + 1, last)]
        if self.packed and z == 0:
            below = shift(x[last], 64, 1)
        if self.packed and z == last:
            above = shift(x[0], 64, 1)
        return near(x[z], below, above, self.cast[z], self.span[z], self.height[z], self.height[z + 1])

    def start(self):
        return [self.relax[z] * self.source[z] for z in range(self.depth)]

    def sweep(self, x):
        return [
            (1.0 - WEIGHT) * x[z] + self.relax[z] * (self.near(x, z) + self.source[z])
            for z in range(self.depth)
        ]

    def residual(self, x):
        return [self.source[z] - self.diag[z] * x[z] + self.near(x, z) for z in range(self.depth)]


def fine_level(visc, source, outside, packed):
    depth = len(visc)
    shape = visc[0].shape
    weight = jnp.where(outside, 0.0, WEIGHT)
    cast = [2.0 / (v + shift(v, 1, 0)) for v in visc]
    span = [2.0 / (v + shift(v, 1, 1)) for v in visc]
    inner = [2.0 / (a + b) for a, b in zip(visc[:-1], visc[1:])]
    if packed:
        bottom = jnp.where(iota(shape, 1) < 64, 0.0, 2.0 / (visc[0] + shift(visc[-1], 64, 1)))
        top = shift(bottom, 64, 1)
    else:
        bottom = top = jnp.zeros(shape, F32)
    height = [bottom] + inner + [top]
    diag = [diagonal_of(cast[z], span[z], height[z], height[z + 1]) for z in range(depth)]
    relax = [weight / d for d in diag]
    return Level(cast, span, height, diag, relax, source, depth, packed)


def keep(level, x, refs):
    for ref, values in zip(refs, (x, level.source, level.cast, level.span, level.height, level.diag, level.relax)):
        for z, value in enumerate(values):
            ref[z] = value[CUT]


def coarse_parts(visc, remains, scratch):
    parts = []
    count = len(visc) // 2
    for a, values in enumerate(([1.0 / v for v in visc], remains)):
        for k in range(count):
            scratch[a * count + k] = values[2 * k] + values[2 * k + 1]
            ref = scratch.at[a * count + k]
            parts.append(ref[pl.ds(0, HALF, stride=2), :] + ref[pl.ds(1, HALF, stride=2), :])
    return jnp.concatenate(parts, axis=0)


def ends(value, first, last, edge):
    rows = value.shape[0]
    low = jnp.where(first, jnp.broadcast_to(value[edge : edge + 1], (edge, BS)), value[:edge])
    high = jnp.where(last, jnp.broadcast_to(value[rows - edge - 1 : rows - edge], (edge, BS)), value[rows - edge :])
    return jnp.concatenate([low, value[edge : rows - edge], high], axis=0)


def beyond(rows, edge):
    row = iota((rows, BS), 0)
    index = lax.axis_index("cast")
    first, last = index == 0, index == lax.axis_size("cast") - 1
    return first, last, (first & (row < edge)) | (last & (row >= rows - edge))


def height_faces(coeff):
    flat = jnp.zeros_like(coeff[0])
    inner = [harmonic(a, b) for a, b in zip(coeff[:-1], coeff[1:])]
    return [flat] + inner + [flat]


def whole_level(coeff, source):
    shape = coeff[0].shape
    row = iota(shape, 0)
    height = height_faces(coeff)
    cast, span, diag, relax = [], [], [], []
    for z, c in enumerate(coeff):
        lower = jnp.where(row == 0, 0.0, harmonic(shift(c, 1, 0), c))
        ends = jnp.where((row == 0) | (row == shape[0] - 1), c, 0.0)
        side = harmonic(shift(c, 1, 1), c)
        total = diagonal_of(lower, side, height[z], height[z + 1]) + ends
        cast.append(lower)
        span.append(side)
        diag.append(total)
        relax.append(WEIGHT / total)
    return Level(cast, span, height, diag, relax, source, len(coeff))


def pair_rows(value, scratch):
    rows = value.shape[0]
    scratch[...] = value
    return scratch[pl.ds(0, rows // 2, stride=2), :] + scratch[pl.ds(1, rows // 2, stride=2), :]


def by_side(axis, near_pair, far_pair):
    even = lax.rem(lax.axis_index(axis), 2) == 0
    return jnp.where(even, far_pair, near_pair), jnp.where(even, near_pair, far_pair)


def extended(own, near_pair, far_pair, a, z):
    before, after = by_side("cast", near_pair[a, z], far_pair[a, z])
    return jnp.concatenate([before, own[a, z], after], axis=0)


def stage_kernel(table_in, phase_in, source_in, out, table, phase, sems):
    copies = [
        pltpu.make_async_copy(table_in, table, sems.at[0]),
        pltpu.make_async_copy(phase_in, phase, sems.at[1]),
        pltpu.make_async_copy(source_in, out.at[1], sems.at[2]),
    ]
    for copy in copies:
        copy.start()
    copies[0].wait()
    copies[1].wait()
    for z in range(HZ):
        p = phase[z]
        out[0, z] = jnp.where(p == 0, table[0], jnp.where(p == 1, table[1], table[2]))
    copies[2].wait()


def margin_kernel(own, near_cast, far_cast, near_span, far_span):
    lane = iota((SENT, BS), 1)
    outer = (iota((SENT, BS), 0) < 8) | (iota((SENT, BS), 0) >= SENT - 8)
    seg = lane % HALO
    for a in range(2):
        for group in range(2):
            head = tail = None
            for sub in range(4):
                for half in range(2):
                    z = group * 4 + sub + 8 * half
                    start = 16 * sub + 64 * half
                    slab = extended(own, near_cast, far_cast, a, z)
                    inner, far = slab[8 : ROWS - 8], jnp.concatenate([slab[:8], slab[8:24], slab[ROWS - 8 :]], axis=0)
                    h = jnp.where(outer & (seg >= 12), shift(far, start + 12, 1), shift(inner, start, 1))
                    t = jnp.where(outer & (seg < 4), shift(far, start + HALO - 12, 1), shift(inner, start + HALO, 1))
                    inside = (lane >= start) & (lane < start + HALO)
                    head = h if head is None else jnp.where(inside, h, head)
                    tail = t if tail is None else jnp.where(inside, t, tail)
            far_span[a, group], near_span[a, group] = by_side("span", tail, head)


def spread_rows(sent, step, more):
    moved = shift(sent, step, 1)
    return jnp.concatenate([shift(sent[:8], step + more, 1), moved, shift(sent[-8:], step + more, 1)], axis=0)


def own_kernel(own, near_cast, far_cast, x, b, cast, span, height, diag, relax, merged, inner, scratch):
    first, last, outside = beyond(ROWS, HALO)
    visc, source = [], []
    for z in range(HZ):
        v, s = (extended(own, near_cast, far_cast, a, z) for a in range(2))
        visc.append(ends(v, first, last, HALO))
        source.append(s)
    lane = iota((ROWS, BS), 1)
    for a, field in enumerate((visc, source)):
        for k in range(PACK):
            low, high = field[k], field[k + PACK]
            inner[a, k] = jnp.where(
                lane < 32,
                shift(low, 16, 1),
                jnp.where(lane < 64, shift(low, 48, 1), jnp.where(lane < 96, shift(high, 80, 1), shift(high, 112, 1))),
            )
    level = fine_level(visc, source, outside, False)
    values = level.sweep(level.start())
    keep(level, values, (x, b, cast, span, height, diag, relax))
    parts = coarse_parts(visc, level.residual(values), scratch)
    i, j = iota((BS, BS), 0), iota((BS, BS), 1)
    merge = (i // 2 == j) & (i >= 8) & (i < 120)
    total = product(parts, merge)
    for k in range(HZ):
        merged[k] = total[HALF * k : HALF * (k + 1)]


def edge_kernel(
    near_span, far_span, inner, merged, x, b, cast, span, height, diag, relax,
    x1, b1, cast1, span1, height1, relax1, slots, scratch, rows8,
):
    first, last, outside = beyond(ROWS, HALO)
    lane = iota((ROWS, BS), 1) % 64
    fields = []
    for a in range(2):
        slabs = []
        for k in range(PACK):
            group, sub = divmod(k, 4)
            left, right = by_side("span", near_span[a, group], far_span[a, group])
            l, r = spread_rows(left, -16 * sub, 12), spread_rows(right, 48 - 16 * sub, -12)
            value = jnp.where(lane < 16, l, jnp.where(lane >= 48, r, inner[a, k]))
            slabs.append(ends(value, first, last, HALO) if a == 0 else value)
        fields.append(slabs)
    visc, source = fields
    level = fine_level(visc, source, outside, True)
    values = level.sweep(level.start())
    keep(level, values, (x, b, cast, span, height, diag, relax))
    parts = coarse_parts(visc, level.residual(values), scratch)
    i, j = iota((BS, 2 * BS), 0), iota((BS, 2 * BS), 1)
    m, ring_lane = i % 64, j % BS
    target = jnp.where(m < 24, (m // 2 + 120) % BS, m // 2 + 40)
    used = (m < 24) | (m >= 40)
    merge = used & (target == ring_lane) & (i // 64 == j // BS)
    total = product(parts, merge)

    edge = HALO // 2
    first, last, outside = beyond(HALF, edge)
    weight = jnp.where(outside, 0.0, WEIGHT)
    coarse = []
    for k in range(HZ):
        a, z = divmod(k, 8)
        side, pos = divmod(z, 4)
        row = HALF * (4 * a + pos)
        coarse.append(merged[k] + total[row : row + HALF, BS * side : BS * (side + 1)])
    lane = iota((HALF, BS), 1)
    known = (lane < 72) | (lane >= 120)
    coeff = [jnp.where(known, 0.125 * ends(c, first, last, edge), 1.0) for c in coarse[:8]]
    source = [0.5 * c for c in coarse[8:]]
    height = height_faces(coeff)
    cast_faces = [harmonic(shift(c, 1, 0), c) for c in coeff]
    span_faces = [harmonic(shift(c, 1, 1), c) for c in coeff]
    diagonal = [diagonal_of(cast_faces[z], span_faces[z], height[z], height[z + 1]) for z in range(8)]
    level = Level(cast_faces, span_faces, height, diagonal, [weight / d for d in diagonal], source, 8)
    values = level.sweep(level.start())
    for ref, items in ((x1, values), (b1, source), (cast1, cast_faces), (span1, span_faces), (height1, height), (relax1, level.relax)):
        for z, item in enumerate(items):
            ref[z] = item
    remains = level.residual(values)

    i, j = iota((4 * BS, BS), 0), iota((4 * BS, BS), 1)
    move = (i % BS < 64) & (i % BS // 2 + 32 * (i // BS) == j)
    fields = []
    for k in range(4):
        rows = slice(edge, edge + 8)
        c = coeff[2 * k][rows] + coeff[2 * k + 1][rows]
        r = remains[2 * k][rows] + remains[2 * k + 1][rows]
        rows8[k] = jnp.concatenate([0.125 * c, 0.5 * r], axis=0)
        fields.append(rows8[k, pl.ds(0, 8, stride=2), :] + rows8[k, pl.ds(1, 8, stride=2), :])
    total = product(jnp.concatenate(fields, axis=1), move)
    for d in range(slots.shape[0]):
        slots[d] = total


def ascent_kernel(
    own, far_column, near_column,
    xo, bo, casto, spano, heighto, diago, relaxo,
    xe, be, caste, spane, heighte, diage, relaxe,
    x1, b1, cast1, span1, height1, relax1,
    solution_out, residual_out, tiles, pairs, wide2, padded2, wide1, wide_own, wide_edge, results, sems,
):
    count = own.shape[0]
    rows = 4 * count
    lane = iota((rows, 128), 1)
    index = lax.axis_index("cast")

    fields = []
    for part in range(2):
        for d in range(count):
            rows_d = slice(4 * part, 4 * part + 4)
            left, right = by_side("span", near_column[d, rows_d], far_column[d, rows_d])
            for s, block in enumerate((own[d, rows_d], right, left)):
                tiles[s, 4 * d : 4 * d + 4] = block
        slabs = []
        for z in range(4):
            o = shift(tiles[0], -32 * z, 1)
            r = shift(tiles[1], 32 - 32 * z, 1)
            l = shift(tiles[2], 96 - 32 * z, 1)
            fill = 1.0 if part == 0 else 0.0
            slabs.append(jnp.where(lane < 32, o, jnp.where(lane < 64, r, jnp.where(lane >= 96, l, fill))))
        fields.append(slabs)
    coeff2, source2 = fields
    level2 = whole_level(coeff2, source2)
    x2 = level2.sweep(level2.start())
    remains = level2.residual(x2)

    a, b = iota((128, 128), 0), iota((128, 128), 1)
    narrow = ((a < 64) & (a // 2 == b)) | ((a >= 96) & (a // 2 + 64 == b))
    widen = ((b < 64) & (b // 2 == a)) | ((b >= 96) & (b // 2 + 64 == a))
    gathered = []
    for field in (coeff2, remains):
        for k in range(2):
            gathered.append(pair_rows(field[2 * k] + field[2 * k + 1], pairs))
    merged = product(jnp.concatenate(gathered, axis=0), narrow)
    half = rows // 2
    lane3 = iota((half, 128), 1)
    known = (lane3 < 32) | (lane3 >= 112)
    coeff3 = [jnp.where(known, 0.125 * merged[half * k : half * (k + 1)], 1.0) for k in range(2)]
    source3 = [0.5 * merged[half * (2 + k) : half * (3 + k)] for k in range(2)]
    level3 = whole_level(coeff3, source3)
    x3 = level3.start()
    for _ in range(SWEEPS_COARSE - 1):
        x3 = level3.sweep(x3)

    spread = product(jnp.concatenate(x3, axis=0), widen)
    for k in range(2):
        wide2[k, pl.ds(0, half, stride=2), :] = spread[half * k : half * (k + 1)]
        wide2[k, pl.ds(1, half, stride=2), :] = spread[half * k : half * (k + 1)]
    x2 = [x2[z] + wide2[z // 2] for z in range(4)]
    x2 = level2.sweep(level2.sweep(x2))

    for z in range(4):
        padded2[z, 0:8] = jnp.zeros((8, 128), F32)
        padded2[z, 8 : 8 + rows] = x2[z]
        padded2[z, 8 + rows : 16 + rows] = jnp.zeros((8, 128), F32)
    grow = ((b < 96) & (b // 2 == a)) | ((b >= 96) & (b // 2 + 64 == a))
    local = [padded2[z, pl.ds(4 * index + 4, 16), :] for z in range(4)]
    spread = product(jnp.concatenate(local, axis=0), grow)
    for z in range(4):
        wide1[z, pl.ds(0, 16, stride=2), :] = spread[16 * z : 16 * z + 16]
        wide1[z, pl.ds(1, 16, stride=2), :] = spread[16 * z : 16 * z + 16]
    level1 = Level(cast1, span1, height1, None, relax1, b1, 8)
    x = [x1[z] + wide1[z // 2, 0:HALF] for z in range(8)]
    x = level1.sweep(level1.sweep(x))

    i, j = iota((BS, BS), 0), iota((BS, BS), 1)
    spread = product(jnp.concatenate(x, axis=0), j // 2 == i)
    for z in range(8):
        for s in range(2):
            wide_own[z, pl.ds(s, HALF, stride=2), :] = spread[HALF * z : HALF * (z + 1)]
    i, j = iota((2 * BS, BS), 0), iota((2 * BS, BS), 1)
    m = j % 64
    origin = jnp.where(m < 32, (m // 2 + 120) % BS, m // 2 + 40)
    expand = (origin == i % BS) & (i // BS == j // 64)
    sides = [jnp.concatenate([x[k], x[k + 4]], axis=1) for k in range(4)]
    spread = product(jnp.concatenate(sides, axis=0), expand)
    for k in range(4):
        for s in range(2):
            wide_edge[k, pl.ds(s, HALF, stride=2), :] = spread[HALF * k : HALF * (k + 1)]
    level_own = Level(casto, spano, heighto, diago, relaxo, bo, HZ)
    level_edge = Level(caste, spane, heighte, diage, relaxe, be, PACK, True)
    own_x = [xo[z] + wide_own[z // 2, CUT] for z in range(HZ)]
    edge_x = [xe[k] + wide_edge[k // 2, CUT] for k in range(PACK)]
    edge_x = level_edge.sweep(level_edge.sweep(edge_x))
    own_x = level_own.sweep(level_own.sweep(own_x))
    lane = iota((BC, BS), 1)
    rows = slice(4, 4 + BC)

    def give(number, out, mid, side):
        for z in range(HZ):
            half, k = divmod(z, PACK)
            low = shift(side[k][rows], -16 - 64 * half, 1)
            high = shift(side[k][rows], 80 - 64 * half, 1)
            results[number, z] = jnp.where(lane < 8, low, jnp.where(lane >= 120, high, mid[z][rows]))
        copy = pltpu.make_async_copy(results.at[number], out, sems.at[number])
        copy.start()
        return copy

    first = give(0, solution_out, own_x, edge_x)
    second = give(1, residual_out, level_own.residual(own_x), level_edge.residual(edge_x))
    first.wait()
    second.wait()


VMEM = pl.BlockSpec(memory_space=pltpu.VMEM)
HBM = pl.BlockSpec(memory_space=pltpu.HBM)
PARAMS = pltpu.CompilerParams(vmem_limit_bytes=16 * 1024 * 1024)
INTERPRET = False


def call(kernel, in_specs, outs, scratch=(), out_spec=VMEM):
    return pl.pallas_call(
        kernel,
        in_specs=in_specs,
        out_specs=[out_spec] * len(outs),
        out_shape=[jax.ShapeDtypeStruct(s, F32) for s in outs],
        scratch_shapes=[pltpu.VMEM(s, F32) if isinstance(s, tuple) else s for s in scratch],
        compiler_params=PARAMS,
        interpret=INTERPRET,
    )


def swap(value, axis, far):
    size = lax.axis_size(axis)
    partner = [(((i - 1) ^ 1) + 1) % size if far else i ^ 1 for i in range(size)]
    return lax.ppermute(value, axis, list(enumerate(partner)))


def shards(phase, viscosity_table, pressure_source):
    count = lax.axis_size("cast")
    packed = (2, 2, SENT, BS)
    own_state = [(HZ, KEPT, BS)] * 4 + [(HZ + 1, KEPT, BS)] + [(HZ, KEPT, BS)] * 2
    edge_state = [(PACK, KEPT, BS)] * 4 + [(PACK + 1, KEPT, BS)] + [(PACK, KEPT, BS)] * 2
    level1_state = [(8, HALF, BS)] * 4 + [(9, HALF, BS), (8, HALF, BS)]

    arguments = (pltpu.with_memory_space_constraint(a, pltpu.HBM) for a in (viscosity_table, phase, pressure_source))
    stage_scratch = [pltpu.SMEM((3,), F32), pltpu.VMEM((HZ, BC, BS), jnp.int32), pltpu.SemaphoreType.DMA((3,))]
    (own,) = call(stage_kernel, [HBM] * 3, [(2, HZ, BC, BS)], stage_scratch)(*arguments)
    far_cast = swap(own, "cast", True)
    near_cast = swap(own, "cast", False)
    near_span, far_span = call(margin_kernel, [VMEM] * 3, [packed, packed])(own, near_cast, far_cast)
    near_span = swap(near_span, "span", False)
    far_span = swap(far_span, "span", True)
    *kept_own, merged, inner = call(
        own_kernel,
        [VMEM] * 3,
        own_state + [(HZ, HALF, BS), (2, PACK, ROWS, BS)],
        [(HZ, ROWS, BS)],
    )(own, near_cast, far_cast)
    *kept_edge, slots = call(
        edge_kernel,
        [VMEM] * 4,
        edge_state + level1_state + [(count, 8, BS)],
        [(8, ROWS, BS), (4, 16, BS)],
    )(near_span, far_span, inner, merged)

    column = lax.all_to_all(slots, "cast", 0, 0)
    near_column = swap(column, "span", False)
    far_column = swap(column, "span", True)
    rows = 4 * count
    scratch = [
        (3, rows, BS),
        (rows, BS),
        (2, rows, BS),
        (4, rows + 16, BS),
        (4, 32, BS),
        (8, ROWS, BS),
        (4, ROWS, BS),
        (2, HZ, BC, BS),
        pltpu.SemaphoreType.DMA((2,)),
    ]
    state = kept_own + kept_edge
    return tuple(
        call(ascent_kernel, [VMEM] * (3 + len(state)), [(HZ, BC, BS)] * 2, scratch, HBM)(
            column, far_column, near_column, *state
        )
    )


def solution(mesh):
    blocks = P(None, "cast", "span")
    return jax.shard_map(
        shards,
        mesh=mesh,
        in_specs=(blocks, P(), blocks),
        out_specs=(blocks, blocks),
        check_vma=False,
    )
```

```python
import jax
import jax.numpy as jnp
from jax import lax
from jax.experimental import pallas as pl
from jax.experimental.pallas import tpu as pltpu
from jax.sharding import PartitionSpec as P

HZ, BC, BS = 16, 16, 128
HALO = 16
ROWS = BC + 2 * HALO
CUT = slice(HALO - 4, HALO + BC + 4)
KEPT = BC + 8
HALF = ROWS // 2
SENT = BC + 16
PACK = HZ // 2
SWEEPS_COARSE = 8
WEIGHT = 0.8
F32 = jnp.float32
BF16 = jnp.bfloat16


def shift(x, step, axis):
    return pltpu.roll(x, step % x.shape[axis], axis)


def iota(shape, axis):
    return lax.broadcasted_iota(jnp.int32, shape, axis)


def product(a, b):
    high = a.astype(BF16)
    low = (a - high.astype(F32)).astype(BF16)
    return jnp.dot(high, b, preferred_element_type=F32) + jnp.dot(low, b, preferred_element_type=F32)


def harmonic(a, b):
    return 2.0 * a * b / (a + b)


def near(x, below, above, cast, span, low, high):
    return (
        cast * shift(x, 1, 0)
        + shift(cast * x, -1, 0)
        + span * shift(x, 1, 1)
        + shift(span * x, -1, 1)
        + low * below
        + high * above
    )


def diagonal_of(cast, span, low, high):
    return cast + shift(cast, -1, 0) + span + shift(span, -1, 1) + low + high


class Level:
    def __init__(self, cast, span, height, diag, relax, source, depth, packed=False):
        self.cast, self.span, self.height = cast, span, height
        self.diag, self.relax, self.source = diag, relax, source
        self.depth, self.packed = depth, packed

    def near(self, x, z):
        last = self.depth - 1
        below, above = x[max(z - 1, 0)], x[min(z + 1, last)]
        if self.packed and z == 0:
            below = shift(x[last], 64, 1)
        if self.packed and z == last:
            above = shift(x[0], 64, 1)
        return near(x[z], below, above, self.cast[z], self.span[z], self.height[z], self.height[z + 1])

    def start(self):
        return [self.relax[z] * self.source[z] for z in range(self.depth)]

    def sweep(self, x):
        return [
            (1.0 - WEIGHT) * x[z] + self.relax[z] * (self.near(x, z) + self.source[z])
            for z in range(self.depth)
        ]

    def solve(self, sweeps):
        part = [
            (
                relax * self.cast[z],
                relax * shift(self.cast[z], -1, 0),
                relax * self.span[z],
                relax * shift(self.span[z], -1, 1),
                relax * self.height[1],
            )
            for z, relax in enumerate(self.relax)
        ]
        first = x = self.start()
        for _ in range(sweeps):
            x = [
                ((1.0 - WEIGHT) * x[z] + first[z] + part[z][4] * x[1 - z])
                + (part[z][0] * shift(x[z], 1, 0) + part[z][1] * shift(x[z], -1, 0))
                + (part[z][2] * shift(x[z], 1, 1) + part[z][3] * shift(x[z], -1, 1))
                for z in range(2)
            ]
        return x

    def residual(self, x):
        return [self.source[z] - self.diag[z] * x[z] + self.near(x, z) for z in range(self.depth)]


def fine_level(visc, source, outside, packed):
    depth = len(visc)
    shape = visc[0].shape
    weight = jnp.where(outside, 0.0, WEIGHT)
    cast = [2.0 / (v + shift(v, 1, 0)) for v in visc]
    span = [2.0 / (v + shift(v, 1, 1)) for v in visc]
    inner = [2.0 / (a + b) for a, b in zip(visc[:-1], visc[1:])]
    if packed:
        bottom = jnp.where(iota(shape, 1) < 64, 0.0, 2.0 / (visc[0] + shift(visc[-1], 64, 1)))
        top = shift(bottom, 64, 1)
    else:
        bottom = top = jnp.zeros(shape, F32)
    height = [bottom] + inner + [top]
    diag = [diagonal_of(cast[z], span[z], height[z], height[z + 1]) for z in range(depth)]
    relax = [weight / d for d in diag]
    return Level(cast, span, height, diag, relax, source, depth, packed)


def keep(level, x, refs):
    for ref, values in zip(refs, (x, level.source, level.cast, level.span, level.height, level.diag, level.relax)):
        for z, value in enumerate(values):
            ref[z] = value[CUT]


def coarse_parts(visc, remains, scratch):
    parts = []
    count = len(visc) // 2
    for a, values in enumerate(([1.0 / v for v in visc], remains)):
        for k in range(count):
            scratch[a * count + k] = values[2 * k] + values[2 * k + 1]
            ref = scratch.at[a * count + k]
            parts.append(ref[pl.ds(0, HALF, stride=2), :] + ref[pl.ds(1, HALF, stride=2), :])
    return jnp.concatenate(parts, axis=0)


def ends(value, first, last, edge):
    rows = value.shape[0]
    low = jnp.where(first, jnp.broadcast_to(value[edge : edge + 1], (edge, BS)), value[:edge])
    high = jnp.where(last, jnp.broadcast_to(value[rows - edge - 1 : rows - edge], (edge, BS)), value[rows - edge :])
    return jnp.concatenate([low, value[edge : rows - edge], high], axis=0)


def beyond(rows, edge):
    row = iota((rows, BS), 0)
    index = lax.axis_index("cast")
    first, last = index == 0, index == lax.axis_size("cast") - 1
    return first, last, (first & (row < edge)) | (last & (row >= rows - edge))


def height_faces(coeff):
    flat = jnp.zeros_like(coeff[0])
    inner = [harmonic(a, b) for a, b in zip(coeff[:-1], coeff[1:])]
    return [flat] + inner + [flat]


def whole_level(coeff, source):
    shape = coeff[0].shape
    row = iota(shape, 0)
    height = height_faces(coeff)
    cast, span, diag, relax = [], [], [], []
    for z, c in enumerate(coeff):
        lower = jnp.where(row == 0, 0.0, harmonic(shift(c, 1, 0), c))
        ends = jnp.where((row == 0) | (row == shape[0] - 1), c, 0.0)
        side = harmonic(shift(c, 1, 1), c)
        total = diagonal_of(lower, side, height[z], height[z + 1]) + ends
        cast.append(lower)
        span.append(side)
        diag.append(total)
        relax.append(WEIGHT / total)
    return Level(cast, span, height, diag, relax, source, len(coeff))


def pair_rows(value, scratch):
    rows = value.shape[0]
    scratch[...] = value
    return scratch[pl.ds(0, rows // 2, stride=2), :] + scratch[pl.ds(1, rows // 2, stride=2), :]


def by_side(axis, near_pair, far_pair):
    even = lax.rem(lax.axis_index(axis), 2) == 0
    return jnp.where(even, far_pair, near_pair), jnp.where(even, near_pair, far_pair)


def extended(own, near_pair, far_pair, a, z):
    before, after = by_side("cast", near_pair[a, z], far_pair[a, z])
    return jnp.concatenate([before, own[a, z], after], axis=0)


def stage_kernel(table_in, phase_in, source_in, out, table, phase, sems):
    copies = [
        pltpu.make_async_copy(table_in, table, sems.at[0]),
        pltpu.make_async_copy(phase_in, phase, sems.at[1]),
        pltpu.make_async_copy(source_in, out.at[1], sems.at[2]),
    ]
    for copy in copies:
        copy.start()
    copies[0].wait()
    copies[1].wait()
    for z in range(HZ):
        p = phase[z]
        out[0, z] = jnp.where(p == 0, table[0], jnp.where(p == 1, table[1], table[2]))
    copies[2].wait()


def ones(where):
    return jnp.where(where, 1.0, 0.0).astype(BF16)


def prepare_kernel(own, near_own, far_own, own_merge, edge_merge, move, narrow, widen, grow, double, expand):
    lane = iota((BC, BS), 1)
    for a in range(2):
        for group in range(2):
            head = tail = None
            for start, z in places(group):
                h, t = shift(own[a, z], start, 1), shift(own[a, z], start + HALO, 1)
                inside = (lane >= start) & (lane < start + HALO)
                head = h if head is None else jnp.where(inside, h, head)
                tail = t if tail is None else jnp.where(inside, t, tail)
            far_own[a, group], near_own[a, group] = by_side("span", tail, head)
    i, j = iota((BS, BS), 0), iota((BS, BS), 1)
    own_merge[...] = ones((i // 2 == j) & (i >= 8) & (i < 120))
    narrow[...] = ones(((i < 64) & (i // 2 == j)) | ((i >= 96) & (i // 2 + 64 == j)))
    widen[...] = ones(((j < 64) & (j // 2 == i)) | ((j >= 96) & (j // 2 + 64 == i)))
    grow[...] = ones(((j < 96) & (j // 2 == i)) | ((j >= 96) & (j // 2 + 64 == i)))
    double[...] = ones(j // 2 == i)
    i, j = iota((BS, 2 * BS), 0), iota((BS, 2 * BS), 1)
    m = i % 64
    target = jnp.where(m < 24, (m // 2 + 120) % BS, m // 2 + 40)
    edge_merge[...] = ones(((m < 24) | (m >= 40)) & (target == j % BS) & (i // 64 == j // BS))
    i, j = iota((4 * BS, BS), 0), iota((4 * BS, BS), 1)
    move[...] = ones((i % BS < 64) & (i % BS // 2 + 32 * (i // BS) == j))
    i, j = iota((2 * BS, BS), 0), iota((2 * BS, BS), 1)
    m = j % 64
    origin = jnp.where(m < 32, (m // 2 + 120) % BS, m // 2 + 40)
    expand[...] = ones((origin == i % BS) & (i // BS == j // 64))


def places(group):
    return [(16 * sub + 64 * half, group * 4 + sub + 8 * half) for sub in range(4) for half in range(2)]


def margin_kernel(near_own, far_own, near_cast, far_cast, near_span, far_span):
    lane = iota((16, BS), 1)
    seg = lane % HALO
    for a in range(2):
        for group in range(2):
            head = tail = None
            for start, z in places(group):
                before, after = by_side("cast", near_cast[a, z], far_cast[a, z])
                inner = jnp.concatenate([before[8:], after[:8]], axis=0)
                far = jnp.concatenate([before[:8], after[8:]], axis=0)
                h = jnp.where(seg >= 12, shift(far, start + 12, 1), shift(inner, start, 1))
                t = jnp.where(seg < 4, shift(far, start + HALO - 12, 1), shift(inner, start + HALO, 1))
                inside = (lane >= start) & (lane < start + HALO)
                head = h if head is None else jnp.where(inside, h, head)
                tail = t if tail is None else jnp.where(inside, t, tail)
            sides = by_side("span", tail, head)
            for out, packed, value in ((far_span, far_own, sides[0]), (near_span, near_own, sides[1])):
                out[a, group, :8] = value[:8]
                out[a, group, 8:24] = packed[a, group]
                out[a, group, 24:] = value[8:]


def spread_rows(sent, step, more):
    moved = shift(sent, step, 1)
    return jnp.concatenate([shift(sent[:8], step + more, 1), moved, shift(sent[-8:], step + more, 1)], axis=0)


def own_kernel(own, near_cast, far_cast, own_merge, x, b, cast, span, height, diag, relax, merged, inner, scratch):
    first, last, outside = beyond(ROWS, HALO)
    visc, source = [], []
    for z in range(HZ):
        v, s = (extended(own, near_cast, far_cast, a, z) for a in range(2))
        visc.append(ends(v, first, last, HALO))
        source.append(s)
    lane = iota((ROWS, BS), 1)
    for a, field in enumerate((visc, source)):
        for k in range(PACK):
            low, high = field[k], field[k + PACK]
            inner[a, k] = jnp.where(
                lane < 32,
                shift(low, 16, 1),
                jnp.where(lane < 64, shift(low, 48, 1), jnp.where(lane < 96, shift(high, 80, 1), shift(high, 112, 1))),
            )
    level = fine_level(visc, source, outside, False)
    values = level.sweep(level.start())
    keep(level, values, (x, b, cast, span, height, diag, relax))
    parts = coarse_parts(visc, level.residual(values), scratch)
    total = product(parts, own_merge[...])
    for k in range(HZ):
        merged[k] = total[HALF * k : HALF * (k + 1)]


def edge_levels(near_span, far_span, inner, merged, edge_merge, scratch):
    first, last, outside = beyond(ROWS, HALO)
    lane = iota((ROWS, BS), 1) % 64
    fields = []
    for a in range(2):
        slabs = []
        for k in range(PACK):
            group, sub = divmod(k, 4)
            left, right = by_side("span", near_span[a, group], far_span[a, group])
            l, r = spread_rows(left, -16 * sub, 12), spread_rows(right, 48 - 16 * sub, -12)
            value = jnp.where(lane < 16, l, jnp.where(lane >= 48, r, inner[a, k]))
            slabs.append(ends(value, first, last, HALO) if a == 0 else value)
        fields.append(slabs)
    visc, source = fields
    level = fine_level(visc, source, outside, True)
    values = level.sweep(level.start())
    fine = level, values
    parts = coarse_parts(visc, level.residual(values), scratch)
    total = product(parts, edge_merge[...])

    edge = HALO // 2
    first, last, outside = beyond(HALF, edge)
    weight = jnp.where(outside, 0.0, WEIGHT)
    coarse = []
    for k in range(HZ):
        a, z = divmod(k, 8)
        side, pos = divmod(z, 4)
        row = HALF * (4 * a + pos)
        coarse.append(merged[k] + total[row : row + HALF, BS * side : BS * (side + 1)])
    lane = iota((HALF, BS), 1)
    known = (lane < 72) | (lane >= 120)
    coeff = [jnp.where(known, 0.125 * ends(c, first, last, edge), 1.0) for c in coarse[:8]]
    source = [0.5 * c for c in coarse[8:]]
    height = height_faces(coeff)
    cast_faces = [harmonic(shift(c, 1, 0), c) for c in coeff]
    span_faces = [harmonic(shift(c, 1, 1), c) for c in coeff]
    diagonal = [diagonal_of(cast_faces[z], span_faces[z], height[z], height[z + 1]) for z in range(8)]
    level = Level(cast_faces, span_faces, height, diagonal, [weight / d for d in diagonal], source, 8)
    return fine, (level, level.sweep(level.start()), coeff)


def state_kernel(
    near_span, far_span, inner, merged, edge_merge, x, b, cast, span, height, diag, relax,
    x1, b1, cast1, span1, height1, relax1, scratch,
):
    fine, (level, values, _) = edge_levels(near_span, far_span, inner, merged, edge_merge, scratch)
    keep(*fine, (x, b, cast, span, height, diag, relax))
    kept = (x1, values), (b1, level.source), (cast1, level.cast), (span1, level.span), (height1, level.height), (relax1, level.relax)
    for ref, items in kept:
        for z, item in enumerate(items):
            ref[z] = item


def edge_kernel(near_span, far_span, inner, merged, edge_merge, move, slots, scratch, rows8):
    _, (level, values, coeff) = edge_levels(near_span, far_span, inner, merged, edge_merge, scratch)
    remains = level.residual(values)
    edge = HALO // 2

    fields = []
    for k in range(4):
        rows = slice(edge, edge + 8)
        c = coeff[2 * k][rows] + coeff[2 * k + 1][rows]
        r = remains[2 * k][rows] + remains[2 * k + 1][rows]
        rows8[k] = jnp.concatenate([0.125 * c, 0.5 * r], axis=0)
        fields.append(rows8[k, pl.ds(0, 8, stride=2), :] + rows8[k, pl.ds(1, 8, stride=2), :])
    total = product(jnp.concatenate(fields, axis=1), move[...])
    for d in range(slots.shape[0]):
        slots[d] = total


def ascent_kernel(
    own, far_column, near_column, narrow, widen, grow, double, expand,
    xo, bo, casto, spano, heighto, diago, relaxo,
    xe, be, caste, spane, heighte, diage, relaxe,
    x1, b1, cast1, span1, height1, relax1,
    solution_out, residual_out, tiles, pairs, wide2, padded2, wide1, wide_own, wide_edge, results, sems,
):
    count = own.shape[0]
    rows = 4 * count
    lane = iota((rows, 128), 1)
    index = lax.axis_index("cast")

    fields = []
    for part in range(2):
        for d in range(count):
            rows_d = slice(4 * part, 4 * part + 4)
            left, right = by_side("span", near_column[d, rows_d], far_column[d, rows_d])
            for s, block in enumerate((own[d, rows_d], right, left)):
                tiles[s, 4 * d : 4 * d + 4] = block
        slabs = []
        for z in range(4):
            o = shift(tiles[0], -32 * z, 1)
            r = shift(tiles[1], 32 - 32 * z, 1)
            l = shift(tiles[2], 96 - 32 * z, 1)
            fill = 1.0 if part == 0 else 0.0
            slabs.append(jnp.where(lane < 32, o, jnp.where(lane < 64, r, jnp.where(lane >= 96, l, fill))))
        fields.append(slabs)
    coeff2, source2 = fields
    level2 = whole_level(coeff2, source2)
    x2 = level2.sweep(level2.start())
    remains = level2.residual(x2)

    gathered = []
    for field in (coeff2, remains):
        for k in range(2):
            gathered.append(pair_rows(field[2 * k] + field[2 * k + 1], pairs))
    merged = product(jnp.concatenate(gathered, axis=0), narrow[...])
    half = rows // 2
    lane3 = iota((half, 128), 1)
    known = (lane3 < 32) | (lane3 >= 112)
    coeff3 = [jnp.where(known, 0.125 * merged[half * k : half * (k + 1)], 1.0) for k in range(2)]
    source3 = [0.5 * merged[half * (2 + k) : half * (3 + k)] for k in range(2)]
    level3 = whole_level(coeff3, source3)
    x3 = level3.solve(SWEEPS_COARSE - 1)

    spread = product(jnp.concatenate(x3, axis=0), widen[...])
    for k in range(2):
        wide2[k, pl.ds(0, half, stride=2), :] = spread[half * k : half * (k + 1)]
        wide2[k, pl.ds(1, half, stride=2), :] = spread[half * k : half * (k + 1)]
    x2 = [x2[z] + wide2[z // 2] for z in range(4)]
    x2 = level2.sweep(level2.sweep(x2))

    for z in range(4):
        padded2[z, 0:8] = jnp.zeros((8, 128), F32)
        padded2[z, 8 : 8 + rows] = x2[z]
        padded2[z, 8 + rows : 16 + rows] = jnp.zeros((8, 128), F32)
    local = [padded2[z, pl.ds(4 * index + 4, 16), :] for z in range(4)]
    spread = product(jnp.concatenate(local, axis=0), grow[...])
    for z in range(4):
        wide1[z, pl.ds(0, 16, stride=2), :] = spread[16 * z : 16 * z + 16]
        wide1[z, pl.ds(1, 16, stride=2), :] = spread[16 * z : 16 * z + 16]
    level1 = Level(cast1, span1, height1, None, relax1, b1, 8)
    x = [x1[z] + wide1[z // 2, 0:HALF] for z in range(8)]
    x = level1.sweep(level1.sweep(x))

    spread = product(jnp.concatenate(x, axis=0), double[...])
    for z in range(8):
        for s in range(2):
            wide_own[z, pl.ds(s, HALF, stride=2), :] = spread[HALF * z : HALF * (z + 1)]
    sides = [jnp.concatenate([x[k], x[k + 4]], axis=1) for k in range(4)]
    spread = product(jnp.concatenate(sides, axis=0), expand[...])
    for k in range(4):
        for s in range(2):
            wide_edge[k, pl.ds(s, HALF, stride=2), :] = spread[HALF * k : HALF * (k + 1)]
    level_own = Level(casto, spano, heighto, diago, relaxo, bo, HZ)
    level_edge = Level(caste, spane, heighte, diage, relaxe, be, PACK, True)
    own_x = [xo[z] + wide_own[z // 2, CUT] for z in range(HZ)]
    edge_x = [xe[k] + wide_edge[k // 2, CUT] for k in range(PACK)]
    edge_x = level_edge.sweep(level_edge.sweep(edge_x))
    own_x = level_own.sweep(level_own.sweep(own_x))
    lane = iota((BC, BS), 1)
    rows = slice(4, 4 + BC)

    copies = []

    def give(number, out, z, mid, side):
        half, k = divmod(z, PACK)
        low = shift(side[rows], -16 - 64 * half, 1)
        high = shift(side[rows], 80 - 64 * half, 1)
        results[number, z] = jnp.where(lane < 8, low, jnp.where(lane >= 120, high, mid[rows]))
        if z % 4 == 3:
            quarter = pl.ds(z - 3, 4)
            copy = pltpu.make_async_copy(results.at[number, quarter], out.at[quarter], sems.at[number, z // 4])
            copy.start()
            copies.append(copy)

    for z in range(HZ):
        give(0, solution_out, z, own_x[z], edge_x[z % PACK])
    edge_r = level_edge.residual(edge_x)
    own_r = level_own.residual(own_x)
    for z in range(HZ):
        give(1, residual_out, z, own_r[z], edge_r[z % PACK])
    for copy in copies:
        copy.wait()


VMEM = pl.BlockSpec(memory_space=pltpu.VMEM)
HBM = pl.BlockSpec(memory_space=pltpu.HBM)
PARAMS = pltpu.CompilerParams(vmem_limit_bytes=16 * 1024 * 1024)
INTERPRET = False


def call(kernel, in_specs, outs, scratch=(), out_spec=VMEM):
    return pl.pallas_call(
        kernel,
        in_specs=in_specs,
        out_specs=[out_spec] * len(outs),
        out_shape=[jax.ShapeDtypeStruct(s, F32) if isinstance(s, tuple) else s for s in outs],
        scratch_shapes=[pltpu.VMEM(s, F32) if isinstance(s, tuple) else s for s in scratch],
        compiler_params=PARAMS,
        interpret=INTERPRET,
    )


def swap(value, axis, far):
    size = lax.axis_size(axis)
    partner = [(((i - 1) ^ 1) + 1) % size if far else i ^ 1 for i in range(size)]
    return lax.ppermute(value, axis, list(enumerate(partner)))


def shards(phase, viscosity_table, pressure_source):
    count = lax.axis_size("cast")
    packed = (2, 2, SENT, BS)
    own_state = [(HZ, KEPT, BS)] * 4 + [(HZ + 1, KEPT, BS)] + [(HZ, KEPT, BS)] * 2
    edge_state = [(PACK, KEPT, BS)] * 4 + [(PACK + 1, KEPT, BS)] + [(PACK, KEPT, BS)] * 2
    level1_state = [(8, HALF, BS)] * 4 + [(9, HALF, BS), (8, HALF, BS)]

    arguments = (pltpu.with_memory_space_constraint(a, pltpu.HBM) for a in (viscosity_table, phase, pressure_source))
    stage_scratch = [pltpu.SMEM((3,), F32), pltpu.VMEM((HZ, BC, BS), jnp.int32), pltpu.SemaphoreType.DMA((3,))]
    (own,) = call(stage_kernel, [HBM] * 3, [(2, HZ, BC, BS)], stage_scratch)(*arguments)
    far_cast = swap(own, "cast", True)
    near_cast = swap(own, "cast", False)
    square = (BS, BS)
    tables = [square, (BS, 2 * BS), (4 * BS, BS), square, square, square, square, (2 * BS, BS)]
    tables = [jax.ShapeDtypeStruct(t, BF16) for t in tables]
    near_own, far_own, own_merge, edge_merge, move, *spreads = call(
        prepare_kernel, [VMEM], [(2, 2, BC, BS)] * 2 + tables
    )(own)
    near_span, far_span = call(margin_kernel, [VMEM] * 4, [packed, packed])(near_own, far_own, near_cast, far_cast)
    near_span = swap(near_span, "span", False)
    far_span = swap(far_span, "span", True)
    *kept_own, merged, inner = call(
        own_kernel,
        [VMEM] * 4,
        own_state + [(HZ, HALF, BS), (2, PACK, ROWS, BS)],
        [(HZ, ROWS, BS)],
    )(own, near_cast, far_cast, own_merge)
    (slots,) = call(
        edge_kernel, [VMEM] * 6, [(count, 8, BS)], [(8, ROWS, BS), (4, 16, BS)]
    )(near_span, far_span, inner, merged, edge_merge, move)
    kept_edge = call(state_kernel, [VMEM] * 5, edge_state + level1_state, [(8, ROWS, BS)])(
        near_span, far_span, inner, merged, edge_merge
    )

    column = lax.all_to_all(slots, "cast", 0, 0)
    near_column = swap(column, "span", False)
    far_column = swap(column, "span", True)
    rows = 4 * count
    scratch = [
        (3, rows, BS),
        (rows, BS),
        (2, rows, BS),
        (4, rows + 16, BS),
        (4, 32, BS),
        (8, ROWS, BS),
        (4, ROWS, BS),
        (2, HZ, BC, BS),
        pltpu.SemaphoreType.DMA((2, 4)),
    ]
    state = spreads + kept_own + list(kept_edge)
    return tuple(
        call(ascent_kernel, [VMEM] * (3 + len(state)), [(HZ, BC, BS)] * 2, scratch, HBM)(
            column, far_column, near_column, *state
        )
    )


def solution(mesh):
    blocks = P(None, "cast", "span")
    return jax.shard_map(
        shards,
        mesh=mesh,
        in_specs=(blocks, P(), blocks),
        out_specs=(blocks, blocks),
        check_vma=False,
    )
```

```python
import jax
import jax.numpy as jnp
from jax import lax
from jax.experimental import pallas as pl
from jax.experimental.pallas import tpu as pltpu
from jax.sharding import PartitionSpec as P

HZ, BC, BS = 16, 16, 128
HALO = 16
ROWS = BC + 2 * HALO
HALF = ROWS // 2
KEPT = BC + 8
KEPT1 = HALF - 8
SENT = BC + 16
PACK = HZ // 2
SWEEPS_COARSE = 8
WEIGHT = 0.8
F32 = jnp.float32
BF16 = jnp.bfloat16


def shift(x, step, axis):
    return pltpu.roll(x, step % x.shape[axis], axis)


def iota(shape, axis):
    return lax.broadcasted_iota(jnp.int32, shape, axis)


def product(a, b):
    high = a.astype(BF16)
    low = (a - high.astype(F32)).astype(BF16)
    return jnp.dot(high, b, preferred_element_type=F32) + jnp.dot(low, b, preferred_element_type=F32)


def harmonic(a, b):
    return 2.0 * a * b / (a + b)


def near(x, below, above, cast, span, low, high):
    return (
        cast * shift(x, 1, 0)
        + shift(cast * x, -1, 0)
        + span * shift(x, 1, 1)
        + shift(span * x, -1, 1)
        + low * below
        + high * above
    )


def diagonal_of(cast, span, low, high):
    return cast + shift(cast, -1, 0) + span + shift(span, -1, 1) + low + high


class Level:
    def __init__(self, cast, span, height, diag, relax, source, depth, packed=False):
        self.cast, self.span, self.height = cast, span, height
        self.diag, self.relax, self.source = diag, relax, source
        self.depth, self.packed = depth, packed

    def near(self, x, z):
        last = self.depth - 1
        below, above = x[max(z - 1, 0)], x[min(z + 1, last)]
        if self.packed and z == 0:
            below = shift(x[last], 64, 1)
        if self.packed and z == last:
            above = shift(x[0], 64, 1)
        return near(x[z], below, above, self.cast[z], self.span[z], self.height[z], self.height[z + 1])

    def start(self):
        return [self.relax[z] * self.source[z] for z in range(self.depth)]

    def sweep(self, x):
        return [
            (1.0 - WEIGHT) * x[z] + self.relax[z] * (self.near(x, z) + self.source[z])
            for z in range(self.depth)
        ]

    def solve(self, sweeps):
        part = [
            (
                relax * self.cast[z],
                relax * shift(self.cast[z], -1, 0),
                relax * self.span[z],
                relax * shift(self.span[z], -1, 1),
                relax * self.height[1],
            )
            for z, relax in enumerate(self.relax)
        ]
        first = x = self.start()
        for _ in range(sweeps):
            x = [
                ((1.0 - WEIGHT) * x[z] + first[z] + part[z][4] * x[1 - z])
                + (part[z][0] * shift(x[z], 1, 0) + part[z][1] * shift(x[z], -1, 0))
                + (part[z][2] * shift(x[z], 1, 1) + part[z][3] * shift(x[z], -1, 1))
                for z in range(2)
            ]
        return x

    def residual(self, x):
        return [self.source[z] - self.diag[z] * x[z] + self.near(x, z) for z in range(self.depth)]


def fine_level(visc, source, outside, packed):
    depth = len(visc)
    shape = visc[0].shape
    weight = jnp.where(outside, 0.0, WEIGHT)
    cast = [2.0 / (v + shift(v, 1, 0)) for v in visc]
    span = [2.0 / (v + shift(v, 1, 1)) for v in visc]
    inner = [2.0 / (a + b) for a, b in zip(visc[:-1], visc[1:])]
    if packed:
        bottom = jnp.where(iota(shape, 1) < 64, 0.0, 2.0 / (visc[0] + shift(visc[-1], 64, 1)))
        top = shift(bottom, 64, 1)
    else:
        bottom = top = jnp.zeros(shape, F32)
    height = [bottom] + inner + [top]
    diag = [diagonal_of(cast[z], span[z], height[z], height[z + 1]) for z in range(depth)]
    relax = [weight / d for d in diag]
    return Level(cast, span, height, diag, relax, source, depth, packed)


def kept_rows(value):
    edge = jnp.where(iota((8, BS), 0) < 4, value[HALO + BC : HALO + BC + 8], value[HALO - 8 : HALO])
    return jnp.concatenate([value[HALO : HALO + BC], edge], axis=0)


def kept_rows1(value):
    return jnp.concatenate([value[8:16], jnp.where(iota((8, BS), 0) < 4, value[16:], value[:8])], axis=0)


def keep(level, x, refs):
    for ref, values in zip(refs, (x, level.source, level.cast, level.span, level.height, level.diag, level.relax)):
        for z, value in enumerate(values):
            ref[z] = kept_rows(value)


def coarse_parts(visc, remains, scratch):
    parts = []
    count = len(visc) // 2
    half = visc[0].shape[0] // 2
    for a, values in enumerate(([1.0 / v for v in visc], remains)):
        for k in range(count):
            scratch[a * count + k] = values[2 * k] + values[2 * k + 1]
            ref = scratch.at[a * count + k]
            parts.append(ref[pl.ds(0, half, stride=2), :] + ref[pl.ds(1, half, stride=2), :])
    return jnp.concatenate(parts, axis=0)


def ends(value, first, last, edge):
    rows = value.shape[0]
    row = iota((rows, BS), 0)
    value = jnp.where(first & (row < edge), jnp.broadcast_to(value[edge : edge + 1], (rows, BS)), value)
    stop = rows - edge
    return jnp.where(last & (row >= stop), jnp.broadcast_to(value[stop - 1 : stop], (rows, BS)), value)


def beyond(rows, edge):
    row = iota((rows, BS), 0)
    index = lax.axis_index("cast")
    first, last = index == 0, index == lax.axis_size("cast") - 1
    return first, last, (first & (row < edge)) | (last & (row >= rows - edge))


def height_faces(coeff):
    flat = jnp.zeros_like(coeff[0])
    inner = [harmonic(a, b) for a, b in zip(coeff[:-1], coeff[1:])]
    return [flat] + inner + [flat]


def whole_level(coeff, source):
    shape = coeff[0].shape
    row = iota(shape, 0)
    height = height_faces(coeff)
    cast, span, diag, relax = [], [], [], []
    for z, c in enumerate(coeff):
        lower = jnp.where(row == 0, 0.0, harmonic(shift(c, 1, 0), c))
        ends = jnp.where((row == 0) | (row == shape[0] - 1), c, 0.0)
        side = harmonic(shift(c, 1, 1), c)
        total = diagonal_of(lower, side, height[z], height[z + 1]) + ends
        cast.append(lower)
        span.append(side)
        diag.append(total)
        relax.append(WEIGHT / total)
    return Level(cast, span, height, diag, relax, source, len(coeff))


def pair_rows(value, scratch):
    rows = value.shape[0]
    scratch[...] = value
    return scratch[pl.ds(0, rows // 2, stride=2), :] + scratch[pl.ds(1, rows // 2, stride=2), :]


def by_side(axis, near_pair, far_pair):
    even = lax.rem(lax.axis_index(axis), 2) == 0
    return jnp.where(even, far_pair, near_pair), jnp.where(even, near_pair, far_pair)


def extended(own, near_pair, far_pair, a, z):
    before, after = by_side("cast", near_pair[a, z], far_pair[a, z])
    return jnp.concatenate([before, own[a, z], after], axis=0)


def stage_kernel(table_in, phase_in, source_in, out, table, phase, sems):
    copies = [
        pltpu.make_async_copy(table_in, table, sems.at[0]),
        pltpu.make_async_copy(phase_in, phase, sems.at[1]),
        pltpu.make_async_copy(source_in, out.at[1], sems.at[2]),
    ]
    for copy in copies:
        copy.start()
    copies[0].wait()
    copies[1].wait()
    for z in range(HZ):
        p = phase[z]
        out[0, z] = jnp.where(p == 0, table[0], jnp.where(p == 1, table[1], table[2]))
    copies[2].wait()


def ones(where):
    return jnp.where(where, 1.0, 0.0).astype(BF16)


def prepare_kernel(own, near_own, far_own, own_merge, edge_merge, move, narrow, widen, grow, double, expand):
    lane = iota((BC, BS), 1)
    for a in range(2):
        for group in range(2):
            head = tail = None
            for start, z in places(group):
                h, t = shift(own[a, z], start, 1), shift(own[a, z], start + HALO, 1)
                inside = (lane >= start) & (lane < start + HALO)
                head = h if head is None else jnp.where(inside, h, head)
                tail = t if tail is None else jnp.where(inside, t, tail)
            far_own[a, group], near_own[a, group] = by_side("span", tail, head)
    i, j = iota((BS, BS), 0), iota((BS, BS), 1)
    own_merge[...] = ones((i // 2 == j) & (i >= 8) & (i < 120))
    narrow[...] = ones(((i < 64) & (i // 2 == j)) | ((i >= 96) & (i // 2 + 64 == j)))
    widen[...] = ones(((j < 64) & (j // 2 == i)) | ((j >= 96) & (j // 2 + 64 == i)))
    grow[...] = ones(((j < 96) & (j // 2 == i)) | ((j >= 96) & (j // 2 + 64 == i)))
    double[...] = ones(j // 2 == i)
    i, j = iota((BS, 2 * BS), 0), iota((BS, 2 * BS), 1)
    m = i % 64
    target = jnp.where(m < 24, (m // 2 + 120) % BS, m // 2 + 40)
    edge_merge[...] = ones(((m < 24) | (m >= 40)) & (target == j % BS) & (i // 64 == j // BS))
    i, j = iota((4 * BS, BS), 0), iota((4 * BS, BS), 1)
    move[...] = ones((i % BS < 64) & (i % BS // 2 + 32 * (i // BS) == j))
    i, j = iota((2 * BS, BS), 0), iota((2 * BS, BS), 1)
    m = j % 64
    origin = jnp.where(m < 32, (m // 2 + 120) % BS, m // 2 + 40)
    expand[...] = ones((origin == i % BS) & (i // BS == j // 64))


def places(group):
    return [(16 * sub + 64 * half, group * 4 + sub + 8 * half) for sub in range(4) for half in range(2)]


def margin_kernel(near_own, far_own, near_cast, far_cast, near_span, far_span):
    lane = iota((16, BS), 1)
    seg = lane % HALO
    for a in range(2):
        for group in range(2):
            head = tail = None
            for start, z in places(group):
                before, after = by_side("cast", near_cast[a, z], far_cast[a, z])
                inner = jnp.concatenate([before[8:], after[:8]], axis=0)
                far = jnp.concatenate([before[:8], after[8:]], axis=0)
                h = jnp.where(seg >= 12, shift(far, start + 12, 1), shift(inner, start, 1))
                t = jnp.where(seg < 4, shift(far, start + HALO - 12, 1), shift(inner, start + HALO, 1))
                inside = (lane >= start) & (lane < start + HALO)
                head = h if head is None else jnp.where(inside, h, head)
                tail = t if tail is None else jnp.where(inside, t, tail)
            sides = by_side("span", tail, head)
            for out, packed, value in ((far_span, far_own, sides[0]), (near_span, near_own, sides[1])):
                out[a, group, :8] = value[:8]
                out[a, group, 8:24] = packed[a, group]
                out[a, group, 24:] = value[8:]


def spread_rows(sent, step, more):
    moved = shift(sent, step, 1)
    return jnp.concatenate([shift(sent[:8], step + more, 1), moved, shift(sent[-8:], step + more, 1)], axis=0)


def own_kernel(own, near_cast, far_cast, own_merge, x, b, cast, span, height, diag, relax, merged, merged_mid, inner, scratch):
    first, last, outside = beyond(ROWS, HALO)
    visc, source = [], []
    for z in range(HZ):
        v, s = (extended(own, near_cast, far_cast, a, z) for a in range(2))
        visc.append(ends(v, first, last, HALO))
        source.append(s)
    lane = iota((ROWS, BS), 1)
    for a, field in enumerate((visc, source)):
        for k in range(PACK):
            low, high = field[k], field[k + PACK]
            inner[a, k] = jnp.where(
                lane < 32,
                shift(low, 16, 1),
                jnp.where(lane < 64, shift(low, 48, 1), jnp.where(lane < 96, shift(high, 80, 1), shift(high, 112, 1))),
            )
    level = fine_level(visc, source, outside, False)
    values = level.sweep(level.start())
    keep(level, values, (x, b, cast, span, height, diag, relax))
    parts = coarse_parts(visc, level.residual(values), scratch)
    total = product(parts, own_merge[...])
    for k in range(HZ):
        merged[k] = total[HALF * k : HALF * (k + 1)]
        merged_mid[k] = total[HALF * k + 4 : HALF * (k + 1) - 4]


def edge_levels(near_span, far_span, inner, merged, edge_merge, scratch, halo):
    rows = BC + 2 * halo
    first, last, outside = beyond(rows, halo)
    lane = iota((rows, BS), 1) % 64
    fields = []
    for a in range(2):
        slabs = []
        for k in range(PACK):
            group, sub = divmod(k, 4)
            left, right = by_side("span", near_span[a, group], far_span[a, group])
            if halo == HALO:
                l, r = spread_rows(left, -16 * sub, 12), spread_rows(right, 48 - 16 * sub, -12)
            else:
                l, r = shift(left, -16 * sub, 1), shift(right, 48 - 16 * sub, 1)
            own = inner[a, k, HALO - halo : HALO + BC + halo]
            value = jnp.where(lane < 16, l, jnp.where(lane >= 48, r, own))
            slabs.append(ends(value, first, last, halo) if a == 0 else value)
        fields.append(slabs)
    visc, source = fields
    level = fine_level(visc, source, outside, True)
    values = level.sweep(level.start())
    fine = level, values
    parts = coarse_parts(visc, level.residual(values), scratch)
    total = product(parts, edge_merge[...])

    edge, half = halo // 2, rows // 2
    first, last, outside = beyond(half, edge)
    weight = jnp.where(outside, 0.0, WEIGHT)
    coarse = []
    for k in range(HZ):
        a, z = divmod(k, 8)
        side, pos = divmod(z, 4)
        row = half * (4 * a + pos)
        coarse.append(merged[k] + total[row : row + half, BS * side : BS * (side + 1)])
    lane = iota((half, BS), 1)
    known = (lane < 72) | (lane >= 120)
    coeff = [jnp.where(known, 0.125 * ends(c, first, last, edge), 1.0) for c in coarse[:8]]
    source = [0.5 * c for c in coarse[8:]]
    height = height_faces(coeff)
    cast_faces = [harmonic(shift(c, 1, 0), c) for c in coeff]
    span_faces = [harmonic(shift(c, 1, 1), c) for c in coeff]
    diagonal = [diagonal_of(cast_faces[z], span_faces[z], height[z], height[z + 1]) for z in range(8)]
    level = Level(cast_faces, span_faces, height, diagonal, [weight / d for d in diagonal], source, 8)
    return fine, (level, level.sweep(level.start()), coeff)


def state_kernel(
    near_span, far_span, inner, merged, edge_merge, x, b, cast, span, height, diag, relax,
    x1, b1, cast1, span1, height1, relax1, scratch,
):
    fine, (level, values, _) = edge_levels(near_span, far_span, inner, merged, edge_merge, scratch, HALO)
    keep(*fine, (x, b, cast, span, height, diag, relax))
    kept = (x1, values), (b1, level.source), (cast1, level.cast), (span1, level.span), (height1, level.height), (relax1, level.relax)
    for ref, items in kept:
        for z, item in enumerate(items):
            ref[z] = kept_rows1(item)


def edge_kernel(near_span, far_span, inner, merged, edge_merge, move, slots, scratch, rows8):
    _, (level, values, coeff) = edge_levels(near_span, far_span, inner, merged, edge_merge, scratch, 8)
    remains = level.residual(values)
    edge = 4

    fields = []
    for k in range(4):
        rows = slice(edge, edge + 8)
        c = coeff[2 * k][rows] + coeff[2 * k + 1][rows]
        r = remains[2 * k][rows] + remains[2 * k + 1][rows]
        rows8[k] = jnp.concatenate([0.125 * c, 0.5 * r], axis=0)
        fields.append(rows8[k, pl.ds(0, 8, stride=2), :] + rows8[k, pl.ds(1, 8, stride=2), :])
    total = product(jnp.concatenate(fields, axis=1), move[...])
    for d in range(slots.shape[0]):
        slots[d] = total


def ascent_kernel(
    own, far_column, near_column, narrow, widen, grow, double, expand,
    xo, bo, casto, spano, heighto, diago, relaxo,
    xe, be, caste, spane, heighte, diage, relaxe,
    x1, b1, cast1, span1, height1, relax1,
    solution_out, residual_out, tiles, pairs, wide2, padded2, wide1, wide_own, wide_edge, results, sems,
):
    count = own.shape[0]
    rows = 4 * count
    lane = iota((rows, 128), 1)
    index = lax.axis_index("cast")

    fields = []
    for part in range(2):
        for d in range(count):
            rows_d = slice(4 * part, 4 * part + 4)
            left, right = by_side("span", near_column[d, rows_d], far_column[d, rows_d])
            for s, block in enumerate((own[d, rows_d], right, left)):
                tiles[s, 4 * d : 4 * d + 4] = block
        slabs = []
        for z in range(4):
            o = shift(tiles[0], -32 * z, 1)
            r = shift(tiles[1], 32 - 32 * z, 1)
            l = shift(tiles[2], 96 - 32 * z, 1)
            fill = 1.0 if part == 0 else 0.0
            slabs.append(jnp.where(lane < 32, o, jnp.where(lane < 64, r, jnp.where(lane >= 96, l, fill))))
        fields.append(slabs)
    coeff2, source2 = fields
    level2 = whole_level(coeff2, source2)
    x2 = level2.sweep(level2.start())
    remains = level2.residual(x2)

    gathered = []
    for field in (coeff2, remains):
        for k in range(2):
            gathered.append(pair_rows(field[2 * k] + field[2 * k + 1], pairs))
    merged = product(jnp.concatenate(gathered, axis=0), narrow[...])
    half = rows // 2
    lane3 = iota((half, 128), 1)
    known = (lane3 < 32) | (lane3 >= 112)
    coeff3 = [jnp.where(known, 0.125 * merged[half * k : half * (k + 1)], 1.0) for k in range(2)]
    source3 = [0.5 * merged[half * (2 + k) : half * (3 + k)] for k in range(2)]
    level3 = whole_level(coeff3, source3)
    x3 = level3.solve(SWEEPS_COARSE - 1)

    spread = product(jnp.concatenate(x3, axis=0), widen[...])
    for k in range(2):
        wide2[k, pl.ds(0, half, stride=2), :] = spread[half * k : half * (k + 1)]
        wide2[k, pl.ds(1, half, stride=2), :] = spread[half * k : half * (k + 1)]
    x2 = [x2[z] + wide2[z // 2] for z in range(4)]
    x2 = level2.sweep(level2.sweep(x2))

    for z in range(4):
        padded2[z, 0:8] = jnp.zeros((8, 128), F32)
        padded2[z, 8 : 8 + rows] = x2[z]
        padded2[z, 8 + rows : 16 + rows] = jnp.zeros((8, 128), F32)
    local = [shift(padded2[z, pl.ds(4 * index + 6, 8), :], -2, 0) for z in range(4)]
    spread = product(jnp.concatenate(local, axis=0), grow[...])
    for z in range(4):
        for s in range(2):
            wide1[z, pl.ds(s, 8, stride=2), :] = spread[8 * z : 8 * z + 8]
    level1 = Level(cast1, span1, height1, None, relax1, b1, 8)
    x = [x1[z] + wide1[z // 2] for z in range(8)]
    x = level1.sweep(level1.sweep(x))

    spread = product(jnp.concatenate(x, axis=0), double[...])
    for z in range(8):
        for s in range(2):
            wide_own[z, pl.ds(s, KEPT1, stride=2), :] = spread[KEPT1 * z : KEPT1 * (z + 1)]
    sides = [jnp.concatenate([x[k], x[k + 4]], axis=1) for k in range(4)]
    spread = product(jnp.concatenate(sides, axis=0), expand[...])
    for k in range(4):
        for s in range(2):
            wide_edge[k, pl.ds(s, KEPT1, stride=2), :] = spread[KEPT1 * k : KEPT1 * (k + 1)]
    level_own = Level(casto, spano, heighto, diago, relaxo, bo, HZ)
    level_edge = Level(caste, spane, heighte, diage, relaxe, be, PACK, True)

    def refined(wide, k):
        edge = jnp.where(iota((8, BS), 0) < 4, wide[k, BC : BC + 8], wide[k, BC + 8 :])
        return jnp.concatenate([wide[k, :BC], edge], axis=0)

    own_wide = [refined(wide_own, k) for k in range(8)]
    edge_wide = [refined(wide_edge, k) for k in range(4)]
    own_x = [xo[z] + own_wide[z // 2] for z in range(HZ)]
    edge_x = [xe[k] + edge_wide[k // 2] for k in range(PACK)]
    edge_x = level_edge.sweep(level_edge.sweep(edge_x))
    own_x = level_own.sweep(level_own.sweep(own_x))
    lane = iota((BC, BS), 1)
    rows = slice(0, BC)

    copies = []

    def give(number, out, z, mid, side):
        half, k = divmod(z, PACK)
        low = shift(side[rows], -16 - 64 * half, 1)
        high = shift(side[rows], 80 - 64 * half, 1)
        results[number, z] = jnp.where(lane < 8, low, jnp.where(lane >= 120, high, mid[rows]))
        if z % 4 == 3:
            quarter = pl.ds(z - 3, 4)
            copy = pltpu.make_async_copy(results.at[number, quarter], out.at[quarter], sems.at[number, z // 4])
            copy.start()
            copies.append(copy)

    for z in range(HZ):
        give(0, solution_out, z, own_x[z], edge_x[z % PACK])
    edge_r = level_edge.residual(edge_x)
    own_r = level_own.residual(own_x)
    for z in range(HZ):
        give(1, residual_out, z, own_r[z], edge_r[z % PACK])
    for copy in copies:
        copy.wait()


VMEM = pl.BlockSpec(memory_space=pltpu.VMEM)
HBM = pl.BlockSpec(memory_space=pltpu.HBM)
PARAMS = pltpu.CompilerParams(vmem_limit_bytes=16 * 1024 * 1024)
INTERPRET = False


def call(kernel, in_specs, outs, scratch=(), out_spec=VMEM):
    return pl.pallas_call(
        kernel,
        in_specs=in_specs,
        out_specs=[out_spec] * len(outs),
        out_shape=[jax.ShapeDtypeStruct(s, F32) if isinstance(s, tuple) else s for s in outs],
        scratch_shapes=[pltpu.VMEM(s, F32) if isinstance(s, tuple) else s for s in scratch],
        compiler_params=PARAMS,
        interpret=INTERPRET,
    )


def swap(value, axis, far):
    size = lax.axis_size(axis)
    partner = [(((i - 1) ^ 1) + 1) % size if far else i ^ 1 for i in range(size)]
    return lax.ppermute(value, axis, list(enumerate(partner)))


def shards(phase, viscosity_table, pressure_source):
    count = lax.axis_size("cast")
    packed = (2, 2, SENT, BS)
    own_state = [(HZ, KEPT, BS)] * 4 + [(HZ + 1, KEPT, BS)] + [(HZ, KEPT, BS)] * 2
    edge_state = [(PACK, KEPT, BS)] * 4 + [(PACK + 1, KEPT, BS)] + [(PACK, KEPT, BS)] * 2
    level1_state = [(8, KEPT1, BS)] * 4 + [(9, KEPT1, BS), (8, KEPT1, BS)]

    arguments = (pltpu.with_memory_space_constraint(a, pltpu.HBM) for a in (viscosity_table, phase, pressure_source))
    stage_scratch = [pltpu.SMEM((3,), F32), pltpu.VMEM((HZ, BC, BS), jnp.int32), pltpu.SemaphoreType.DMA((3,))]
    (own,) = call(stage_kernel, [HBM] * 3, [(2, HZ, BC, BS)], stage_scratch)(*arguments)
    far_cast = swap(own, "cast", True)
    near_cast = swap(own, "cast", False)
    square = (BS, BS)
    tables = [square, (BS, 2 * BS), (4 * BS, BS), square, square, square, square, (2 * BS, BS)]
    tables = [jax.ShapeDtypeStruct(t, BF16) for t in tables]
    near_own, far_own, own_merge, edge_merge, move, *spreads = call(
        prepare_kernel, [VMEM], [(2, 2, BC, BS)] * 2 + tables
    )(own)
    near_span, far_span = call(margin_kernel, [VMEM] * 4, [packed, packed])(near_own, far_own, near_cast, far_cast)
    near_span = swap(near_span, "span", False)
    far_span = swap(far_span, "span", True)
    *kept_own, merged, merged_mid, inner = call(
        own_kernel,
        [VMEM] * 4,
        own_state + [(HZ, HALF, BS), (HZ, HALF - 8, BS), (2, PACK, ROWS, BS)],
        [(HZ, ROWS, BS)],
    )(own, near_cast, far_cast, own_merge)
    (slots,) = call(
        edge_kernel, [VMEM] * 6, [(count, 8, BS)], [(8, SENT, BS), (4, 16, BS)]
    )(near_span, far_span, inner, merged_mid, edge_merge, move)
    kept_edge = call(state_kernel, [VMEM] * 5, edge_state + level1_state, [(8, ROWS, BS)])(
        near_span, far_span, inner, merged, edge_merge
    )

    column = lax.all_to_all(slots, "cast", 0, 0)
    near_column = swap(column, "span", False)
    far_column = swap(column, "span", True)
    rows = 4 * count
    scratch = [
        (3, rows, BS),
        (rows, BS),
        (2, rows, BS),
        (4, rows + 16, BS),
        (4, KEPT1, BS),
        (8, 2 * KEPT1, BS),
        (4, 2 * KEPT1, BS),
        (2, HZ, BC, BS),
        pltpu.SemaphoreType.DMA((2, 4)),
    ]
    state = spreads + kept_own + list(kept_edge)
    return tuple(
        call(ascent_kernel, [VMEM] * (3 + len(state)), [(HZ, BC, BS)] * 2, scratch, HBM)(
            column, far_column, near_column, *state
        )
    )


def solution(mesh):
    blocks = P(None, "cast", "span")
    return jax.shard_map(
        shards,
        mesh=mesh,
        in_specs=(blocks, P(), blocks),
        out_specs=(blocks, blocks),
        check_vma=False,
    )
```

```python
import jax
import jax.numpy as jnp
from jax import lax
from jax.experimental import pallas as pl
from jax.experimental.pallas import tpu as pltpu
from jax.sharding import PartitionSpec as P

HZ, BC, BS = 16, 16, 128
HALO = 16
ROWS = BC + 2 * HALO
HALF = ROWS // 2
KEPT = BC + 8
KEPT1 = HALF - 8
SENT = BC + 16
REACH = (13, 12)
BASE = (0, REACH[0] * HZ)
CAST_ROWS = sum(REACH) * HZ
PACK = HZ // 2
SWEEPS_COARSE = 8
WEIGHT = 0.8
F32 = jnp.float32
BF16 = jnp.bfloat16


def shift(x, step, axis):
    if step == 0:
        return x
    return pltpu.roll(x, step % x.shape[axis], axis)


def iota(shape, axis):
    return lax.broadcasted_iota(jnp.int32, shape, axis)


def product(a, b):
    high = a.astype(BF16)
    low = (a - high.astype(F32)).astype(BF16)
    return jnp.dot(high, b, preferred_element_type=F32) + jnp.dot(low, b, preferred_element_type=F32)


def harmonic(a, b):
    return 2.0 * a * b / (a + b)


def near(x, below, above, cast, span, low, high):
    return (
        cast * shift(x, 1, 0)
        + shift(cast * x, -1, 0)
        + span * shift(x, 1, 1)
        + shift(span * x, -1, 1)
        + low * below
        + high * above
    )


def diagonal_of(cast, span, low, high):
    return cast + shift(cast, -1, 0) + span + shift(span, -1, 1) + low + high


class Level:
    def __init__(self, cast, span, height, diag, relax, source, depth, packed=False):
        self.cast, self.span, self.height = cast, span, height
        self.diag, self.relax, self.source = diag, relax, source
        self.depth, self.packed = depth, packed

    def near(self, x, z):
        last = self.depth - 1
        below, above = x[max(z - 1, 0)], x[min(z + 1, last)]
        if self.packed and z == 0:
            below = shift(x[last], 64, 1)
        if self.packed and z == last:
            above = shift(x[0], 64, 1)
        return near(x[z], below, above, self.cast[z], self.span[z], self.height[z], self.height[z + 1])

    def start(self):
        return [self.relax[z] * self.source[z] for z in range(self.depth)]

    def sweep(self, x):
        return [
            (1.0 - WEIGHT) * x[z] + self.relax[z] * (self.near(x, z) + self.source[z])
            for z in range(self.depth)
        ]

    def solve(self, sweeps):
        part = [
            (
                relax * self.cast[z],
                relax * shift(self.cast[z], -1, 0),
                relax * self.span[z],
                relax * shift(self.span[z], -1, 1),
                relax * self.height[1],
            )
            for z, relax in enumerate(self.relax)
        ]
        first = x = self.start()
        for _ in range(sweeps):
            x = [
                ((1.0 - WEIGHT) * x[z] + first[z] + part[z][4] * x[1 - z])
                + (part[z][0] * shift(x[z], 1, 0) + part[z][1] * shift(x[z], -1, 0))
                + (part[z][2] * shift(x[z], 1, 1) + part[z][3] * shift(x[z], -1, 1))
                for z in range(2)
            ]
        return x

    def residual(self, x):
        return [self.source[z] - self.diag[z] * x[z] + self.near(x, z) for z in range(self.depth)]


def fine_level(visc, source, outside, packed):
    depth = len(visc)
    shape = visc[0].shape
    weight = jnp.where(outside, 0.0, WEIGHT)
    cast = [2.0 / (v + shift(v, 1, 0)) for v in visc]
    span = [2.0 / (v + shift(v, 1, 1)) for v in visc]
    inner = [2.0 / (a + b) for a, b in zip(visc[:-1], visc[1:])]
    if packed:
        bottom = jnp.where(iota(shape, 1) < 64, 0.0, 2.0 / (visc[0] + shift(visc[-1], 64, 1)))
        top = shift(bottom, 64, 1)
    else:
        bottom = top = jnp.zeros(shape, F32)
    height = [bottom] + inner + [top]
    diag = [diagonal_of(cast[z], span[z], height[z], height[z + 1]) for z in range(depth)]
    relax = [weight / d for d in diag]
    return Level(cast, span, height, diag, relax, source, depth, packed)


def kept_rows(value):
    edge = jnp.where(iota((8, BS), 0) < 4, value[HALO + BC : HALO + BC + 8], value[HALO - 8 : HALO])
    return jnp.concatenate([value[HALO : HALO + BC], edge], axis=0)


def kept_rows1(value):
    return jnp.concatenate([value[8:16], jnp.where(iota((8, BS), 0) < 4, value[16:], value[:8])], axis=0)


def keep(level, x, refs):
    for ref, values in zip(refs, (x, level.source, level.cast, level.span, level.height, level.diag, level.relax)):
        for z, value in enumerate(values):
            ref[z] = kept_rows(value)


def coarse_parts(visc, remains, scratch):
    parts = []
    count = len(visc) // 2
    half = visc[0].shape[0] // 2
    for a, values in enumerate(([1.0 / v for v in visc], remains)):
        for k in range(count):
            scratch[a * count + k] = values[2 * k] + values[2 * k + 1]
            ref = scratch.at[a * count + k]
            parts.append(ref[pl.ds(0, half, stride=2), :] + ref[pl.ds(1, half, stride=2), :])
    return jnp.concatenate(parts, axis=0)


def ends(value, first, last, edge):
    rows = value.shape[0]
    row = iota((rows, BS), 0)
    value = jnp.where(first & (row < edge), jnp.broadcast_to(value[edge : edge + 1], (rows, BS)), value)
    stop = rows - edge
    return jnp.where(last & (row >= stop), jnp.broadcast_to(value[stop - 1 : stop], (rows, BS)), value)


def beyond(rows, edge):
    row = iota((rows, BS), 0)
    index = lax.axis_index("cast")
    first, last = index == 0, index == lax.axis_size("cast") - 1
    return first, last, (first & (row < edge)) | (last & (row >= rows - edge))


def height_faces(coeff):
    flat = jnp.zeros_like(coeff[0])
    inner = [harmonic(a, b) for a, b in zip(coeff[:-1], coeff[1:])]
    return [flat] + inner + [flat]


def whole_level(coeff, source):
    shape = coeff[0].shape
    row = iota(shape, 0)
    height = height_faces(coeff)
    cast, span, diag, relax = [], [], [], []
    for z, c in enumerate(coeff):
        lower = jnp.where(row == 0, 0.0, harmonic(shift(c, 1, 0), c))
        ends = jnp.where((row == 0) | (row == shape[0] - 1), c, 0.0)
        side = harmonic(shift(c, 1, 1), c)
        total = diagonal_of(lower, side, height[z], height[z + 1]) + ends
        cast.append(lower)
        span.append(side)
        diag.append(total)
        relax.append(WEIGHT / total)
    return Level(cast, span, height, diag, relax, source, len(coeff))


def pair_rows(value, scratch):
    rows = value.shape[0]
    scratch[...] = value
    return scratch[pl.ds(0, rows // 2, stride=2), :] + scratch[pl.ds(1, rows // 2, stride=2), :]


def by_side(axis, near_pair, far_pair):
    even = lax.rem(lax.axis_index(axis), 2) == 0
    return jnp.where(even, far_pair, near_pair), jnp.where(even, near_pair, far_pair)


def beyond_rows(near_cast, far_cast, a, z):
    reach, base = REACH[a], BASE[a]
    start = base + reach * z

    stop = base + reach * HZ
    even = lax.rem(lax.axis_index("cast"), 2) == 0

    def window(first, one, other):
        at = min(max(first, base), stop - HALO)
        rows = slice(at, at + HALO)
        return shift(jnp.where(even, one[rows], other[rows]), at - first, 0)

    return window(start - (HALO - reach), far_cast, near_cast), window(start, near_cast, far_cast)


def extended(own, near_cast, far_cast, a, z):
    before, after = beyond_rows(near_cast, far_cast, a, z)
    return jnp.concatenate([before, own[a, z], after], axis=0)


def stage_kernel(table_in, phase_in, source_in, out, far_out, near_out, table, phase, sems):
    even = lax.rem(lax.axis_index("cast"), 2) == 0

    def put(a, z, value):
        reach = REACH[a]
        first, last = value, shift(value, reach - HALO, 0)
        rows = HALO if a == 0 or z < HZ - 1 else reach
        place = slice(BASE[a] + reach * z, BASE[a] + reach * z + rows)
        near_out[place] = jnp.where(even, last, first)[:rows]
        far_out[place] = jnp.where(even, first, last)[:rows]

    copies = [
        pltpu.make_async_copy(table_in, table, sems.at[0]),
        pltpu.make_async_copy(phase_in, phase, sems.at[1]),
        pltpu.make_async_copy(source_in, out.at[1], sems.at[2]),
    ]
    for copy in copies:
        copy.start()
    copies[0].wait()
    copies[1].wait()
    for z in range(HZ):
        p = phase[z]
        value = jnp.where(p == 0, table[0], jnp.where(p == 1, table[1], table[2]))
        out[0, z] = value
        put(0, z, value)
    copies[2].wait()
    for z in range(HZ):
        put(1, z, out[1, z])


def ones(where):
    return jnp.where(where, 1.0, 0.0).astype(BF16)


def prepare_kernel(own, near_own, far_own, own_merge, edge_merge, move, narrow, widen, grow, double, expand):
    lane = iota((BC, BS), 1)
    for a in range(2):
        for group in range(2):
            head = tail = None
            for start, z in places(group):
                h, t = shift(own[a, z], start, 1), shift(own[a, z], start + HALO, 1)
                inside = (lane >= start) & (lane < start + HALO)
                head = h if head is None else jnp.where(inside, h, head)
                tail = t if tail is None else jnp.where(inside, t, tail)
            far_own[a, group], near_own[a, group] = by_side("span", tail, head)
    i, j = iota((BS, BS), 0), iota((BS, BS), 1)
    own_merge[...] = ones((i // 2 == j) & (i >= 8) & (i < 120))
    narrow[...] = ones(((i < 64) & (i // 2 == j)) | ((i >= 96) & (i // 2 + 64 == j)))
    widen[...] = ones(((j < 64) & (j // 2 == i)) | ((j >= 96) & (j // 2 + 64 == i)))
    grow[...] = ones(((j < 96) & (j // 2 == i)) | ((j >= 96) & (j // 2 + 64 == i)))
    double[...] = ones(j // 2 == i)
    i, j = iota((BS, 2 * BS), 0), iota((BS, 2 * BS), 1)
    m = i % 64
    target = jnp.where(m < 24, (m // 2 + 120) % BS, m // 2 + 40)
    edge_merge[...] = ones(((m < 24) | (m >= 40)) & (target == j % BS) & (i // 64 == j // BS))
    i, j = iota((4 * BS, BS), 0), iota((4 * BS, BS), 1)
    move[...] = ones((i % BS < 64) & (i % BS // 2 + 32 * (i // BS) == j))
    i, j = iota((2 * BS, BS), 0), iota((2 * BS, BS), 1)
    m = j % 64
    origin = jnp.where(m < 32, (m // 2 + 120) % BS, m // 2 + 40)
    expand[...] = ones((origin == i % BS) & (i // BS == j // 64))


def places(group):
    return [(16 * sub + 64 * half, group * 4 + sub + 8 * half) for sub in range(4) for half in range(2)]


def margin_kernel(near_own, far_own, near_cast, far_cast, near_span, far_span):
    lane = iota((16, BS), 1)
    seg = lane % HALO
    for a in range(2):
        for group in range(2):
            head = tail = None
            for start, z in places(group):
                before, after = beyond_rows(near_cast, far_cast, a, z)
                inner = jnp.concatenate([before[8:], after[:8]], axis=0)
                far = jnp.concatenate([before[:8], after[8:]], axis=0)
                h = jnp.where(seg >= 12, shift(far, start + 12, 1), shift(inner, start, 1))
                t = jnp.where(seg < 4, shift(far, start + HALO - 12, 1), shift(inner, start + HALO, 1))
                inside = (lane >= start) & (lane < start + HALO)
                head = h if head is None else jnp.where(inside, h, head)
                tail = t if tail is None else jnp.where(inside, t, tail)
            sides = by_side("span", tail, head)
            for out, packed, value in ((far_span, far_own, sides[0]), (near_span, near_own, sides[1])):
                out[a, group, :8] = value[:8]
                out[a, group, 8:24] = packed[a, group]
                out[a, group, 24:] = value[8:]


def spread_rows(sent, step, more):
    moved = shift(sent, step, 1)
    return jnp.concatenate([shift(sent[:8], step + more, 1), moved, shift(sent[-8:], step + more, 1)], axis=0)


def own_kernel(own, near_cast, far_cast, own_merge, x, b, cast, span, height, diag, relax, merged, merged_mid, inner, scratch):
    first, last, outside = beyond(ROWS, HALO)
    visc, source = [], []
    for z in range(HZ):
        v, s = (extended(own, near_cast, far_cast, a, z) for a in range(2))
        visc.append(ends(v, first, last, HALO))
        source.append(s)
    lane = iota((ROWS, BS), 1)
    for a, field in enumerate((visc, source)):
        for k in range(PACK):
            low, high = field[k], field[k + PACK]
            inner[a, k] = jnp.where(
                lane < 32,
                shift(low, 16, 1),
                jnp.where(lane < 64, shift(low, 48, 1), jnp.where(lane < 96, shift(high, 80, 1), shift(high, 112, 1))),
            )
    level = fine_level(visc, source, outside, False)
    values = level.sweep(level.start())
    keep(level, values, (x, b, cast, span, height, diag, relax))
    parts = coarse_parts(visc, level.residual(values), scratch)
    total = product(parts, own_merge[...])
    for k in range(HZ):
        merged[k] = total[HALF * k : HALF * (k + 1)]
        merged_mid[k] = total[HALF * k + 4 : HALF * (k + 1) - 4]


def edge_levels(near_span, far_span, inner, merged, edge_merge, scratch, halo):
    rows = BC + 2 * halo
    first, last, outside = beyond(rows, halo)
    lane = iota((rows, BS), 1) % 64
    fields = []
    for a in range(2):
        slabs = []
        for k in range(PACK):
            group, sub = divmod(k, 4)
            left, right = by_side("span", near_span[a, group], far_span[a, group])
            if halo == HALO:
                l, r = spread_rows(left, -16 * sub, 12), spread_rows(right, 48 - 16 * sub, -12)
            else:
                l, r = shift(left, -16 * sub, 1), shift(right, 48 - 16 * sub, 1)
            own = inner[a, k, HALO - halo : HALO + BC + halo]
            value = jnp.where(lane < 16, l, jnp.where(lane >= 48, r, own))
            slabs.append(ends(value, first, last, halo) if a == 0 else value)
        fields.append(slabs)
    visc, source = fields
    level = fine_level(visc, source, outside, True)
    values = level.sweep(level.start())
    fine = level, values
    parts = coarse_parts(visc, level.residual(values), scratch)
    total = product(parts, edge_merge[...])

    edge, half = halo // 2, rows // 2
    first, last, outside = beyond(half, edge)
    weight = jnp.where(outside, 0.0, WEIGHT)
    coarse = []
    for k in range(HZ):
        a, z = divmod(k, 8)
        side, pos = divmod(z, 4)
        row = half * (4 * a + pos)
        coarse.append(merged[k] + total[row : row + half, BS * side : BS * (side + 1)])
    lane = iota((half, BS), 1)
    known = (lane < 72) | (lane >= 120)
    coeff = [jnp.where(known, 0.125 * ends(c, first, last, edge), 1.0) for c in coarse[:8]]
    source = [0.5 * c for c in coarse[8:]]
    height = height_faces(coeff)
    cast_faces = [harmonic(shift(c, 1, 0), c) for c in coeff]
    span_faces = [harmonic(shift(c, 1, 1), c) for c in coeff]
    diagonal = [diagonal_of(cast_faces[z], span_faces[z], height[z], height[z + 1]) for z in range(8)]
    level = Level(cast_faces, span_faces, height, diagonal, [weight / d for d in diagonal], source, 8)
    return fine, (level, level.sweep(level.start()), coeff)


def state_kernel(
    near_span, far_span, inner, merged, edge_merge, x, b, cast, span, height, diag, relax,
    x1, b1, cast1, span1, height1, relax1, scratch,
):
    fine, (level, values, _) = edge_levels(near_span, far_span, inner, merged, edge_merge, scratch, HALO)
    keep(*fine, (x, b, cast, span, height, diag, relax))
    kept = (x1, values), (b1, level.source), (cast1, level.cast), (span1, level.span), (height1, level.height), (relax1, level.relax)
    for ref, items in kept:
        for z, item in enumerate(items):
            ref[z] = kept_rows1(item)


def edge_kernel(near_span, far_span, inner, merged, edge_merge, move, slots, scratch, rows8):
    _, (level, values, coeff) = edge_levels(near_span, far_span, inner, merged, edge_merge, scratch, 8)
    remains = level.residual(values)
    edge = 4

    fields = []
    for k in range(4):
        rows = slice(edge, edge + 8)
        c = coeff[2 * k][rows] + coeff[2 * k + 1][rows]
        r = remains[2 * k][rows] + remains[2 * k + 1][rows]
        rows8[k] = jnp.concatenate([0.125 * c, 0.5 * r], axis=0)
        fields.append(rows8[k, pl.ds(0, 8, stride=2), :] + rows8[k, pl.ds(1, 8, stride=2), :])
    total = product(jnp.concatenate(fields, axis=1), move[...])
    for d in range(slots.shape[0]):
        slots[d] = total


def ascent_kernel(
    own, far_column, near_column, narrow, widen, grow, double, expand,
    xo, bo, casto, spano, heighto, diago, relaxo,
    xe, be, caste, spane, heighte, diage, relaxe,
    x1, b1, cast1, span1, height1, relax1,
    solution_out, residual_out, tiles, pairs, wide2, padded2, wide1, wide_own, wide_edge, results, sems,
):
    count = own.shape[0]
    rows = 4 * count
    lane = iota((rows, 128), 1)
    index = lax.axis_index("cast")

    fields = []
    for part in range(2):
        for d in range(count):
            rows_d = slice(4 * part, 4 * part + 4)
            left, right = by_side("span", near_column[d, rows_d], far_column[d, rows_d])
            for s, block in enumerate((own[d, rows_d], right, left)):
                tiles[s, 4 * d : 4 * d + 4] = block
        slabs = []
        for z in range(4):
            o = shift(tiles[0], -32 * z, 1)
            r = shift(tiles[1], 32 - 32 * z, 1)
            l = shift(tiles[2], 96 - 32 * z, 1)
            fill = 1.0 if part == 0 else 0.0
            slabs.append(jnp.where(lane < 32, o, jnp.where(lane < 64, r, jnp.where(lane >= 96, l, fill))))
        fields.append(slabs)
    coeff2, source2 = fields
    level2 = whole_level(coeff2, source2)
    x2 = level2.sweep(level2.start())
    remains = level2.residual(x2)

    gathered = []
    for field in (coeff2, remains):
        for k in range(2):
            gathered.append(pair_rows(field[2 * k] + field[2 * k + 1], pairs))
    merged = product(jnp.concatenate(gathered, axis=0), narrow[...])
    half = rows // 2
    lane3 = iota((half, 128), 1)
    known = (lane3 < 32) | (lane3 >= 112)
    coeff3 = [jnp.where(known, 0.125 * merged[half * k : half * (k + 1)], 1.0) for k in range(2)]
    source3 = [0.5 * merged[half * (2 + k) : half * (3 + k)] for k in range(2)]
    level3 = whole_level(coeff3, source3)
    x3 = level3.solve(SWEEPS_COARSE - 1)

    spread = product(jnp.concatenate(x3, axis=0), widen[...])
    for k in range(2):
        wide2[k, pl.ds(0, half, stride=2), :] = spread[half * k : half * (k + 1)]
        wide2[k, pl.ds(1, half, stride=2), :] = spread[half * k : half * (k + 1)]
    x2 = [x2[z] + wide2[z // 2] for z in range(4)]
    x2 = level2.sweep(level2.sweep(x2))

    for z in range(4):
        padded2[z, 0:8] = jnp.zeros((8, 128), F32)
        padded2[z, 8 : 8 + rows] = x2[z]
        padded2[z, 8 + rows : 16 + rows] = jnp.zeros((8, 128), F32)
    local = [shift(padded2[z, pl.ds(4 * index + 6, 8), :], -2, 0) for z in range(4)]
    spread = product(jnp.concatenate(local, axis=0), grow[...])
    for z in range(4):
        for s in range(2):
            wide1[z, pl.ds(s, 8, stride=2), :] = spread[8 * z : 8 * z + 8]
    level1 = Level(cast1, span1, height1, None, relax1, b1, 8)
    x = [x1[z] + wide1[z // 2] for z in range(8)]
    x = level1.sweep(level1.sweep(x))

    spread = product(jnp.concatenate(x, axis=0), double[...])
    for z in range(8):
        for s in range(2):
            wide_own[z, pl.ds(s, KEPT1, stride=2), :] = spread[KEPT1 * z : KEPT1 * (z + 1)]
    sides = [jnp.concatenate([x[k], x[k + 4]], axis=1) for k in range(4)]
    spread = product(jnp.concatenate(sides, axis=0), expand[...])
    for k in range(4):
        for s in range(2):
            wide_edge[k, pl.ds(s, KEPT1, stride=2), :] = spread[KEPT1 * k : KEPT1 * (k + 1)]
    level_own = Level(casto, spano, heighto, diago, relaxo, bo, HZ)
    level_edge = Level(caste, spane, heighte, diage, relaxe, be, PACK, True)

    def refined(wide, k):
        edge = jnp.where(iota((8, BS), 0) < 4, wide[k, BC : BC + 8], wide[k, BC + 8 :])
        return jnp.concatenate([wide[k, :BC], edge], axis=0)

    own_wide = [refined(wide_own, k) for k in range(8)]
    edge_wide = [refined(wide_edge, k) for k in range(4)]
    own_x = [xo[z] + own_wide[z // 2] for z in range(HZ)]
    edge_x = [xe[k] + edge_wide[k // 2] for k in range(PACK)]
    edge_x = level_edge.sweep(level_edge.sweep(edge_x))
    own_x = level_own.sweep(level_own.sweep(own_x))
    lane = iota((BC, BS), 1)
    rows = slice(0, BC)

    copies = []

    def give(number, out, z, mid, side):
        half, k = divmod(z, PACK)
        low = shift(side[rows], -16 - 64 * half, 1)
        high = shift(side[rows], 80 - 64 * half, 1)
        results[number, z] = jnp.where(lane < 8, low, jnp.where(lane >= 120, high, mid[rows]))
        if z % 4 == 3:
            quarter = pl.ds(z - 3, 4)
            copy = pltpu.make_async_copy(results.at[number, quarter], out.at[quarter], sems.at[number, z // 4])
            copy.start()
            copies.append(copy)

    for z in range(HZ):
        give(0, solution_out, z, own_x[z], edge_x[z % PACK])
    edge_r = level_edge.residual(edge_x)
    own_r = level_own.residual(own_x)
    for z in range(HZ):
        give(1, residual_out, z, own_r[z], edge_r[z % PACK])
    for copy in copies:
        copy.wait()


VMEM = pl.BlockSpec(memory_space=pltpu.VMEM)
HBM = pl.BlockSpec(memory_space=pltpu.HBM)
PARAMS = pltpu.CompilerParams(vmem_limit_bytes=16 * 1024 * 1024)
INTERPRET = False


def call(kernel, in_specs, outs, scratch=(), out_spec=VMEM):
    return pl.pallas_call(
        kernel,
        in_specs=in_specs,
        out_specs=[out_spec] * len(outs),
        out_shape=[jax.ShapeDtypeStruct(s, F32) if isinstance(s, tuple) else s for s in outs],
        scratch_shapes=[pltpu.VMEM(s, F32) if isinstance(s, tuple) else s for s in scratch],
        compiler_params=PARAMS,
        interpret=INTERPRET,
    )


def swap(value, axis, far):
    size = lax.axis_size(axis)
    partner = [(((i - 1) ^ 1) + 1) % size if far else i ^ 1 for i in range(size)]
    return lax.ppermute(value, axis, list(enumerate(partner)))


def shards(phase, viscosity_table, pressure_source):
    count = lax.axis_size("cast")
    packed = (2, 2, SENT, BS)
    own_state = [(HZ, KEPT, BS)] * 4 + [(HZ + 1, KEPT, BS)] + [(HZ, KEPT, BS)] * 2
    edge_state = [(PACK, KEPT, BS)] * 4 + [(PACK + 1, KEPT, BS)] + [(PACK, KEPT, BS)] * 2
    level1_state = [(8, KEPT1, BS)] * 4 + [(9, KEPT1, BS), (8, KEPT1, BS)]

    arguments = (pltpu.with_memory_space_constraint(a, pltpu.HBM) for a in (viscosity_table, phase, pressure_source))
    stage_scratch = [pltpu.SMEM((3,), F32), pltpu.VMEM((HZ, BC, BS), jnp.int32), pltpu.SemaphoreType.DMA((3,))]
    own, far_cast, near_cast = call(
        stage_kernel, [HBM] * 3, [(2, HZ, BC, BS), (CAST_ROWS, BS), (CAST_ROWS, BS)], stage_scratch
    )(*arguments)
    far_cast = swap(far_cast, "cast", True)
    near_cast = swap(near_cast, "cast", False)
    square = (BS, BS)
    tables = [square, (BS, 2 * BS), (4 * BS, BS), square, square, square, square, (2 * BS, BS)]
    tables = [jax.ShapeDtypeStruct(t, BF16) for t in tables]
    near_own, far_own, own_merge, edge_merge, move, *spreads = call(
        prepare_kernel, [VMEM], [(2, 2, BC, BS)] * 2 + tables
    )(own)
    near_span, far_span = call(margin_kernel, [VMEM] * 4, [packed, packed])(near_own, far_own, near_cast, far_cast)
    near_span = swap(near_span, "span", False)
    far_span = swap(far_span, "span", True)
    *kept_own, merged, merged_mid, inner = call(
        own_kernel,
        [VMEM] * 4,
        own_state + [(HZ, HALF, BS), (HZ, HALF - 8, BS), (2, PACK, ROWS, BS)],
        [(HZ, ROWS, BS)],
    )(own, near_cast, far_cast, own_merge)
    (slots,) = call(
        edge_kernel, [VMEM] * 6, [(count, 8, BS)], [(8, SENT, BS), (4, 16, BS)]
    )(near_span, far_span, inner, merged_mid, edge_merge, move)
    kept_edge = call(state_kernel, [VMEM] * 5, edge_state + level1_state, [(8, ROWS, BS)])(
        near_span, far_span, inner, merged, edge_merge
    )

    column = lax.all_to_all(slots, "cast", 0, 0)
    near_column = swap(column, "span", False)
    far_column = swap(column, "span", True)
    rows = 4 * count
    scratch = [
        (3, rows, BS),
        (rows, BS),
        (2, rows, BS),
        (4, rows + 16, BS),
        (4, KEPT1, BS),
        (8, 2 * KEPT1, BS),
        (4, 2 * KEPT1, BS),
        (2, HZ, BC, BS),
        pltpu.SemaphoreType.DMA((2, 4)),
    ]
    state = spreads + kept_own + list(kept_edge)
    return tuple(
        call(ascent_kernel, [VMEM] * (3 + len(state)), [(HZ, BC, BS)] * 2, scratch, HBM)(
            column, far_column, near_column, *state
        )
    )


def solution(mesh):
    blocks = P(None, "cast", "span")
    return jax.shard_map(
        shards,
        mesh=mesh,
        in_specs=(blocks, P(), blocks),
        out_specs=(blocks, blocks),
        check_vma=False,
    )
```

```python
import jax
import jax.numpy as jnp
from jax import lax
from jax.experimental import pallas as pl
from jax.experimental.pallas import tpu as pltpu
from jax.sharding import PartitionSpec as P

HZ, BC, BS = 16, 16, 128
HALO = 16
ROWS = BC + 2 * HALO
HALF = ROWS // 2
KEPT = BC + 8
KEPT1 = HALF - 8
SENT = BC + 16
REACH = (13, 12)
BASE = (0, REACH[0] * HZ)
CAST_ROWS = sum(REACH) * HZ
PACK = HZ // 2
SWEEPS_COARSE = 8
WEIGHT = 0.8
F32 = jnp.float32
BF16 = jnp.bfloat16


def shift(x, step, axis):
    if step == 0:
        return x
    return pltpu.roll(x, step % x.shape[axis], axis)


def iota(shape, axis):
    return lax.broadcasted_iota(jnp.int32, shape, axis)


def product(a, b):
    high = a.astype(BF16)
    low = (a - high.astype(F32)).astype(BF16)
    return jnp.dot(high, b, preferred_element_type=F32) + jnp.dot(low, b, preferred_element_type=F32)


def harmonic(a, b):
    return 2.0 * a * b / (a + b)


def near(x, below, above, cast, span, low, high):
    return (
        cast * shift(x, 1, 0)
        + shift(cast * x, -1, 0)
        + span * shift(x, 1, 1)
        + shift(span * x, -1, 1)
        + low * below
        + high * above
    )


def diagonal_of(cast, span, low, high):
    return cast + shift(cast, -1, 0) + span + shift(span, -1, 1) + low + high


class Level:
    def __init__(self, cast, span, height, diag, relax, source, depth, packed=False):
        self.cast, self.span, self.height = cast, span, height
        self.diag, self.relax, self.source = diag, relax, source
        self.depth, self.packed = depth, packed

    def near(self, x, z):
        last = self.depth - 1
        below, above = x[max(z - 1, 0)], x[min(z + 1, last)]
        if self.packed and z == 0:
            below = shift(x[last], 64, 1)
        if self.packed and z == last:
            above = shift(x[0], 64, 1)
        return near(x[z], below, above, self.cast[z], self.span[z], self.height[z], self.height[z + 1])

    def start(self):
        return [self.relax[z] * self.source[z] for z in range(self.depth)]

    def sweep(self, x):
        return [
            (1.0 - WEIGHT) * x[z] + self.relax[z] * (self.near(x, z) + self.source[z])
            for z in range(self.depth)
        ]

    def solve(self, sweeps):
        part = [
            (
                relax * self.cast[z],
                relax * shift(self.cast[z], -1, 0),
                relax * self.span[z],
                relax * shift(self.span[z], -1, 1),
                relax * self.height[1],
            )
            for z, relax in enumerate(self.relax)
        ]
        first = x = self.start()
        for _ in range(sweeps):
            x = [
                ((1.0 - WEIGHT) * x[z] + first[z] + part[z][4] * x[1 - z])
                + (part[z][0] * shift(x[z], 1, 0) + part[z][1] * shift(x[z], -1, 0))
                + (part[z][2] * shift(x[z], 1, 1) + part[z][3] * shift(x[z], -1, 1))
                for z in range(2)
            ]
        return x

    def residual(self, x):
        return [self.source[z] - self.diag[z] * x[z] + self.near(x, z) for z in range(self.depth)]


def fine_level(visc, source, outside, packed):
    depth = len(visc)
    shape = visc[0].shape
    weight = jnp.where(outside, 0.0, WEIGHT)
    cast = [2.0 / (v + shift(v, 1, 0)) for v in visc]
    span = [2.0 / (v + shift(v, 1, 1)) for v in visc]
    inner = [2.0 / (a + b) for a, b in zip(visc[:-1], visc[1:])]
    if packed:
        bottom = jnp.where(iota(shape, 1) < 64, 0.0, 2.0 / (visc[0] + shift(visc[-1], 64, 1)))
        top = shift(bottom, 64, 1)
    else:
        bottom = top = jnp.zeros(shape, F32)
    height = [bottom] + inner + [top]
    diag = [diagonal_of(cast[z], span[z], height[z], height[z + 1]) for z in range(depth)]
    relax = [weight / d for d in diag]
    return Level(cast, span, height, diag, relax, source, depth, packed)


def kept_rows(value):
    edge = jnp.where(iota((8, BS), 0) < 4, value[HALO + BC : HALO + BC + 8], value[HALO - 8 : HALO])
    return jnp.concatenate([value[HALO : HALO + BC], edge], axis=0)


def kept_rows1(value):
    return jnp.concatenate([value[8:16], jnp.where(iota((8, BS), 0) < 4, value[16:], value[:8])], axis=0)


def keep(level, x, refs):
    for ref, values in zip(refs, (x, level.source, level.cast, level.span, level.height, level.diag, level.relax)):
        for z, value in enumerate(values):
            ref[z] = kept_rows(value)


def coarse_parts(visc, remains, scratch):
    parts = []
    count = len(visc) // 2
    half = visc[0].shape[0] // 2
    for a, values in enumerate(([1.0 / v for v in visc], remains)):
        for k in range(count):
            scratch[a * count + k] = values[2 * k] + values[2 * k + 1]
            ref = scratch.at[a * count + k]
            parts.append(ref[pl.ds(0, half, stride=2), :] + ref[pl.ds(1, half, stride=2), :])
    return jnp.concatenate(parts, axis=0)


def ends(value, first, last, edge):
    rows = value.shape[0]
    row = iota((rows, BS), 0)
    value = jnp.where(first & (row < edge), jnp.broadcast_to(value[edge : edge + 1], (rows, BS)), value)
    stop = rows - edge
    return jnp.where(last & (row >= stop), jnp.broadcast_to(value[stop - 1 : stop], (rows, BS)), value)


def beyond(rows, edge):
    row = iota((rows, BS), 0)
    index = lax.axis_index("cast")
    first, last = index == 0, index == lax.axis_size("cast") - 1
    return first, last, (first & (row < edge)) | (last & (row >= rows - edge))


def height_faces(coeff):
    flat = jnp.zeros_like(coeff[0])
    inner = [harmonic(a, b) for a, b in zip(coeff[:-1], coeff[1:])]
    return [flat] + inner + [flat]


def whole_level(coeff, source):
    shape = coeff[0].shape
    row = iota(shape, 0)
    height = height_faces(coeff)
    cast, span, diag, relax = [], [], [], []
    for z, c in enumerate(coeff):
        lower = jnp.where(row == 0, 0.0, harmonic(shift(c, 1, 0), c))
        ends = jnp.where((row == 0) | (row == shape[0] - 1), c, 0.0)
        side = harmonic(shift(c, 1, 1), c)
        total = diagonal_of(lower, side, height[z], height[z + 1]) + ends
        cast.append(lower)
        span.append(side)
        diag.append(total)
        relax.append(WEIGHT / total)
    return Level(cast, span, height, diag, relax, source, len(coeff))


def pair_rows(value, scratch):
    rows = value.shape[0]
    scratch[...] = value
    return scratch[pl.ds(0, rows // 2, stride=2), :] + scratch[pl.ds(1, rows // 2, stride=2), :]


def by_side(axis, near_pair, far_pair):
    even = lax.rem(lax.axis_index(axis), 2) == 0
    return jnp.where(even, far_pair, near_pair), jnp.where(even, near_pair, far_pair)


def beyond_rows(near_cast, far_cast, a, z):
    reach, base = REACH[a], BASE[a]
    start = base + reach * z

    stop = base + reach * HZ
    even = lax.rem(lax.axis_index("cast"), 2) == 0

    def window(first, one, other):
        at = min(max(first, base), stop - HALO)
        rows = slice(at, at + HALO)
        return shift(jnp.where(even, one[rows], other[rows]), at - first, 0)

    return window(start - (HALO - reach), far_cast, near_cast), window(start, near_cast, far_cast)


def extended(own, near_cast, far_cast, a, z):
    before, after = beyond_rows(near_cast, far_cast, a, z)
    return jnp.concatenate([before, own[a, z], after], axis=0)


def stage_kernel(table_in, phase_in, source_in, out, far_out, near_out, table, phase, sems):
    even = lax.rem(lax.axis_index("cast"), 2) == 0

    def put(a, z, value):
        reach = REACH[a]
        first, last = value, shift(value, reach - HALO, 0)
        rows = HALO if a == 0 or z < HZ - 1 else reach
        place = slice(BASE[a] + reach * z, BASE[a] + reach * z + rows)
        near_out[place] = jnp.where(even, last, first)[:rows]
        far_out[place] = jnp.where(even, first, last)[:rows]

    copies = [
        pltpu.make_async_copy(table_in, table, sems.at[0]),
        pltpu.make_async_copy(phase_in, phase, sems.at[1]),
        pltpu.make_async_copy(source_in, out.at[1], sems.at[2]),
    ]
    for copy in copies:
        copy.start()
    copies[0].wait()
    copies[1].wait()
    for z in range(HZ):
        p = phase[z]
        value = jnp.where(p == 0, table[0], jnp.where(p == 1, table[1], table[2]))
        out[0, z] = value
        put(0, z, value)
    copies[2].wait()
    for z in range(HZ):
        put(1, z, out[1, z])


def ones(where):
    return jnp.where(where, 1.0, 0.0).astype(BF16)


def prepare_kernel(own, near_own, far_own, own_merge, edge_merge, move, narrow, widen, grow, double, expand):
    lane = iota((BC, BS), 1)
    for a in range(2):
        for group in range(2):
            head = tail = None
            for start, z in places(group):
                h, t = shift(own[a, z], start, 1), shift(own[a, z], start + HALO, 1)
                inside = (lane >= start) & (lane < start + HALO)
                head = h if head is None else jnp.where(inside, h, head)
                tail = t if tail is None else jnp.where(inside, t, tail)
            far_own[a, group], near_own[a, group] = by_side("span", tail, head)
    i, j = iota((BS, BS), 0), iota((BS, BS), 1)
    own_merge[...] = ones((i // 2 == j) & (i >= 8) & (i < 120))
    narrow[...] = ones(((i < 64) & (i // 2 == j)) | ((i >= 96) & (i // 2 + 64 == j)))
    widen[...] = ones(((j < 64) & (j // 2 == i)) | ((j >= 96) & (j // 2 + 64 == i)))
    grow[...] = ones(((j < 96) & (j // 2 == i)) | ((j >= 96) & (j // 2 + 64 == i)))
    double[...] = ones(j // 2 == i)
    i, j = iota((BS, 2 * BS), 0), iota((BS, 2 * BS), 1)
    m = i % 64
    target = jnp.where(m < 24, (m // 2 + 120) % BS, m // 2 + 40)
    edge_merge[...] = ones(((m < 24) | (m >= 40)) & (target == j % BS) & (i // 64 == j // BS))
    i, j = iota((4 * BS, BS), 0), iota((4 * BS, BS), 1)
    move[...] = ones((i % BS < 64) & (i % BS // 2 + 32 * (i // BS) == j))
    i, j = iota((2 * BS, BS), 0), iota((2 * BS, BS), 1)
    m = j % 64
    origin = jnp.where(m < 32, (m // 2 + 120) % BS, m // 2 + 40)
    expand[...] = ones((origin == i % BS) & (i // BS == j // 64))


def places(group):
    return [(16 * sub + 64 * half, group * 4 + sub + 8 * half) for sub in range(4) for half in range(2)]


def margin_kernel(near_own, far_own, far_cast, near_cast, near_span, far_span):
    lane = iota((16, BS), 1)
    seg = lane % HALO
    for a in range(2):
        for group in range(2):
            head = tail = None
            for start, z in places(group):
                before, after = beyond_rows(near_cast, far_cast, a, z)
                inner = jnp.concatenate([before[8:], after[:8]], axis=0)
                far = jnp.concatenate([before[:8], after[8:]], axis=0)
                h = jnp.where(seg >= 12, shift(far, start + 12, 1), shift(inner, start, 1))
                t = jnp.where(seg < 4, shift(far, start + HALO - 12, 1), shift(inner, start + HALO, 1))
                inside = (lane >= start) & (lane < start + HALO)
                head = h if head is None else jnp.where(inside, h, head)
                tail = t if tail is None else jnp.where(inside, t, tail)
            sides = by_side("span", tail, head)
            for out, packed, value in ((far_span, far_own, sides[0]), (near_span, near_own, sides[1])):
                out[a, group, :8] = value[:8]
                out[a, group, 8:24] = packed[a, group]
                out[a, group, 24:] = value[8:]


def spread_rows(sent, step, more):
    moved = shift(sent, step, 1)
    return jnp.concatenate([shift(sent[:8], step + more, 1), moved, shift(sent[-8:], step + more, 1)], axis=0)


def own_kernel(own, far_cast, near_cast, own_merge, x, b, cast, span, height, diag, relax, merged, merged_mid, inner, scratch):
    first, last, outside = beyond(ROWS, HALO)
    visc, source = [], []
    for z in range(HZ):
        v, s = (extended(own, near_cast, far_cast, a, z) for a in range(2))
        visc.append(ends(v, first, last, HALO))
        source.append(s)
    lane = iota((ROWS, BS), 1)
    for a, field in enumerate((visc, source)):
        for k in range(PACK):
            low, high = field[k], field[k + PACK]
            inner[a, k] = jnp.where(
                lane < 32,
                shift(low, 16, 1),
                jnp.where(lane < 64, shift(low, 48, 1), jnp.where(lane < 96, shift(high, 80, 1), shift(high, 112, 1))),
            )
    level = fine_level(visc, source, outside, False)
    values = level.sweep(level.start())
    keep(level, values, (x, b, cast, span, height, diag, relax))
    parts = coarse_parts(visc, level.residual(values), scratch)
    total = product(parts, own_merge[...])
    for k in range(HZ):
        merged[k] = total[HALF * k : HALF * (k + 1)]
        merged_mid[k] = total[HALF * k + 4 : HALF * (k + 1) - 4]


def edge_levels(near_span, far_span, inner, merged, edge_merge, scratch, halo):
    rows = BC + 2 * halo
    first, last, outside = beyond(rows, halo)
    lane = iota((rows, BS), 1) % 64
    fields = []
    for a in range(2):
        slabs = []
        for k in range(PACK):
            group, sub = divmod(k, 4)
            left, right = by_side("span", near_span[a, group], far_span[a, group])
            if halo == HALO:
                l, r = spread_rows(left, -16 * sub, 12), spread_rows(right, 48 - 16 * sub, -12)
            else:
                l, r = shift(left, -16 * sub, 1), shift(right, 48 - 16 * sub, 1)
            own = inner[a, k, HALO - halo : HALO + BC + halo]
            value = jnp.where(lane < 16, l, jnp.where(lane >= 48, r, own))
            slabs.append(ends(value, first, last, halo) if a == 0 else value)
        fields.append(slabs)
    visc, source = fields
    level = fine_level(visc, source, outside, True)
    values = level.sweep(level.start())
    fine = level, values
    parts = coarse_parts(visc, level.residual(values), scratch)
    total = product(parts, edge_merge[...])

    edge, half = halo // 2, rows // 2
    first, last, outside = beyond(half, edge)
    weight = jnp.where(outside, 0.0, WEIGHT)
    coarse = []
    for k in range(HZ):
        a, z = divmod(k, 8)
        side, pos = divmod(z, 4)
        row = half * (4 * a + pos)
        coarse.append(merged[k] + total[row : row + half, BS * side : BS * (side + 1)])
    lane = iota((half, BS), 1)
    known = (lane < 72) | (lane >= 120)
    coeff = [jnp.where(known, 0.125 * ends(c, first, last, edge), 1.0) for c in coarse[:8]]
    source = [0.5 * c for c in coarse[8:]]
    height = height_faces(coeff)
    cast_faces = [harmonic(shift(c, 1, 0), c) for c in coeff]
    span_faces = [harmonic(shift(c, 1, 1), c) for c in coeff]
    diagonal = [diagonal_of(cast_faces[z], span_faces[z], height[z], height[z + 1]) for z in range(8)]
    level = Level(cast_faces, span_faces, height, diagonal, [weight / d for d in diagonal], source, 8)
    return fine, (level, level.sweep(level.start()), coeff)


def state_kernel(
    near_span, far_span, inner, merged, edge_merge, x, b, cast, span, height, diag, relax,
    x1, b1, cast1, span1, height1, relax1, scratch,
):
    fine, (level, values, _) = edge_levels(near_span, far_span, inner, merged, edge_merge, scratch, HALO)
    keep(*fine, (x, b, cast, span, height, diag, relax))
    kept = (x1, values), (b1, level.source), (cast1, level.cast), (span1, level.span), (height1, level.height), (relax1, level.relax)
    for ref, items in kept:
        for z, item in enumerate(items):
            ref[z] = kept_rows1(item)


def edge_kernel(near_span, far_span, inner, merged, edge_merge, move, slots, scratch, rows8):
    _, (level, values, coeff) = edge_levels(near_span, far_span, inner, merged, edge_merge, scratch, 8)
    remains = level.residual(values)
    edge = 4

    fields = []
    for k in range(4):
        rows = slice(edge, edge + 8)
        c = coeff[2 * k][rows] + coeff[2 * k + 1][rows]
        r = remains[2 * k][rows] + remains[2 * k + 1][rows]
        rows8[k] = jnp.concatenate([0.125 * c, 0.5 * r], axis=0)
        fields.append(rows8[k, pl.ds(0, 8, stride=2), :] + rows8[k, pl.ds(1, 8, stride=2), :])
    total = product(jnp.concatenate(fields, axis=1), move[...])
    for d in range(slots.shape[0]):
        slots[d] = total


def ascent_kernel(
    own, far_column, near_column, narrow, widen, grow, double, expand,
    xo, bo, casto, spano, heighto, diago, relaxo,
    xe, be, caste, spane, heighte, diage, relaxe,
    x1, b1, cast1, span1, height1, relax1,
    solution_out, residual_out, tiles, pairs, wide2, padded2, wide1, wide_own, wide_edge, results, sems,
):
    count = own.shape[0]
    rows = 4 * count
    part_lane = iota((rows, 128), 1) // 32
    index = lax.axis_index("cast")

    fields = []
    for part in range(2):
        for d in range(count):
            rows_d = slice(4 * part, 4 * part + 4)
            left, right = by_side("span", near_column[d, rows_d], far_column[d, rows_d])
            for s, block in enumerate((own[d, rows_d], right, left)):
                tiles[s, 4 * d : 4 * d + 4] = block
        own_tile, right, left = tiles[0], shift(tiles[1], 32, 1), shift(tiles[2], -32, 1)
        slabs = []
        for z in range(4):
            both = jnp.where(part_lane == (z + 1) % 4, right, left)
            slabs.append(shift(jnp.where(part_lane == z, own_tile, both), -32 * z, 1))
        fields.append(slabs)
    coeff2, source2 = fields
    level2 = whole_level(coeff2, source2)
    x2 = level2.sweep(level2.start())
    remains = level2.residual(x2)

    gathered = []
    for field in (coeff2, remains):
        for k in range(2):
            gathered.append(pair_rows(field[2 * k] + field[2 * k + 1], pairs))
    merged = product(jnp.concatenate(gathered, axis=0), narrow[...])
    half = rows // 2
    lane3 = iota((half, 128), 1)
    known = (lane3 < 32) | (lane3 >= 112)
    coeff3 = [jnp.where(known, 0.125 * merged[half * k : half * (k + 1)], 1.0) for k in range(2)]
    source3 = [0.5 * merged[half * (2 + k) : half * (3 + k)] for k in range(2)]
    level3 = whole_level(coeff3, source3)
    x3 = level3.solve(SWEEPS_COARSE - 1)

    spread = product(jnp.concatenate(x3, axis=0), widen[...])
    for k in range(2):
        wide2[k, pl.ds(0, half, stride=2), :] = spread[half * k : half * (k + 1)]
        wide2[k, pl.ds(1, half, stride=2), :] = spread[half * k : half * (k + 1)]
    x2 = [x2[z] + wide2[z // 2] for z in range(4)]
    x2 = level2.sweep(level2.sweep(x2))

    for z in range(4):
        padded2[z, 0:8] = jnp.zeros((8, 128), F32)
        padded2[z, 8 : 8 + rows] = x2[z]
        padded2[z, 8 + rows : 16 + rows] = jnp.zeros((8, 128), F32)
    local = [shift(padded2[z, pl.ds(4 * index + 6, 8), :], -2, 0) for z in range(4)]
    spread = product(jnp.concatenate(local, axis=0), grow[...])
    for z in range(4):
        for s in range(2):
            wide1[z, pl.ds(s, 8, stride=2), :] = spread[8 * z : 8 * z + 8]
    level1 = Level(cast1, span1, height1, None, relax1, b1, 8)
    x = [x1[z] + wide1[z // 2] for z in range(8)]
    x = level1.sweep(level1.sweep(x))

    spread = product(jnp.concatenate(x, axis=0), double[...])
    for z in range(8):
        for s in range(2):
            wide_own[z, pl.ds(s, KEPT1, stride=2), :] = spread[KEPT1 * z : KEPT1 * (z + 1)]
    sides = [jnp.concatenate([x[k], x[k + 4]], axis=1) for k in range(4)]
    spread = product(jnp.concatenate(sides, axis=0), expand[...])
    for k in range(4):
        for s in range(2):
            wide_edge[k, pl.ds(s, KEPT1, stride=2), :] = spread[KEPT1 * k : KEPT1 * (k + 1)]
    level_own = Level(casto, spano, heighto, diago, relaxo, bo, HZ)
    level_edge = Level(caste, spane, heighte, diage, relaxe, be, PACK, True)

    def refined(wide, k):
        edge = jnp.where(iota((8, BS), 0) < 4, wide[k, BC : BC + 8], wide[k, BC + 8 :])
        return jnp.concatenate([wide[k, :BC], edge], axis=0)

    own_wide = [refined(wide_own, k) for k in range(8)]
    edge_wide = [refined(wide_edge, k) for k in range(4)]
    own_x = [xo[z] + own_wide[z // 2] for z in range(HZ)]
    edge_x = [xe[k] + edge_wide[k // 2] for k in range(PACK)]
    edge_x = level_edge.sweep(level_edge.sweep(edge_x))
    own_x = level_own.sweep(level_own.sweep(own_x))
    lane = iota((BC, BS), 1)
    rows = slice(0, BC)

    copies = []

    beside = lane % 64 < 16

    def joined(side):
        return jnp.where(beside, shift(side[rows], -32, 1), side[rows])

    def give(number, out, z, mid, side):
        value = shift(side, -16 - 64 * (z // PACK), 1)
        results[number, z] = jnp.where((lane < 8) | (lane >= 120), value, mid[rows])
        if z % 4 == 3:
            quarter = pl.ds(z - 3, 4)
            copy = pltpu.make_async_copy(results.at[number, quarter], out.at[quarter], sems.at[number, z // 4])
            copy.start()
            copies.append(copy)

    sides = [joined(value) for value in edge_x]
    for z in range(HZ):
        give(0, solution_out, z, own_x[z], sides[z % PACK])
    edge_r = level_edge.residual(edge_x)
    own_r = level_own.residual(own_x)
    sides = [joined(value) for value in edge_r]
    for z in range(HZ):
        give(1, residual_out, z, own_r[z], sides[z % PACK])
    for copy in copies:
        copy.wait()


VMEM = pl.BlockSpec(memory_space=pltpu.VMEM)
HBM = pl.BlockSpec(memory_space=pltpu.HBM)
PARAMS = pltpu.CompilerParams(vmem_limit_bytes=16 * 1024 * 1024)
INTERPRET = False


def call(kernel, in_specs, outs, scratch=(), out_spec=VMEM):
    return pl.pallas_call(
        kernel,
        in_specs=in_specs,
        out_specs=[out_spec] * len(outs),
        out_shape=[jax.ShapeDtypeStruct(s, F32) if isinstance(s, tuple) else s for s in outs],
        scratch_shapes=[pltpu.VMEM(s, F32) if isinstance(s, tuple) else s for s in scratch],
        compiler_params=PARAMS,
        interpret=INTERPRET,
    )


def swap(value, axis, far):
    size = lax.axis_size(axis)
    partner = [(((i - 1) ^ 1) + 1) % size if far else i ^ 1 for i in range(size)]
    return lax.ppermute(value, axis, list(enumerate(partner)))


def shards(phase, viscosity_table, pressure_source):
    count = lax.axis_size("cast")
    packed = (2, 2, SENT, BS)
    own_state = [(HZ, KEPT, BS)] * 4 + [(HZ + 1, KEPT, BS)] + [(HZ, KEPT, BS)] * 2
    edge_state = [(PACK, KEPT, BS)] * 4 + [(PACK + 1, KEPT, BS)] + [(PACK, KEPT, BS)] * 2
    level1_state = [(8, KEPT1, BS)] * 4 + [(9, KEPT1, BS), (8, KEPT1, BS)]

    arguments = (pltpu.with_memory_space_constraint(a, pltpu.HBM) for a in (viscosity_table, phase, pressure_source))
    stage_scratch = [pltpu.SMEM((3,), F32), pltpu.VMEM((HZ, BC, BS), jnp.int32), pltpu.SemaphoreType.DMA((3,))]
    own, far_cast, near_cast = call(
        stage_kernel, [HBM] * 3, [(2, HZ, BC, BS), (CAST_ROWS, BS), (CAST_ROWS, BS)], stage_scratch
    )(*arguments)
    far_cast = swap(far_cast, "cast", True)
    near_cast = swap(near_cast, "cast", False)
    square = (BS, BS)
    tables = [square, (BS, 2 * BS), (4 * BS, BS), square, square, square, square, (2 * BS, BS)]
    tables = [jax.ShapeDtypeStruct(t, BF16) for t in tables]
    near_own, far_own, own_merge, edge_merge, move, *spreads = call(
        prepare_kernel, [VMEM], [(2, 2, BC, BS)] * 2 + tables
    )(own)
    near_span, far_span = call(margin_kernel, [VMEM] * 4, [packed, packed])(near_own, far_own, far_cast, near_cast)
    near_span = swap(near_span, "span", False)
    far_span = swap(far_span, "span", True)
    *kept_own, merged, merged_mid, inner = call(
        own_kernel,
        [VMEM] * 4,
        own_state + [(HZ, HALF, BS), (HZ, HALF - 8, BS), (2, PACK, ROWS, BS)],
        [(HZ, ROWS, BS)],
    )(own, far_cast, near_cast, own_merge)
    (slots,) = call(
        edge_kernel, [VMEM] * 6, [(count, 8, BS)], [(8, SENT, BS), (4, 16, BS)]
    )(near_span, far_span, inner, merged_mid, edge_merge, move)
    kept_edge = call(state_kernel, [VMEM] * 5, edge_state + level1_state, [(8, ROWS, BS)])(
        near_span, far_span, inner, merged, edge_merge
    )

    column = lax.all_to_all(slots, "cast", 0, 0)
    near_column = swap(column, "span", False)
    far_column = swap(column, "span", True)
    rows = 4 * count
    scratch = [
        (3, rows, BS),
        (rows, BS),
        (2, rows, BS),
        (4, rows + 16, BS),
        (4, KEPT1, BS),
        (8, 2 * KEPT1, BS),
        (4, 2 * KEPT1, BS),
        (2, HZ, BC, BS),
        pltpu.SemaphoreType.DMA((2, 4)),
    ]
    state = spreads + kept_own + list(kept_edge)
    return tuple(
        call(ascent_kernel, [VMEM] * (3 + len(state)), [(HZ, BC, BS)] * 2, scratch, HBM)(
            column, far_column, near_column, *state
        )
    )


def solution(mesh):
    blocks = P(None, "cast", "span")
    return jax.shard_map(
        shards,
        mesh=mesh,
        in_specs=(blocks, P(), blocks),
        out_specs=(blocks, blocks),
        check_vma=False,
    )
```

```python
import jax
import jax.numpy as jnp
from jax import lax
from jax.experimental import pallas as pl
from jax.experimental.pallas import tpu as pltpu
from jax.sharding import PartitionSpec as P

HZ, BC, BS = 16, 16, 128
HALO = 16
ROWS = BC + 2 * HALO
HALF = ROWS // 2
KEPT = BC + 8
KEPT1 = HALF - 8
SENT = BC + 16
REACH = (13, 12)
BASE = (0, REACH[0] * HZ)
CAST_ROWS = sum(REACH) * HZ
PACK = HZ // 2
SWEEPS_COARSE = 8
WEIGHT = 0.8
F32 = jnp.float32
BF16 = jnp.bfloat16


def shift(x, step, axis):
    if step == 0:
        return x
    return pltpu.roll(x, step % x.shape[axis], axis)


def iota(shape, axis):
    return lax.broadcasted_iota(jnp.int32, shape, axis)


def product(a, b):
    high = a.astype(BF16)
    low = (a - high.astype(F32)).astype(BF16)
    return jnp.dot(high, b, preferred_element_type=F32) + jnp.dot(low, b, preferred_element_type=F32)


def harmonic(a, b):
    return 2.0 * a * b / (a + b)


def near(x, below, above, cast, span, low, high):
    return (
        cast * shift(x, 1, 0)
        + shift(cast * x, -1, 0)
        + span * shift(x, 1, 1)
        + shift(span * x, -1, 1)
        + low * below
        + high * above
    )


def diagonal_of(cast, span, low, high):
    return cast + shift(cast, -1, 0) + span + shift(span, -1, 1) + low + high


class Level:
    def __init__(self, cast, span, height, diag, relax, source, depth, packed=1):
        self.cast, self.span, self.height = cast, span, height
        self.diag, self.relax, self.source = diag, relax, source
        self.depth, self.packed = depth, packed

    def near(self, x, z):
        last = self.depth - 1
        below, above = x[max(z - 1, 0)], x[min(z + 1, last)]
        if self.packed > 1 and z == 0:
            below = shift(x[last], BS // self.packed, 1)
        if self.packed > 1 and z == last:
            above = shift(x[0], -(BS // self.packed), 1)
        return near(x[z], below, above, self.cast[z], self.span[z], self.height[z], self.height[z + 1])

    def start(self):
        return [self.relax[z] * self.source[z] for z in range(self.depth)]

    def sweep(self, x):
        return [
            (1.0 - WEIGHT) * x[z] + self.relax[z] * (self.near(x, z) + self.source[z])
            for z in range(self.depth)
        ]

    def solve(self, sweeps):
        part = [
            (
                relax * self.cast[z],
                relax * shift(self.cast[z], -1, 0),
                relax * self.span[z],
                relax * shift(self.span[z], -1, 1),
                relax * self.height[1],
            )
            for z, relax in enumerate(self.relax)
        ]
        first = x = self.start()
        for _ in range(sweeps):
            x = [
                ((1.0 - WEIGHT) * x[z] + first[z] + part[z][4] * x[1 - z])
                + (part[z][0] * shift(x[z], 1, 0) + part[z][1] * shift(x[z], -1, 0))
                + (part[z][2] * shift(x[z], 1, 1) + part[z][3] * shift(x[z], -1, 1))
                for z in range(2)
            ]
        return x

    def residual(self, x):
        return [self.source[z] - self.diag[z] * x[z] + self.near(x, z) for z in range(self.depth)]


def fine_level(visc, source, outside, packed):
    depth = len(visc)
    shape = visc[0].shape
    weight = jnp.where(outside, 0.0, WEIGHT)
    cast = [2.0 / (v + shift(v, 1, 0)) for v in visc]
    span = [2.0 / (v + shift(v, 1, 1)) for v in visc]
    inner = [2.0 / (a + b) for a, b in zip(visc[:-1], visc[1:])]
    if packed > 1:
        width = BS // packed
        bottom = jnp.where(iota(shape, 1) < width, 0.0, 2.0 / (visc[0] + shift(visc[-1], width, 1)))
        top = shift(bottom, -width, 1)
    else:
        bottom = top = jnp.zeros(shape, F32)
    height = [bottom] + inner + [top]
    diag = [diagonal_of(cast[z], span[z], height[z], height[z + 1]) for z in range(depth)]
    relax = [weight / d for d in diag]
    return Level(cast, span, height, diag, relax, source, depth, packed)


def kept_rows(value):
    edge = jnp.where(iota((8, BS), 0) < 4, value[HALO + BC : HALO + BC + 8], value[HALO - 8 : HALO])
    return jnp.concatenate([value[HALO : HALO + BC], edge], axis=0)


def kept_rows1(value):
    return jnp.concatenate([value[8:16], jnp.where(iota((8, BS), 0) < 4, value[16:], value[:8])], axis=0)


def keep(level, x, refs):
    for ref, values in zip(refs, (x, level.source, level.cast, level.span, level.height, level.diag, level.relax)):
        for z, value in enumerate(values):
            ref[z] = kept_rows(value)


def coarse_parts(visc, remains, scratch):
    parts = []
    count = len(visc) // 2
    half = visc[0].shape[0] // 2
    for a, values in enumerate(([1.0 / v for v in visc], remains)):
        for k in range(count):
            scratch[a * count + k] = values[2 * k] + values[2 * k + 1]
            ref = scratch.at[a * count + k]
            parts.append(ref[pl.ds(0, half, stride=2), :] + ref[pl.ds(1, half, stride=2), :])
    return jnp.concatenate(parts, axis=0)


def ends(value, first, last, edge):
    rows = value.shape[0]
    row = iota((rows, BS), 0)
    value = jnp.where(first & (row < edge), jnp.broadcast_to(value[edge : edge + 1], (rows, BS)), value)
    stop = rows - edge
    return jnp.where(last & (row >= stop), jnp.broadcast_to(value[stop - 1 : stop], (rows, BS)), value)


def beyond(rows, edge):
    row = iota((rows, BS), 0)
    index = lax.axis_index("cast")
    first, last = index == 0, index == lax.axis_size("cast") - 1
    return first, last, (first & (row < edge)) | (last & (row >= rows - edge))


def height_faces(coeff):
    flat = jnp.zeros_like(coeff[0])
    inner = [harmonic(a, b) for a, b in zip(coeff[:-1], coeff[1:])]
    return [flat] + inner + [flat]


def whole_level(coeff, source):
    shape = coeff[0].shape
    row = iota(shape, 0)
    height = height_faces(coeff)
    cast, span, diag, relax = [], [], [], []
    for z, c in enumerate(coeff):
        lower = jnp.where(row == 0, 0.0, harmonic(shift(c, 1, 0), c))
        ends = jnp.where((row == 0) | (row == shape[0] - 1), c, 0.0)
        side = harmonic(shift(c, 1, 1), c)
        total = diagonal_of(lower, side, height[z], height[z + 1]) + ends
        cast.append(lower)
        span.append(side)
        diag.append(total)
        relax.append(WEIGHT / total)
    return Level(cast, span, height, diag, relax, source, len(coeff))


def pair_rows(value, scratch):
    rows = value.shape[0]
    scratch[...] = value
    return scratch[pl.ds(0, rows // 2, stride=2), :] + scratch[pl.ds(1, rows // 2, stride=2), :]


def by_side(axis, near_pair, far_pair):
    even = lax.rem(lax.axis_index(axis), 2) == 0
    return jnp.where(even, far_pair, near_pair), jnp.where(even, near_pair, far_pair)


def beyond_rows(near_cast, far_cast, a, z):
    reach, base = REACH[a], BASE[a]
    start = base + reach * z

    stop = base + reach * HZ
    even = lax.rem(lax.axis_index("cast"), 2) == 0

    def window(first, one, other):
        at = min(max(first, base), stop - HALO)
        rows = slice(at, at + HALO)
        return shift(jnp.where(even, one[rows], other[rows]), at - first, 0)

    return window(start - (HALO - reach), far_cast, near_cast), window(start, near_cast, far_cast)


def extended(own, near_cast, far_cast, a, z):
    before, after = beyond_rows(near_cast, far_cast, a, z)
    return jnp.concatenate([before, own[a, z], after], axis=0)


def stage_kernel(table_in, phase_in, source_in, out, far_out, near_out, table, phase, sems):
    even = lax.rem(lax.axis_index("cast"), 2) == 0

    def put(a, z, value):
        reach = REACH[a]
        first, last = value, shift(value, reach - HALO, 0)
        rows = HALO if a == 0 or z < HZ - 1 else reach
        place = slice(BASE[a] + reach * z, BASE[a] + reach * z + rows)
        near_out[place] = jnp.where(even, last, first)[:rows]
        far_out[place] = jnp.where(even, first, last)[:rows]

    copies = [
        pltpu.make_async_copy(table_in, table, sems.at[0]),
        pltpu.make_async_copy(phase_in, phase, sems.at[1]),
        pltpu.make_async_copy(source_in, out.at[1], sems.at[2]),
    ]
    for copy in copies:
        copy.start()
    copies[0].wait()
    copies[1].wait()
    for z in range(HZ):
        p = phase[z]
        value = jnp.where(p == 0, table[0], jnp.where(p == 1, table[1], table[2]))
        out[0, z] = value
        put(0, z, value)
    copies[2].wait()
    for z in range(HZ):
        put(1, z, out[1, z])


def ones(where):
    return jnp.where(where, 1.0, 0.0).astype(BF16)


def prepare_kernel(own, near_own, far_own, own_merge, mid_merge, edge_merge, slot_merge, move, narrow, widen, grow, double, expand):
    lane = iota((BC, BS), 1)
    for a in range(2):
        for group in range(2):
            head = tail = None
            for start, z in places(group):
                h, t = shift(own[a, z], start, 1), shift(own[a, z], start + HALO, 1)
                inside = (lane >= start) & (lane < start + HALO)
                head = h if head is None else jnp.where(inside, h, head)
                tail = t if tail is None else jnp.where(inside, t, tail)
            far_own[a, group], near_own[a, group] = by_side("span", tail, head)
    i, j = iota((BS, BS), 0), iota((BS, BS), 1)
    own_merge[...] = ones((i // 2 == j) & (i >= 8) & (i < 120))
    mid_merge[...] = ones((i // 2 == j) & (i >= 4) & (i < 124))
    narrow[...] = ones(((i < 64) & (i // 2 == j)) | ((i >= 96) & (i // 2 + 64 == j)))
    widen[...] = ones(((j < 64) & (j // 2 == i)) | ((j >= 96) & (j // 2 + 64 == i)))
    grow[...] = ones(((j < 96) & (j // 2 == i)) | ((j >= 96) & (j // 2 + 64 == i)))
    double[...] = ones(j // 2 == i)
    i, j = iota((BS, 2 * BS), 0), iota((BS, 2 * BS), 1)
    m = i % 64
    target = jnp.where(m < 24, (m // 2 + 120) % BS, m // 2 + 40)
    edge_merge[...] = ones(((m < 24) | (m >= 40)) & (target == j % BS) & (i // 64 == j // BS))
    i, j = iota((BS, 4 * BS), 0), iota((BS, 4 * BS), 1)
    m = i % 32
    target = jnp.where(m < 12, (m // 2 + 124) % BS, m // 2 + 52)
    slot_merge[...] = ones(((m < 12) | (m >= 20)) & (target == j % BS) & (i // 32 == j // BS))
    i, j = iota((4 * BS, BS), 0), iota((4 * BS, BS), 1)
    move[...] = ones((i % BS < 64) & (i % BS // 2 + 32 * (i // BS) == j))
    i, j = iota((2 * BS, BS), 0), iota((2 * BS, BS), 1)
    m = j % 64
    origin = jnp.where(m < 32, (m // 2 + 120) % BS, m // 2 + 40)
    expand[...] = ones((origin == i % BS) & (i // BS == j // 64))


def places(group):
    return [(16 * sub + 32 * g, group * 2 + sub + 4 * g) for sub in range(2) for g in range(4)]


def margin_kernel(near_own, far_own, far_cast, near_cast, near_span, far_span):
    lane = iota((16, BS), 1)
    seg = lane % HALO
    for a in range(2):
        for group in range(2):
            head = tail = None
            for start, z in places(group):
                before, after = beyond_rows(near_cast, far_cast, a, z)
                inner = jnp.concatenate([before[8:], after[:8]], axis=0)
                far = jnp.concatenate([before[:8], after[8:]], axis=0)
                h = jnp.where(seg >= 12, shift(far, start + 12, 1), shift(inner, start, 1))
                t = jnp.where(seg < 4, shift(far, start + HALO - 12, 1), shift(inner, start + HALO, 1))
                inside = (lane >= start) & (lane < start + HALO)
                head = h if head is None else jnp.where(inside, h, head)
                tail = t if tail is None else jnp.where(inside, t, tail)
            sides = by_side("span", tail, head)
            for out, packed, value in ((far_span, far_own, sides[0]), (near_span, near_own, sides[1])):
                out[a, group, :8] = value[:8]
                out[a, group, 8:24] = packed[a, group]
                out[a, group, 24:] = value[8:]


def spread_rows(sent, step, more):
    moved = shift(sent, step, 1)
    return jnp.concatenate([shift(sent[:8], step + more, 1), moved, shift(sent[-8:], step + more, 1)], axis=0)


def own_kernel(own, far_cast, near_cast, own_merge, mid_merge, x, b, cast, span, height, diag, relax, merged, merged_mid, inner, inner4, scratch):
    first, last, outside = beyond(ROWS, HALO)
    visc, source = [], []
    for z in range(HZ):
        v, s = (extended(own, near_cast, far_cast, a, z) for a in range(2))
        visc.append(ends(v, first, last, HALO))
        source.append(s)
    lane = iota((ROWS, BS), 1)
    for a, field in enumerate((visc, source)):
        for k in range(PACK):
            low, high = field[k], field[k + PACK]
            inner[a, k] = jnp.where(
                lane < 32,
                shift(low, 16, 1),
                jnp.where(lane < 64, shift(low, 48, 1), jnp.where(lane < 96, shift(high, 80, 1), shift(high, 112, 1))),
            )
        quarter = lane[8 : ROWS - 8]
        for k in range(4):
            value = None
            for g in range(4):
                slab = field[k + 4 * g][8 : ROWS - 8]
                edges = jnp.where(quarter % 32 < 16, shift(slab, 32 * g + 8, 1), shift(slab, 32 * g - 104, 1))
                value = edges if value is None else jnp.where(quarter // 32 == g, edges, value)
            inner4[a, k] = value
    level = fine_level(visc, source, outside, 1)
    values = level.sweep(level.start())
    keep(level, values, (x, b, cast, span, height, diag, relax))
    parts = coarse_parts(visc, level.residual(values), scratch)
    total = product(parts, own_merge[...])
    for k in range(HZ):
        merged[k] = total[HALF * k : HALF * (k + 1)]
    total = product(parts, mid_merge[...])
    for k in range(HZ):
        merged_mid[k] = total[HALF * k + 4 : HALF * (k + 1) - 4]


def edge_levels(near_span, far_span, inner, merged, edge_merge, scratch, halo):
    rows = BC + 2 * halo
    first, last, outside = beyond(rows, halo)
    wide = halo == HALO
    packed = 2 if wide else 4
    lane = iota((rows, BS), 1) % (BS // packed)
    fields = []
    for a in range(2):
        slabs = []
        for k in range(HZ // packed):
            group, offset = k % 4 // 2, 16 * (k % 2) + 32 * (k // 4)
            left, right = by_side("span", near_span[a, group], far_span[a, group])
            if wide:
                l, r = spread_rows(left, -offset, 12), spread_rows(right, 48 - offset, -12)
                value = jnp.where(lane < 16, l, jnp.where(lane >= 48, r, inner[a, k]))
            else:
                l, r = shift(left, -offset - 8, 1), shift(right, 24 - offset, 1)
                value = jnp.where(lane < 8, l, jnp.where(lane >= 24, r, inner[a, k]))
            slabs.append(ends(value, first, last, halo) if a == 0 else value)
        fields.append(slabs)
    visc, source = fields
    level = fine_level(visc, source, outside, packed)
    values = level.sweep(level.start())
    fine = level, values
    parts = coarse_parts(visc, level.residual(values), scratch)
    total = product(parts, edge_merge[...])

    edge, half = halo // 2, rows // 2
    first, last, outside = beyond(half, edge)
    weight = jnp.where(outside, 0.0, WEIGHT)
    coarse = []
    for k in range(HZ):
        a, z = divmod(k, 8)
        side, pos = divmod(z, 4 if wide else 2)
        row = half * (HZ // packed // 2 * a + pos)
        coarse.append(merged[k] + total[row : row + half, BS * side : BS * (side + 1)])
    lane = iota((half, BS), 1)
    known = (lane < BS // 2 + edge) | (lane >= BS - edge)
    coeff = [jnp.where(known, 0.125 * ends(c, first, last, edge), 1.0) for c in coarse[:8]]
    source = [0.5 * c for c in coarse[8:]]
    height = height_faces(coeff)
    cast_faces = [harmonic(shift(c, 1, 0), c) for c in coeff]
    span_faces = [harmonic(shift(c, 1, 1), c) for c in coeff]
    diagonal = [diagonal_of(cast_faces[z], span_faces[z], height[z], height[z + 1]) for z in range(8)]
    level = Level(cast_faces, span_faces, height, diagonal, [weight / d for d in diagonal], source, 8)
    return fine, (level, level.sweep(level.start()), coeff)


def state_kernel(
    near_span, far_span, inner, merged, edge_merge, x, b, cast, span, height, diag, relax,
    x1, b1, cast1, span1, height1, relax1, scratch,
):
    fine, (level, values, _) = edge_levels(near_span, far_span, inner, merged, edge_merge, scratch, HALO)
    keep(*fine, (x, b, cast, span, height, diag, relax))
    kept = (x1, values), (b1, level.source), (cast1, level.cast), (span1, level.span), (height1, level.height), (relax1, level.relax)
    for ref, items in kept:
        for z, item in enumerate(items):
            ref[z] = kept_rows1(item)


def edge_kernel(near_span, far_span, inner, merged, edge_merge, move, slots, scratch, rows8):
    _, (level, values, coeff) = edge_levels(near_span, far_span, inner, merged, edge_merge, scratch, 8)
    remains = level.residual(values)
    edge = 4

    fields = []
    for k in range(4):
        rows = slice(edge, edge + 8)
        c = coeff[2 * k][rows] + coeff[2 * k + 1][rows]
        r = remains[2 * k][rows] + remains[2 * k + 1][rows]
        rows8[k] = jnp.concatenate([0.125 * c, 0.5 * r], axis=0)
        fields.append(rows8[k, pl.ds(0, 8, stride=2), :] + rows8[k, pl.ds(1, 8, stride=2), :])
    total = product(jnp.concatenate(fields, axis=1), move[...])
    for d in range(slots.shape[0]):
        slots[d] = total


def ascent_kernel(
    own, far_column, near_column, narrow, widen, grow, double, expand,
    xo, bo, casto, spano, heighto, diago, relaxo,
    xe, be, caste, spane, heighte, diage, relaxe,
    x1, b1, cast1, span1, height1, relax1,
    solution_out, residual_out, tiles, pairs, wide2, padded2, wide1, wide_own, wide_edge, results, sems,
):
    count = own.shape[0]
    rows = 4 * count
    part_lane = iota((rows, 128), 1) // 32
    index = lax.axis_index("cast")

    fields = []
    for part in range(2):
        for d in range(count):
            rows_d = slice(4 * part, 4 * part + 4)
            left, right = by_side("span", near_column[d, rows_d], far_column[d, rows_d])
            for s, block in enumerate((own[d, rows_d], right, left)):
                tiles[s, 4 * d : 4 * d + 4] = block
        own_tile, right, left = tiles[0], shift(tiles[1], 32, 1), shift(tiles[2], -32, 1)
        slabs = []
        for z in range(4):
            both = jnp.where(part_lane == (z + 1) % 4, right, left)
            slabs.append(shift(jnp.where(part_lane == z, own_tile, both), -32 * z, 1))
        fields.append(slabs)
    coeff2, source2 = fields
    level2 = whole_level(coeff2, source2)
    x2 = level2.sweep(level2.start())
    remains = level2.residual(x2)

    gathered = []
    for field in (coeff2, remains):
        for k in range(2):
            gathered.append(pair_rows(field[2 * k] + field[2 * k + 1], pairs))
    merged = product(jnp.concatenate(gathered, axis=0), narrow[...])
    half = rows // 2
    lane3 = iota((half, 128), 1)
    known = (lane3 < 32) | (lane3 >= 112)
    coeff3 = [jnp.where(known, 0.125 * merged[half * k : half * (k + 1)], 1.0) for k in range(2)]
    source3 = [0.5 * merged[half * (2 + k) : half * (3 + k)] for k in range(2)]
    level3 = whole_level(coeff3, source3)
    x3 = level3.solve(SWEEPS_COARSE - 1)

    spread = product(jnp.concatenate(x3, axis=0), widen[...])
    for k in range(2):
        wide2[k, pl.ds(0, half, stride=2), :] = spread[half * k : half * (k + 1)]
        wide2[k, pl.ds(1, half, stride=2), :] = spread[half * k : half * (k + 1)]
    x2 = [x2[z] + wide2[z // 2] for z in range(4)]
    x2 = level2.sweep(level2.sweep(x2))

    for z in range(4):
        padded2[z, 0:8] = jnp.zeros((8, 128), F32)
        padded2[z, 8 : 8 + rows] = x2[z]
        padded2[z, 8 + rows : 16 + rows] = jnp.zeros((8, 128), F32)
    local = [shift(padded2[z, pl.ds(4 * index + 6, 8), :], -2, 0) for z in range(4)]
    spread = product(jnp.concatenate(local, axis=0), grow[...])
    for z in range(4):
        for s in range(2):
            wide1[z, pl.ds(s, 8, stride=2), :] = spread[8 * z : 8 * z + 8]
    level1 = Level(cast1, span1, height1, None, relax1, b1, 8)
    x = [x1[z] + wide1[z // 2] for z in range(8)]
    x = level1.sweep(level1.sweep(x))

    spread = product(jnp.concatenate(x, axis=0), double[...])
    for z in range(8):
        for s in range(2):
            wide_own[z, pl.ds(s, KEPT1, stride=2), :] = spread[KEPT1 * z : KEPT1 * (z + 1)]
    sides = [jnp.concatenate([x[k], x[k + 4]], axis=1) for k in range(4)]
    spread = product(jnp.concatenate(sides, axis=0), expand[...])
    for k in range(4):
        for s in range(2):
            wide_edge[k, pl.ds(s, KEPT1, stride=2), :] = spread[KEPT1 * k : KEPT1 * (k + 1)]
    level_own = Level(casto, spano, heighto, diago, relaxo, bo, HZ)
    level_edge = Level(caste, spane, heighte, diage, relaxe, be, PACK, 2)

    def refined(wide, k):
        edge = jnp.where(iota((8, BS), 0) < 4, wide[k, BC : BC + 8], wide[k, BC + 8 :])
        return jnp.concatenate([wide[k, :BC], edge], axis=0)

    own_wide = [refined(wide_own, k) for k in range(8)]
    edge_wide = [refined(wide_edge, k) for k in range(4)]
    own_x = [xo[z] + own_wide[z // 2] for z in range(HZ)]
    edge_x = [xe[k] + edge_wide[k // 2] for k in range(PACK)]
    edge_x = level_edge.sweep(level_edge.sweep(edge_x))
    own_x = level_own.sweep(level_own.sweep(own_x))
    lane = iota((BC, BS), 1)
    rows = slice(0, BC)

    copies = []

    beside = lane % 64 < 16

    def joined(side):
        return jnp.where(beside, shift(side[rows], -32, 1), side[rows])

    def give(number, out, z, mid, side):
        value = shift(side, -16 - 64 * (z // PACK), 1)
        results[number, z] = jnp.where((lane < 8) | (lane >= 120), value, mid[rows])
        if z % 4 == 3:
            quarter = pl.ds(z - 3, 4)
            copy = pltpu.make_async_copy(results.at[number, quarter], out.at[quarter], sems.at[number, z // 4])
            copy.start()
            copies.append(copy)

    sides = [joined(value) for value in edge_x]
    for z in range(HZ):
        give(0, solution_out, z, own_x[z], sides[z % PACK])
    edge_r = level_edge.residual(edge_x)
    own_r = level_own.residual(own_x)
    sides = [joined(value) for value in edge_r]
    for z in range(HZ):
        give(1, residual_out, z, own_r[z], sides[z % PACK])
    for copy in copies:
        copy.wait()


VMEM = pl.BlockSpec(memory_space=pltpu.VMEM)
HBM = pl.BlockSpec(memory_space=pltpu.HBM)
PARAMS = pltpu.CompilerParams(vmem_limit_bytes=16 * 1024 * 1024)
INTERPRET = False


def call(kernel, in_specs, outs, scratch=(), out_spec=VMEM):
    return pl.pallas_call(
        kernel,
        in_specs=in_specs,
        out_specs=[out_spec] * len(outs),
        out_shape=[jax.ShapeDtypeStruct(s, F32) if isinstance(s, tuple) else s for s in outs],
        scratch_shapes=[pltpu.VMEM(s, F32) if isinstance(s, tuple) else s for s in scratch],
        compiler_params=PARAMS,
        interpret=INTERPRET,
    )


def swap(value, axis, far):
    size = lax.axis_size(axis)
    partner = [(((i - 1) ^ 1) + 1) % size if far else i ^ 1 for i in range(size)]
    return lax.ppermute(value, axis, list(enumerate(partner)))


def shards(phase, viscosity_table, pressure_source):
    count = lax.axis_size("cast")
    packed = (2, 2, SENT, BS)
    own_state = [(HZ, KEPT, BS)] * 4 + [(HZ + 1, KEPT, BS)] + [(HZ, KEPT, BS)] * 2
    edge_state = [(PACK, KEPT, BS)] * 4 + [(PACK + 1, KEPT, BS)] + [(PACK, KEPT, BS)] * 2
    level1_state = [(8, KEPT1, BS)] * 4 + [(9, KEPT1, BS), (8, KEPT1, BS)]

    arguments = (pltpu.with_memory_space_constraint(a, pltpu.HBM) for a in (viscosity_table, phase, pressure_source))
    stage_scratch = [pltpu.SMEM((3,), F32), pltpu.VMEM((HZ, BC, BS), jnp.int32), pltpu.SemaphoreType.DMA((3,))]
    own, far_cast, near_cast = call(
        stage_kernel, [HBM] * 3, [(2, HZ, BC, BS), (CAST_ROWS, BS), (CAST_ROWS, BS)], stage_scratch
    )(*arguments)
    far_cast = swap(far_cast, "cast", True)
    near_cast = swap(near_cast, "cast", False)
    square = (BS, BS)
    tables = [square, square, (BS, 2 * BS), (BS, 4 * BS), (4 * BS, BS), square, square, square, square, (2 * BS, BS)]
    tables = [jax.ShapeDtypeStruct(t, BF16) for t in tables]
    near_own, far_own, own_merge, mid_merge, edge_merge, slot_merge, move, *spreads = call(
        prepare_kernel, [VMEM], [(2, 2, BC, BS)] * 2 + tables
    )(own)
    near_span, far_span = call(margin_kernel, [VMEM] * 4, [packed, packed])(near_own, far_own, far_cast, near_cast)
    near_span = swap(near_span, "span", False)
    far_span = swap(far_span, "span", True)
    *kept_own, merged, merged_mid, inner, inner4 = call(
        own_kernel,
        [VMEM] * 5,
        own_state + [(HZ, HALF, BS), (HZ, HALF - 8, BS), (2, PACK, ROWS, BS), (2, 4, SENT, BS)],
        [(HZ, ROWS, BS)],
    )(own, far_cast, near_cast, own_merge, mid_merge)
    (slots,) = call(
        edge_kernel, [VMEM] * 6, [(count, 8, BS)], [(4, SENT, BS), (4, 16, BS)]
    )(near_span, far_span, inner4, merged_mid, slot_merge, move)
    kept_edge = call(state_kernel, [VMEM] * 5, edge_state + level1_state, [(8, ROWS, BS)])(
        near_span, far_span, inner, merged, edge_merge
    )

    column = lax.all_to_all(slots, "cast", 0, 0)
    near_column = swap(column, "span", False)
    far_column = swap(column, "span", True)
    rows = 4 * count
    scratch = [
        (3, rows, BS),
        (rows, BS),
        (2, rows, BS),
        (4, rows + 16, BS),
        (4, KEPT1, BS),
        (8, 2 * KEPT1, BS),
        (4, 2 * KEPT1, BS),
        (2, HZ, BC, BS),
        pltpu.SemaphoreType.DMA((2, 4)),
    ]
    state = spreads + kept_own + list(kept_edge)
    return tuple(
        call(ascent_kernel, [VMEM] * (3 + len(state)), [(HZ, BC, BS)] * 2, scratch, HBM)(
            column, far_column, near_column, *state
        )
    )


def solution(mesh):
    blocks = P(None, "cast", "span")
    return jax.shard_map(
        shards,
        mesh=mesh,
        in_specs=(blocks, P(), blocks),
        out_specs=(blocks, blocks),
        check_vma=False,
    )
```

```python
import jax
import jax.numpy as jnp
from jax import lax
from jax.experimental import pallas as pl
from jax.experimental.pallas import tpu as pltpu
from jax.sharding import PartitionSpec as P

HZ, BC, BS = 16, 16, 128
HALO = 16
ROWS = BC + 2 * HALO
HALF = ROWS // 2
KEPT = BC + 8
KEPT1 = HALF - 8
SENT = BC + 16
REACH = (13, 12)
BASE = (0, REACH[0] * HZ)
CAST_ROWS = sum(REACH) * HZ
PACK = HZ // 2
SWEEPS_COARSE = 8
WEIGHT = 0.8
F32 = jnp.float32
BF16 = jnp.bfloat16


def shift(x, step, axis):
    if step == 0:
        return x
    return pltpu.roll(x, step % x.shape[axis], axis)


def iota(shape, axis):
    return lax.broadcasted_iota(jnp.int32, shape, axis)


def product(a, b):
    high = a.astype(BF16)
    low = (a - high.astype(F32)).astype(BF16)
    return jnp.dot(high, b, preferred_element_type=F32) + jnp.dot(low, b, preferred_element_type=F32)


def harmonic(a, b):
    return 2.0 * a * b / (a + b)


def near(x, below, above, cast, span, low, high):
    return (
        cast * shift(x, 1, 0)
        + shift(cast * x, -1, 0)
        + span * shift(x, 1, 1)
        + shift(span * x, -1, 1)
        + low * below
        + high * above
    )


def diagonal_of(cast, span, low, high):
    return cast + shift(cast, -1, 0) + span + shift(span, -1, 1) + low + high


class Level:
    def __init__(self, cast, span, height, diag, relax, source, depth, packed=1):
        self.cast, self.span, self.height = cast, span, height
        self.diag, self.relax, self.source = diag, relax, source
        self.depth, self.packed = depth, packed

    def near(self, x, z):
        last = self.depth - 1
        below, above = x[max(z - 1, 0)], x[min(z + 1, last)]
        if self.packed > 1 and z == 0:
            below = shift(x[last], BS // self.packed, 1)
        if self.packed > 1 and z == last:
            above = shift(x[0], -(BS // self.packed), 1)
        return near(x[z], below, above, self.cast[z], self.span[z], self.height[z], self.height[z + 1])

    def start(self):
        return [self.relax[z] * self.source[z] for z in range(self.depth)]

    def sweep(self, x):
        return [
            (1.0 - WEIGHT) * x[z] + self.relax[z] * (self.near(x, z) + self.source[z])
            for z in range(self.depth)
        ]

    def solve(self, sweeps):
        part = [
            (
                relax * self.cast[z],
                relax * shift(self.cast[z], -1, 0),
                relax * self.span[z],
                relax * shift(self.span[z], -1, 1),
                relax * self.height[1],
            )
            for z, relax in enumerate(self.relax)
        ]
        first = x = self.start()
        for _ in range(sweeps):
            x = [
                ((1.0 - WEIGHT) * x[z] + first[z] + part[z][4] * x[1 - z])
                + (part[z][0] * shift(x[z], 1, 0) + part[z][1] * shift(x[z], -1, 0))
                + (part[z][2] * shift(x[z], 1, 1) + part[z][3] * shift(x[z], -1, 1))
                for z in range(2)
            ]
        return x

    def residual_at(self, x, z):
        return self.source[z] - self.diag[z] * x[z] + self.near(x, z)

    def residual(self, x):
        return [self.residual_at(x, z) for z in range(self.depth)]


def fine_level(visc, source, outside, packed):
    depth = len(visc)
    shape = visc[0].shape
    weight = jnp.where(outside, 0.0, WEIGHT)
    cast = [2.0 / (v + shift(v, 1, 0)) for v in visc]
    span = [2.0 / (v + shift(v, 1, 1)) for v in visc]
    inner = [2.0 / (a + b) for a, b in zip(visc[:-1], visc[1:])]
    if packed > 1:
        width = BS // packed
        bottom = jnp.where(iota(shape, 1) < width, 0.0, 2.0 / (visc[0] + shift(visc[-1], width, 1)))
        top = shift(bottom, -width, 1)
    else:
        bottom = top = jnp.zeros(shape, F32)
    height = [bottom] + inner + [top]
    diag = [diagonal_of(cast[z], span[z], height[z], height[z + 1]) for z in range(depth)]
    relax = [weight / d for d in diag]
    return Level(cast, span, height, diag, relax, source, depth, packed)


def kept_rows(value):
    edge = jnp.where(iota((8, BS), 0) < 4, value[HALO + BC : HALO + BC + 8], value[HALO - 8 : HALO])
    return jnp.concatenate([value[HALO : HALO + BC], edge], axis=0)


def kept_rows1(value):
    return jnp.concatenate([value[8:16], jnp.where(iota((8, BS), 0) < 4, value[16:], value[:8])], axis=0)


def keep(level, x, refs):
    for ref, values in zip(refs, (x, level.source, level.cast, level.span, level.height, level.diag, level.relax)):
        for z, value in enumerate(values):
            ref[z] = kept_rows(value)


def coarse_parts(visc, remains, scratch):
    parts = []
    count = len(visc) // 2
    half = visc[0].shape[0] // 2
    for a, values in enumerate(([1.0 / v for v in visc], remains)):
        for k in range(count):
            scratch[a * count + k] = values[2 * k] + values[2 * k + 1]
            ref = scratch.at[a * count + k]
            parts.append(ref[pl.ds(0, half, stride=2), :] + ref[pl.ds(1, half, stride=2), :])
    return jnp.concatenate(parts, axis=0)


def ends(value, first, last, edge):
    rows = value.shape[0]
    row = iota((rows, BS), 0)
    value = jnp.where(first & (row < edge), jnp.broadcast_to(value[edge : edge + 1], (rows, BS)), value)
    stop = rows - edge
    return jnp.where(last & (row >= stop), jnp.broadcast_to(value[stop - 1 : stop], (rows, BS)), value)


def beyond(rows, edge):
    row = iota((rows, BS), 0)
    index = lax.axis_index("cast")
    first, last = index == 0, index == lax.axis_size("cast") - 1
    return first, last, (first & (row < edge)) | (last & (row >= rows - edge))


def height_faces(coeff):
    flat = jnp.zeros_like(coeff[0])
    inner = [harmonic(a, b) for a, b in zip(coeff[:-1], coeff[1:])]
    return [flat] + inner + [flat]


def whole_level(coeff, source):
    shape = coeff[0].shape
    row = iota(shape, 0)
    height = height_faces(coeff)
    cast, span, diag, relax = [], [], [], []
    for z, c in enumerate(coeff):
        lower = jnp.where(row == 0, 0.0, harmonic(shift(c, 1, 0), c))
        ends = jnp.where((row == 0) | (row == shape[0] - 1), c, 0.0)
        side = harmonic(shift(c, 1, 1), c)
        total = diagonal_of(lower, side, height[z], height[z + 1]) + ends
        cast.append(lower)
        span.append(side)
        diag.append(total)
        relax.append(WEIGHT / total)
    return Level(cast, span, height, diag, relax, source, len(coeff))


def pair_rows(value, scratch):
    rows = value.shape[0]
    scratch[...] = value
    return scratch[pl.ds(0, rows // 2, stride=2), :] + scratch[pl.ds(1, rows // 2, stride=2), :]


def by_side(axis, near_pair, far_pair):
    even = lax.rem(lax.axis_index(axis), 2) == 0
    return jnp.where(even, far_pair, near_pair), jnp.where(even, near_pair, far_pair)


def beyond_rows(near_cast, far_cast, a, z):
    reach, base = REACH[a], BASE[a]
    start = base + reach * z

    stop = base + reach * HZ
    even = lax.rem(lax.axis_index("cast"), 2) == 0

    def window(first, one, other):
        at = min(max(first, base), stop - HALO)
        rows = slice(at, at + HALO)
        return shift(jnp.where(even, one[rows], other[rows]), at - first, 0)

    return window(start - (HALO - reach), far_cast, near_cast), window(start, near_cast, far_cast)


def extended(own, near_cast, far_cast, a, z):
    before, after = beyond_rows(near_cast, far_cast, a, z)
    return jnp.concatenate([before, own[a, z], after], axis=0)


def stage_kernel(table_in, phase_in, source_in, out, far_out, near_out, table, phase, sems):
    even = lax.rem(lax.axis_index("cast"), 2) == 0

    def put(a, z, value):
        reach = REACH[a]
        first, last = value, shift(value, reach - HALO, 0)
        rows = HALO if a == 0 or z < HZ - 1 else reach
        place = slice(BASE[a] + reach * z, BASE[a] + reach * z + rows)
        near_out[place] = jnp.where(even, last, first)[:rows]
        far_out[place] = jnp.where(even, first, last)[:rows]

    copies = [
        pltpu.make_async_copy(table_in, table, sems.at[0]),
        pltpu.make_async_copy(phase_in.at[pl.ds(0, 8)], phase.at[pl.ds(0, 8)], sems.at[1]),
        pltpu.make_async_copy(phase_in.at[pl.ds(8, 8)], phase.at[pl.ds(8, 8)], sems.at[2]),
        pltpu.make_async_copy(source_in, out.at[1], sems.at[3]),
    ]
    for copy in copies:
        copy.start()
    copies[0].wait()
    copies[1].wait()
    for z in range(HZ):
        if z == 8:
            copies[2].wait()
        p = phase[z]
        value = jnp.where(p == 0, table[0], jnp.where(p == 1, table[1], table[2]))
        out[0, z] = value
        put(0, z, value)
    copies[3].wait()
    for z in range(HZ):
        put(1, z, out[1, z])


def ones(where):
    return jnp.where(where, 1.0, 0.0).astype(BF16)


def prepare_kernel(own, near_own, far_own, own_merge, mid_merge, edge_merge, slot_merge, move, narrow, widen, grow, double, expand):
    lane = iota((BC, BS), 1)
    for a in range(2):
        for group in range(2):
            head = tail = None
            for start, z in places(group):
                h, t = shift(own[a, z], start, 1), shift(own[a, z], start + HALO, 1)
                inside = (lane >= start) & (lane < start + HALO)
                head = h if head is None else jnp.where(inside, h, head)
                tail = t if tail is None else jnp.where(inside, t, tail)
            far_own[a, group], near_own[a, group] = by_side("span", tail, head)
    i, j = iota((BS, BS), 0), iota((BS, BS), 1)
    own_merge[...] = ones((i // 2 == j) & (i >= 8) & (i < 120))
    mid_merge[...] = ones((i // 2 == j) & (i >= 4) & (i < 124))
    narrow[...] = ones(((i < 64) & (i // 2 == j)) | ((i >= 96) & (i // 2 + 64 == j)))
    widen[...] = ones(((j < 64) & (j // 2 == i)) | ((j >= 96) & (j // 2 + 64 == i)))
    grow[...] = ones(((j < 96) & (j // 2 == i)) | ((j >= 96) & (j // 2 + 64 == i)))
    double[...] = ones(j // 2 == i)
    i, j = iota((BS, 2 * BS), 0), iota((BS, 2 * BS), 1)
    m = i % 64
    target = jnp.where(m < 24, (m // 2 + 120) % BS, m // 2 + 40)
    edge_merge[...] = ones(((m < 24) | (m >= 40)) & (target == j % BS) & (i // 64 == j // BS))
    i, j = iota((BS, 4 * BS), 0), iota((BS, 4 * BS), 1)
    m = i % 32
    target = jnp.where(m < 12, (m // 2 + 124) % BS, m // 2 + 52)
    slot_merge[...] = ones(((m < 12) | (m >= 20)) & (target == j % BS) & (i // 32 == j // BS))
    i, j = iota((4 * BS, BS), 0), iota((4 * BS, BS), 1)
    move[...] = ones((i % BS < 64) & (i % BS // 2 + 32 * (i // BS) == j))
    i, j = iota((2 * BS, BS), 0), iota((2 * BS, BS), 1)
    m = j % 64
    origin = jnp.where(m < 32, (m // 2 + 120) % BS, m // 2 + 40)
    expand[...] = ones((origin == i % BS) & (i // BS == j // 64))


def places(group):
    return [(16 * sub + 32 * g, group * 2 + sub + 4 * g) for sub in range(2) for g in range(4)]


def margin_kernel(near_own, far_own, far_cast, near_cast, near_span, far_span):
    lane = iota((16, BS), 1)
    seg = lane % HALO
    for a in range(2):
        for group in range(2):
            head = tail = None
            for start, z in places(group):
                before, after = beyond_rows(near_cast, far_cast, a, z)
                inner = jnp.concatenate([before[8:], after[:8]], axis=0)
                far = jnp.concatenate([before[:8], after[8:]], axis=0)
                h = jnp.where(seg >= 12, shift(far, start + 12, 1), shift(inner, start, 1))
                t = jnp.where(seg < 4, shift(far, start + HALO - 12, 1), shift(inner, start + HALO, 1))
                inside = (lane >= start) & (lane < start + HALO)
                head = h if head is None else jnp.where(inside, h, head)
                tail = t if tail is None else jnp.where(inside, t, tail)
            sides = by_side("span", tail, head)
            for out, packed, value in ((far_span, far_own, sides[0]), (near_span, near_own, sides[1])):
                out[a, group, :8] = value[:8]
                out[a, group, 8:24] = packed[a, group]
                out[a, group, 24:] = value[8:]


def spread_rows(sent, step, more):
    moved = shift(sent, step, 1)
    return jnp.concatenate([shift(sent[:8], step + more, 1), moved, shift(sent[-8:], step + more, 1)], axis=0)


def own_kernel(own, far_cast, near_cast, own_merge, mid_merge, x, b, cast, span, height, diag, relax, merged, merged_mid, inner, inner4, scratch):
    first, last, outside = beyond(ROWS, HALO)
    visc, source = [], []
    for z in range(HZ):
        v, s = (extended(own, near_cast, far_cast, a, z) for a in range(2))
        visc.append(ends(v, first, last, HALO))
        source.append(s)
    lane = iota((ROWS, BS), 1)
    for a, field in enumerate((visc, source)):
        for k in range(PACK):
            low, high = field[k], field[k + PACK]
            inner[a, k] = jnp.where(
                lane < 32,
                shift(low, 16, 1),
                jnp.where(lane < 64, shift(low, 48, 1), jnp.where(lane < 96, shift(high, 80, 1), shift(high, 112, 1))),
            )
        quarter = lane[8 : ROWS - 8]
        for k in range(4):
            value = None
            for g in range(4):
                slab = field[k + 4 * g][8 : ROWS - 8]
                edges = jnp.where(quarter % 32 < 16, shift(slab, 32 * g + 8, 1), shift(slab, 32 * g - 104, 1))
                value = edges if value is None else jnp.where(quarter // 32 == g, edges, value)
            inner4[a, k] = value
    level = fine_level(visc, source, outside, 1)
    values = level.sweep(level.start())
    keep(level, values, (x, b, cast, span, height, diag, relax))
    parts = coarse_parts(visc, level.residual(values), scratch)
    total = product(parts, own_merge[...])
    for k in range(HZ):
        merged[k] = total[HALF * k : HALF * (k + 1)]
    total = product(parts, mid_merge[...])
    for k in range(HZ):
        merged_mid[k] = total[HALF * k + 4 : HALF * (k + 1) - 4]


def edge_levels(near_span, far_span, inner, merged, edge_merge, scratch, halo):
    rows = BC + 2 * halo
    first, last, outside = beyond(rows, halo)
    wide = halo == HALO
    packed = 2 if wide else 4
    lane = iota((rows, BS), 1) % (BS // packed)
    fields = []
    for a in range(2):
        slabs = []
        for k in range(HZ // packed):
            group, offset = k % 4 // 2, 16 * (k % 2) + 32 * (k // 4)
            left, right = by_side("span", near_span[a, group], far_span[a, group])
            if wide:
                l, r = spread_rows(left, -offset, 12), spread_rows(right, 48 - offset, -12)
                value = jnp.where(lane < 16, l, jnp.where(lane >= 48, r, inner[a, k]))
            else:
                l, r = shift(left, -offset - 8, 1), shift(right, 24 - offset, 1)
                value = jnp.where(lane < 8, l, jnp.where(lane >= 24, r, inner[a, k]))
            slabs.append(ends(value, first, last, halo) if a == 0 else value)
        fields.append(slabs)
    visc, source = fields
    level = fine_level(visc, source, outside, packed)
    values = level.sweep(level.start())
    fine = level, values
    parts = coarse_parts(visc, level.residual(values), scratch)
    total = product(parts, edge_merge[...])

    edge, half = halo // 2, rows // 2
    first, last, outside = beyond(half, edge)
    weight = jnp.where(outside, 0.0, WEIGHT)
    coarse = []
    for k in range(HZ):
        a, z = divmod(k, 8)
        side, pos = divmod(z, 4 if wide else 2)
        row = half * (HZ // packed // 2 * a + pos)
        coarse.append(merged[k] + total[row : row + half, BS * side : BS * (side + 1)])
    lane = iota((half, BS), 1)
    known = (lane < BS // 2 + edge) | (lane >= BS - edge)
    coeff = [jnp.where(known, 0.125 * ends(c, first, last, edge), 1.0) for c in coarse[:8]]
    source = [0.5 * c for c in coarse[8:]]
    height = height_faces(coeff)
    cast_faces = [harmonic(shift(c, 1, 0), c) for c in coeff]
    span_faces = [harmonic(shift(c, 1, 1), c) for c in coeff]
    diagonal = [diagonal_of(cast_faces[z], span_faces[z], height[z], height[z + 1]) for z in range(8)]
    level = Level(cast_faces, span_faces, height, diagonal, [weight / d for d in diagonal], source, 8)
    return fine, (level, level.sweep(level.start()), coeff)


def state_kernel(
    near_span, far_span, inner, merged, edge_merge, x, b, cast, span, height, diag, relax,
    x1, b1, cast1, span1, height1, relax1, scratch,
):
    fine, (level, values, _) = edge_levels(near_span, far_span, inner, merged, edge_merge, scratch, HALO)
    keep(*fine, (x, b, cast, span, height, diag, relax))
    kept = (x1, values), (b1, level.source), (cast1, level.cast), (span1, level.span), (height1, level.height), (relax1, level.relax)
    for ref, items in kept:
        for z, item in enumerate(items):
            ref[z] = kept_rows1(item)


def edge_kernel(near_span, far_span, inner, merged, edge_merge, move, slots, scratch, rows8):
    _, (level, values, coeff) = edge_levels(near_span, far_span, inner, merged, edge_merge, scratch, 8)
    remains = level.residual(values)
    edge = 4

    fields = []
    for k in range(4):
        rows = slice(edge, edge + 8)
        c = coeff[2 * k][rows] + coeff[2 * k + 1][rows]
        r = remains[2 * k][rows] + remains[2 * k + 1][rows]
        rows8[k] = jnp.concatenate([0.125 * c, 0.5 * r], axis=0)
        fields.append(rows8[k, pl.ds(0, 8, stride=2), :] + rows8[k, pl.ds(1, 8, stride=2), :])
    total = product(jnp.concatenate(fields, axis=1), move[...])
    for d in range(slots.shape[0]):
        slots[d] = total


def ascent_kernel(
    own, far_column, near_column, narrow, widen, grow, double, expand,
    xo, bo, casto, spano, heighto, diago, relaxo,
    xe, be, caste, spane, heighte, diage, relaxe,
    x1, b1, cast1, span1, height1, relax1,
    solution_out, residual_out, tiles, pairs, wide2, padded2, wide1, wide_own, wide_edge, results, sems,
):
    count = own.shape[0]
    rows = 4 * count
    part_lane = iota((rows, 128), 1) // 32
    index = lax.axis_index("cast")

    fields = []
    for part in range(2):
        for d in range(count):
            rows_d = slice(4 * part, 4 * part + 4)
            left, right = by_side("span", near_column[d, rows_d], far_column[d, rows_d])
            for s, block in enumerate((own[d, rows_d], right, left)):
                tiles[s, 4 * d : 4 * d + 4] = block
        own_tile, right, left = tiles[0], shift(tiles[1], 32, 1), shift(tiles[2], -32, 1)
        slabs = []
        for z in range(4):
            both = jnp.where(part_lane == (z + 1) % 4, right, left)
            slabs.append(shift(jnp.where(part_lane == z, own_tile, both), -32 * z, 1))
        fields.append(slabs)
    coeff2, source2 = fields
    level2 = whole_level(coeff2, source2)
    x2 = level2.sweep(level2.start())
    remains = level2.residual(x2)

    gathered = []
    for field in (coeff2, remains):
        for k in range(2):
            gathered.append(pair_rows(field[2 * k] + field[2 * k + 1], pairs))
    merged = product(jnp.concatenate(gathered, axis=0), narrow[...])
    half = rows // 2
    lane3 = iota((half, 128), 1)
    known = (lane3 < 32) | (lane3 >= 112)
    coeff3 = [jnp.where(known, 0.125 * merged[half * k : half * (k + 1)], 1.0) for k in range(2)]
    source3 = [0.5 * merged[half * (2 + k) : half * (3 + k)] for k in range(2)]
    level3 = whole_level(coeff3, source3)
    x3 = level3.solve(SWEEPS_COARSE - 1)

    spread = product(jnp.concatenate(x3, axis=0), widen[...])
    for k in range(2):
        wide2[k, pl.ds(0, half, stride=2), :] = spread[half * k : half * (k + 1)]
        wide2[k, pl.ds(1, half, stride=2), :] = spread[half * k : half * (k + 1)]
    x2 = [x2[z] + wide2[z // 2] for z in range(4)]
    x2 = level2.sweep(level2.sweep(x2))

    for z in range(4):
        padded2[z, 0:8] = jnp.zeros((8, 128), F32)
        padded2[z, 8 : 8 + rows] = x2[z]
        padded2[z, 8 + rows : 16 + rows] = jnp.zeros((8, 128), F32)
    local = [shift(padded2[z, pl.ds(4 * index + 6, 8), :], -2, 0) for z in range(4)]
    spread = product(jnp.concatenate(local, axis=0), grow[...])
    for z in range(4):
        for s in range(2):
            wide1[z, pl.ds(s, 8, stride=2), :] = spread[8 * z : 8 * z + 8]
    level1 = Level(cast1, span1, height1, None, relax1, b1, 8)
    x = [x1[z] + wide1[z // 2] for z in range(8)]
    x = level1.sweep(level1.sweep(x))

    spread = product(jnp.concatenate(x, axis=0), double[...])
    for z in range(8):
        for s in range(2):
            wide_own[z, pl.ds(s, KEPT1, stride=2), :] = spread[KEPT1 * z : KEPT1 * (z + 1)]
    sides = [jnp.concatenate([x[k], x[k + 4]], axis=1) for k in range(4)]
    spread = product(jnp.concatenate(sides, axis=0), expand[...])
    for k in range(4):
        for s in range(2):
            wide_edge[k, pl.ds(s, KEPT1, stride=2), :] = spread[KEPT1 * k : KEPT1 * (k + 1)]
    level_own = Level(casto, spano, heighto, diago, relaxo, bo, HZ)
    level_edge = Level(caste, spane, heighte, diage, relaxe, be, PACK, 2)

    def refined(wide, k):
        edge = jnp.where(iota((8, BS), 0) < 4, wide[k, BC : BC + 8], wide[k, BC + 8 :])
        return jnp.concatenate([wide[k, :BC], edge], axis=0)

    own_wide = [refined(wide_own, k) for k in range(8)]
    edge_wide = [refined(wide_edge, k) for k in range(4)]
    own_x = [xo[z] + own_wide[z // 2] for z in range(HZ)]
    edge_x = [xe[k] + edge_wide[k // 2] for k in range(PACK)]
    edge_x = level_edge.sweep(level_edge.sweep(edge_x))
    own_x = level_own.sweep(level_own.sweep(own_x))
    lane = iota((BC, BS), 1)
    rows = slice(0, BC)

    copies = []

    beside = lane % 64 < 16

    def joined(side):
        return jnp.where(beside, shift(side[rows], -32, 1), side[rows])

    def give(number, out, z, mid, side):
        value = shift(side, -16 - 64 * (z // PACK), 1)
        results[number, z] = jnp.where((lane < 8) | (lane >= 120), value, mid[rows])
        if z % 4 == 3:
            quarter = pl.ds(z - 3, 4)
            copy = pltpu.make_async_copy(results.at[number, quarter], out.at[quarter], sems.at[number, z // 4])
            copy.start()
            copies.append(copy)

    sides = [joined(value) for value in edge_x]
    for z in range(HZ):
        give(0, solution_out, z, own_x[z], sides[z % PACK])
    sides = [joined(value) for value in level_edge.residual(edge_x)]
    for z in range(HZ):
        give(1, residual_out, z, level_own.residual_at(own_x, z), sides[z % PACK])
    for copy in copies:
        copy.wait()


VMEM = pl.BlockSpec(memory_space=pltpu.VMEM)
HBM = pl.BlockSpec(memory_space=pltpu.HBM)
PARAMS = pltpu.CompilerParams(vmem_limit_bytes=16 * 1024 * 1024)
INTERPRET = False


def call(kernel, in_specs, outs, scratch=(), out_spec=VMEM):
    return pl.pallas_call(
        kernel,
        in_specs=in_specs,
        out_specs=[out_spec] * len(outs),
        out_shape=[jax.ShapeDtypeStruct(s, F32) if isinstance(s, tuple) else s for s in outs],
        scratch_shapes=[pltpu.VMEM(s, F32) if isinstance(s, tuple) else s for s in scratch],
        compiler_params=PARAMS,
        interpret=INTERPRET,
    )


def swap(value, axis, far):
    size = lax.axis_size(axis)
    partner = [(((i - 1) ^ 1) + 1) % size if far else i ^ 1 for i in range(size)]
    return lax.ppermute(value, axis, list(enumerate(partner)))


def shards(phase, viscosity_table, pressure_source):
    count = lax.axis_size("cast")
    packed = (2, 2, SENT, BS)
    own_state = [(HZ, KEPT, BS)] * 4 + [(HZ + 1, KEPT, BS)] + [(HZ, KEPT, BS)] * 2
    edge_state = [(PACK, KEPT, BS)] * 4 + [(PACK + 1, KEPT, BS)] + [(PACK, KEPT, BS)] * 2
    level1_state = [(8, KEPT1, BS)] * 4 + [(9, KEPT1, BS), (8, KEPT1, BS)]

    arguments = (pltpu.with_memory_space_constraint(a, pltpu.HBM) for a in (viscosity_table, phase, pressure_source))
    stage_scratch = [pltpu.SMEM((3,), F32), pltpu.VMEM((HZ, BC, BS), jnp.int32), pltpu.SemaphoreType.DMA((4,))]
    own, far_cast, near_cast = call(
        stage_kernel, [HBM] * 3, [(2, HZ, BC, BS), (CAST_ROWS, BS), (CAST_ROWS, BS)], stage_scratch
    )(*arguments)
    far_cast = swap(far_cast, "cast", True)
    near_cast = swap(near_cast, "cast", False)
    square = (BS, BS)
    tables = [square, square, (BS, 2 * BS), (BS, 4 * BS), (4 * BS, BS), square, square, square, square, (2 * BS, BS)]
    tables = [jax.ShapeDtypeStruct(t, BF16) for t in tables]
    near_own, far_own, own_merge, mid_merge, edge_merge, slot_merge, move, *spreads = call(
        prepare_kernel, [VMEM], [(2, 2, BC, BS)] * 2 + tables
    )(own)
    near_span, far_span = call(margin_kernel, [VMEM] * 4, [packed, packed])(near_own, far_own, far_cast, near_cast)
    near_span = swap(near_span, "span", False)
    far_span = swap(far_span, "span", True)
    *kept_own, merged, merged_mid, inner, inner4 = call(
        own_kernel,
        [VMEM] * 5,
        own_state + [(HZ, HALF, BS), (HZ, HALF - 8, BS), (2, PACK, ROWS, BS), (2, 4, SENT, BS)],
        [(HZ, ROWS, BS)],
    )(own, far_cast, near_cast, own_merge, mid_merge)
    (slots,) = call(
        edge_kernel, [VMEM] * 6, [(count, 8, BS)], [(4, SENT, BS), (4, 16, BS)]
    )(near_span, far_span, inner4, merged_mid, slot_merge, move)
    kept_edge = call(state_kernel, [VMEM] * 5, edge_state + level1_state, [(8, ROWS, BS)])(
        near_span, far_span, inner, merged, edge_merge
    )

    column = lax.all_to_all(slots, "cast", 0, 0)
    near_column = swap(column, "span", False)
    far_column = swap(column, "span", True)
    rows = 4 * count
    scratch = [
        (3, rows, BS),
        (rows, BS),
        (2, rows, BS),
        (4, rows + 16, BS),
        (4, KEPT1, BS),
        (8, 2 * KEPT1, BS),
        (4, 2 * KEPT1, BS),
        (2, HZ, BC, BS),
        pltpu.SemaphoreType.DMA((2, 4)),
    ]
    state = spreads + kept_own + list(kept_edge)
    return tuple(
        call(ascent_kernel, [VMEM] * (3 + len(state)), [(HZ, BC, BS)] * 2, scratch, HBM)(
            column, far_column, near_column, *state
        )
    )


def solution(mesh):
    blocks = P(None, "cast", "span")
    return jax.shard_map(
        shards,
        mesh=mesh,
        in_specs=(blocks, P(), blocks),
        out_specs=(blocks, blocks),
        check_vma=False,
    )
```

```python
import jax
import jax.numpy as jnp
from jax import lax
from jax.experimental import pallas as pl
from jax.experimental.pallas import tpu as pltpu
from jax.sharding import PartitionSpec as P

HZ, BC, BS = 16, 16, 128
HALO = 16
ROWS = BC + 2 * HALO
HALF = ROWS // 2
KEPT = BC + 8
KEPT1 = HALF - 8
SENT = BC + 16
REACH = (13, 12)
BASE = (0, REACH[0] * HZ)
CAST_ROWS = sum(REACH) * HZ
PACK = HZ // 2
SWEEPS_COARSE = 8
WEIGHT = 0.8
F32 = jnp.float32
BF16 = jnp.bfloat16


def shift(x, step, axis):
    if step == 0:
        return x
    return pltpu.roll(x, step % x.shape[axis], axis)


def iota(shape, axis):
    return lax.broadcasted_iota(jnp.int32, shape, axis)


def product(a, b):
    high = a.astype(BF16)
    low = (a - high.astype(F32)).astype(BF16)
    parts, twice = jnp.concatenate([high, low], axis=1), jnp.concatenate([b, b], axis=0)
    return jnp.dot(parts, twice, preferred_element_type=F32)


def harmonic(a, b):
    return 2.0 * a * b / (a + b)


def near(x, below, above, cast, span, low, high):
    return (
        cast * shift(x, 1, 0)
        + shift(cast * x, -1, 0)
        + span * shift(x, 1, 1)
        + shift(span * x, -1, 1)
        + low * below
        + high * above
    )


def diagonal_of(cast, span, low, high):
    return cast + shift(cast, -1, 0) + span + shift(span, -1, 1) + low + high


class Level:
    def __init__(self, cast, span, height, diag, relax, source, depth, packed=1):
        self.cast, self.span, self.height = cast, span, height
        self.diag, self.relax, self.source = diag, relax, source
        self.depth, self.packed = depth, packed

    def near(self, x, z):
        last = self.depth - 1
        below, above = x[max(z - 1, 0)], x[min(z + 1, last)]
        if self.packed > 1 and z == 0:
            below = shift(x[last], BS // self.packed, 1)
        if self.packed > 1 and z == last:
            above = shift(x[0], -(BS // self.packed), 1)
        return near(x[z], below, above, self.cast[z], self.span[z], self.height[z], self.height[z + 1])

    def start(self):
        return [self.relax[z] * self.source[z] for z in range(self.depth)]

    def sweep(self, x):
        return [
            (1.0 - WEIGHT) * x[z] + self.relax[z] * (self.near(x, z) + self.source[z])
            for z in range(self.depth)
        ]

    def solve(self, sweeps):
        part = [
            (
                relax * self.cast[z],
                relax * shift(self.cast[z], -1, 0),
                relax * self.span[z],
                relax * shift(self.span[z], -1, 1),
                relax * self.height[1],
            )
            for z, relax in enumerate(self.relax)
        ]
        first = x = self.start()
        for _ in range(sweeps):
            x = [
                ((1.0 - WEIGHT) * x[z] + first[z] + part[z][4] * x[1 - z])
                + (part[z][0] * shift(x[z], 1, 0) + part[z][1] * shift(x[z], -1, 0))
                + (part[z][2] * shift(x[z], 1, 1) + part[z][3] * shift(x[z], -1, 1))
                for z in range(2)
            ]
        return x

    def residual_at(self, x, z):
        return self.source[z] - self.diag[z] * x[z] + self.near(x, z)

    def residual(self, x):
        return [self.residual_at(x, z) for z in range(self.depth)]


def fine_level(visc, source, outside, packed):
    depth = len(visc)
    shape = visc[0].shape
    weight = jnp.where(outside, 0.0, WEIGHT)
    cast = [2.0 / (v + shift(v, 1, 0)) for v in visc]
    span = [2.0 / (v + shift(v, 1, 1)) for v in visc]
    inner = [2.0 / (a + b) for a, b in zip(visc[:-1], visc[1:])]
    if packed > 1:
        width = BS // packed
        bottom = jnp.where(iota(shape, 1) < width, 0.0, 2.0 / (visc[0] + shift(visc[-1], width, 1)))
        top = shift(bottom, -width, 1)
    else:
        bottom = top = jnp.zeros(shape, F32)
    height = [bottom] + inner + [top]
    diag = [diagonal_of(cast[z], span[z], height[z], height[z + 1]) for z in range(depth)]
    relax = [weight / d for d in diag]
    return Level(cast, span, height, diag, relax, source, depth, packed)


def kept_rows(value):
    edge = jnp.where(iota((8, BS), 0) < 4, value[HALO + BC : HALO + BC + 8], value[HALO - 8 : HALO])
    return jnp.concatenate([value[HALO : HALO + BC], edge], axis=0)


def kept_rows1(value):
    return jnp.concatenate([value[8:16], jnp.where(iota((8, BS), 0) < 4, value[16:], value[:8])], axis=0)


def keep(level, x, refs):
    for ref, values in zip(refs, (x, level.source, level.cast, level.span, level.height, level.diag, level.relax)):
        for z, value in enumerate(values):
            ref[z] = kept_rows(value)


def coarse_parts(visc, remains, scratch):
    parts = []
    count = len(visc) // 2
    half = visc[0].shape[0] // 2
    for a, values in enumerate(([1.0 / v for v in visc], remains)):
        for k in range(count):
            scratch[a * count + k] = values[2 * k] + values[2 * k + 1]
            ref = scratch.at[a * count + k]
            parts.append(ref[pl.ds(0, half, stride=2), :] + ref[pl.ds(1, half, stride=2), :])
    return jnp.concatenate(parts, axis=0)


def ends(value, first, last, edge):
    rows = value.shape[0]
    row = iota((rows, BS), 0)
    value = jnp.where(first & (row < edge), jnp.broadcast_to(value[edge : edge + 1], (rows, BS)), value)
    stop = rows - edge
    return jnp.where(last & (row >= stop), jnp.broadcast_to(value[stop - 1 : stop], (rows, BS)), value)


def beyond(rows, edge):
    row = iota((rows, BS), 0)
    index = lax.axis_index("cast")
    first, last = index == 0, index == lax.axis_size("cast") - 1
    return first, last, (first & (row < edge)) | (last & (row >= rows - edge))


def height_faces(coeff):
    flat = jnp.zeros_like(coeff[0])
    inner = [harmonic(a, b) for a, b in zip(coeff[:-1], coeff[1:])]
    return [flat] + inner + [flat]


def whole_level(coeff, source):
    shape = coeff[0].shape
    row = iota(shape, 0)
    height = height_faces(coeff)
    cast, span, diag, relax = [], [], [], []
    for z, c in enumerate(coeff):
        lower = jnp.where(row == 0, 0.0, harmonic(shift(c, 1, 0), c))
        ends = jnp.where((row == 0) | (row == shape[0] - 1), c, 0.0)
        side = harmonic(shift(c, 1, 1), c)
        total = diagonal_of(lower, side, height[z], height[z + 1]) + ends
        cast.append(lower)
        span.append(side)
        diag.append(total)
        relax.append(WEIGHT / total)
    return Level(cast, span, height, diag, relax, source, len(coeff))


def pair_rows(value, scratch):
    rows = value.shape[0]
    scratch[...] = value
    return scratch[pl.ds(0, rows // 2, stride=2), :] + scratch[pl.ds(1, rows // 2, stride=2), :]


def by_side(axis, near_pair, far_pair):
    even = lax.rem(lax.axis_index(axis), 2) == 0
    return jnp.where(even, far_pair, near_pair), jnp.where(even, near_pair, far_pair)


def beyond_rows(near_cast, far_cast, a, z):
    reach, base = REACH[a], BASE[a]
    start = base + reach * z

    stop = base + reach * HZ
    even = lax.rem(lax.axis_index("cast"), 2) == 0

    def window(first, one, other):
        at = min(max(first, base), stop - HALO)
        rows = slice(at, at + HALO)
        return shift(jnp.where(even, one[rows], other[rows]), at - first, 0)

    return window(start - (HALO - reach), far_cast, near_cast), window(start, near_cast, far_cast)


def extended(own, near_cast, far_cast, a, z):
    before, after = beyond_rows(near_cast, far_cast, a, z)
    return jnp.concatenate([before, own[a, z], after], axis=0)


def stage_kernel(table_in, phase_in, source_in, out, far_out, near_out, table, phase, sems):
    even = lax.rem(lax.axis_index("cast"), 2) == 0

    def put(a, z, value):
        reach = REACH[a]
        first, last = value, shift(value, reach - HALO, 0)
        rows = HALO if a == 0 or z < HZ - 1 else reach
        place = slice(BASE[a] + reach * z, BASE[a] + reach * z + rows)
        near_out[place] = jnp.where(even, last, first)[:rows]
        far_out[place] = jnp.where(even, first, last)[:rows]

    copies = [
        pltpu.make_async_copy(table_in, table, sems.at[0]),
        pltpu.make_async_copy(phase_in.at[pl.ds(0, 8)], phase.at[pl.ds(0, 8)], sems.at[1]),
        pltpu.make_async_copy(phase_in.at[pl.ds(8, 8)], phase.at[pl.ds(8, 8)], sems.at[2]),
        pltpu.make_async_copy(source_in, out.at[1], sems.at[3]),
    ]
    for copy in copies:
        copy.start()
    copies[0].wait()
    copies[1].wait()
    for z in range(HZ):
        if z == 8:
            copies[2].wait()
        p = phase[z]
        value = jnp.where(p == 0, table[0], jnp.where(p == 1, table[1], table[2]))
        out[0, z] = value
        put(0, z, value)
    copies[3].wait()
    for z in range(HZ):
        put(1, z, out[1, z])


def ones(where):
    return jnp.where(where, 1.0, 0.0).astype(BF16)


def prepare_kernel(own, near_own, far_own, own_merge, mid_merge, edge_merge, slot_merge, move, narrow, widen, grow, double, expand):
    lane = iota((BC, BS), 1)
    for a in range(2):
        for group in range(2):
            head = tail = None
            for start, z in places(group):
                h, t = shift(own[a, z], start, 1), shift(own[a, z], start + HALO, 1)
                inside = (lane >= start) & (lane < start + HALO)
                head = h if head is None else jnp.where(inside, h, head)
                tail = t if tail is None else jnp.where(inside, t, tail)
            far_own[a, group], near_own[a, group] = by_side("span", tail, head)
    i, j = iota((BS, BS), 0), iota((BS, BS), 1)
    own_merge[...] = ones((i // 2 == j) & (i >= 8) & (i < 120))
    mid_merge[...] = ones((i // 2 == j) & (i >= 4) & (i < 124))
    narrow[...] = ones(((i < 64) & (i // 2 == j)) | ((i >= 96) & (i // 2 + 64 == j)))
    widen[...] = ones(((j < 64) & (j // 2 == i)) | ((j >= 96) & (j // 2 + 64 == i)))
    grow[...] = ones(((j < 96) & (j // 2 == i)) | ((j >= 96) & (j // 2 + 64 == i)))
    double[...] = ones(j // 2 == i)
    i, j = iota((BS, 2 * BS), 0), iota((BS, 2 * BS), 1)
    m = i % 64
    target = jnp.where(m < 24, (m // 2 + 120) % BS, m // 2 + 40)
    edge_merge[...] = ones(((m < 24) | (m >= 40)) & (target == j % BS) & (i // 64 == j // BS))
    i, j = iota((BS, 4 * BS), 0), iota((BS, 4 * BS), 1)
    m = i % 32
    target = jnp.where(m < 12, (m // 2 + 124) % BS, m // 2 + 52)
    slot_merge[...] = ones(((m < 12) | (m >= 20)) & (target == j % BS) & (i // 32 == j // BS))
    i, j = iota((4 * BS, BS), 0), iota((4 * BS, BS), 1)
    move[...] = ones((i % BS < 64) & (i % BS // 2 + 32 * (i // BS) == j))
    i, j = iota((2 * BS, BS), 0), iota((2 * BS, BS), 1)
    m = j % 64
    origin = jnp.where(m < 32, (m // 2 + 120) % BS, m // 2 + 40)
    expand[...] = ones((origin == i % BS) & (i // BS == j // 64))


def places(group):
    return [(16 * sub + 32 * g, group * 2 + sub + 4 * g) for sub in range(2) for g in range(4)]


def margin_kernel(near_own, far_own, far_cast, near_cast, near_span, far_span):
    lane = iota((16, BS), 1)
    seg = lane % HALO
    for a in range(2):
        for group in range(2):
            head = tail = None
            for start, z in places(group):
                before, after = beyond_rows(near_cast, far_cast, a, z)
                inner = jnp.concatenate([before[8:], after[:8]], axis=0)
                far = jnp.concatenate([before[:8], after[8:]], axis=0)
                h = jnp.where(seg >= 12, shift(far, start + 12, 1), shift(inner, start, 1))
                t = jnp.where(seg < 4, shift(far, start + HALO - 12, 1), shift(inner, start + HALO, 1))
                inside = (lane >= start) & (lane < start + HALO)
                head = h if head is None else jnp.where(inside, h, head)
                tail = t if tail is None else jnp.where(inside, t, tail)
            sides = by_side("span", tail, head)
            for out, packed, value in ((far_span, far_own, sides[0]), (near_span, near_own, sides[1])):
                out[a, group, :8] = value[:8]
                out[a, group, 8:24] = packed[a, group]
                out[a, group, 24:] = value[8:]


def spread_rows(sent, step, more):
    moved = shift(sent, step, 1)
    return jnp.concatenate([shift(sent[:8], step + more, 1), moved, shift(sent[-8:], step + more, 1)], axis=0)


def own_kernel(own, far_cast, near_cast, own_merge, mid_merge, x, b, cast, span, height, diag, relax, merged, merged_mid, inner, inner4, scratch):
    first, last, outside = beyond(ROWS, HALO)
    visc, source = [], []
    for z in range(HZ):
        v, s = (extended(own, near_cast, far_cast, a, z) for a in range(2))
        visc.append(ends(v, first, last, HALO))
        source.append(s)
    lane = iota((ROWS, BS), 1)
    for a, field in enumerate((visc, source)):
        for k in range(PACK):
            low, high = field[k], field[k + PACK]
            inner[a, k] = jnp.where(
                lane < 32,
                shift(low, 16, 1),
                jnp.where(lane < 64, shift(low, 48, 1), jnp.where(lane < 96, shift(high, 80, 1), shift(high, 112, 1))),
            )
        quarter = lane[8 : ROWS - 8]
        for k in range(4):
            value = None
            for g in range(4):
                slab = field[k + 4 * g][8 : ROWS - 8]
                edges = jnp.where(quarter % 32 < 16, shift(slab, 32 * g + 8, 1), shift(slab, 32 * g - 104, 1))
                value = edges if value is None else jnp.where(quarter // 32 == g, edges, value)
            inner4[a, k] = value
    level = fine_level(visc, source, outside, 1)
    values = level.sweep(level.start())
    keep(level, values, (x, b, cast, span, height, diag, relax))
    parts = coarse_parts(visc, level.residual(values), scratch)
    total = product(parts, own_merge[...])
    for k in range(HZ):
        merged[k] = total[HALF * k : HALF * (k + 1)]
    total = product(parts, mid_merge[...])
    for k in range(HZ):
        merged_mid[k] = total[HALF * k + 4 : HALF * (k + 1) - 4]


def edge_levels(near_span, far_span, inner, merged, edge_merge, scratch, halo):
    rows = BC + 2 * halo
    first, last, outside = beyond(rows, halo)
    wide = halo == HALO
    packed = 2 if wide else 4
    lane = iota((rows, BS), 1) % (BS // packed)
    fields = []
    for a in range(2):
        slabs = []
        for k in range(HZ // packed):
            group, offset = k % 4 // 2, 16 * (k % 2) + 32 * (k // 4)
            left, right = by_side("span", near_span[a, group], far_span[a, group])
            if wide:
                l, r = spread_rows(left, -offset, 12), spread_rows(right, 48 - offset, -12)
                value = jnp.where(lane < 16, l, jnp.where(lane >= 48, r, inner[a, k]))
            else:
                l, r = shift(left, -offset - 8, 1), shift(right, 24 - offset, 1)
                value = jnp.where(lane < 8, l, jnp.where(lane >= 24, r, inner[a, k]))
            slabs.append(ends(value, first, last, halo) if a == 0 else value)
        fields.append(slabs)
    visc, source = fields
    level = fine_level(visc, source, outside, packed)
    values = level.sweep(level.start())
    fine = level, values
    parts = coarse_parts(visc, level.residual(values), scratch)
    total = product(parts, edge_merge[...])

    edge, half = halo // 2, rows // 2
    first, last, outside = beyond(half, edge)
    weight = jnp.where(outside, 0.0, WEIGHT)
    coarse = []
    for k in range(HZ):
        a, z = divmod(k, 8)
        side, pos = divmod(z, 4 if wide else 2)
        row = half * (HZ // packed // 2 * a + pos)
        coarse.append(merged[k] + total[row : row + half, BS * side : BS * (side + 1)])
    lane = iota((half, BS), 1)
    known = (lane < BS // 2 + edge) | (lane >= BS - edge)
    coeff = [jnp.where(known, 0.125 * ends(c, first, last, edge), 1.0) for c in coarse[:8]]
    source = [0.5 * c for c in coarse[8:]]
    height = height_faces(coeff)
    cast_faces = [harmonic(shift(c, 1, 0), c) for c in coeff]
    span_faces = [harmonic(shift(c, 1, 1), c) for c in coeff]
    diagonal = [diagonal_of(cast_faces[z], span_faces[z], height[z], height[z + 1]) for z in range(8)]
    level = Level(cast_faces, span_faces, height, diagonal, [weight / d for d in diagonal], source, 8)
    return fine, (level, level.sweep(level.start()), coeff)


def state_kernel(
    near_span, far_span, inner, merged, edge_merge, x, b, cast, span, height, diag, relax,
    x1, b1, cast1, span1, height1, relax1, scratch,
):
    fine, (level, values, _) = edge_levels(near_span, far_span, inner, merged, edge_merge, scratch, HALO)
    keep(*fine, (x, b, cast, span, height, diag, relax))
    kept = (x1, values), (b1, level.source), (cast1, level.cast), (span1, level.span), (height1, level.height), (relax1, level.relax)
    for ref, items in kept:
        for z, item in enumerate(items):
            ref[z] = kept_rows1(item)


def edge_kernel(near_span, far_span, inner, merged, edge_merge, move, slots, scratch, rows8):
    _, (level, values, coeff) = edge_levels(near_span, far_span, inner, merged, edge_merge, scratch, 8)
    remains = level.residual(values)
    edge = 4

    fields = []
    for k in range(4):
        rows = slice(edge, edge + 8)
        c = coeff[2 * k][rows] + coeff[2 * k + 1][rows]
        r = remains[2 * k][rows] + remains[2 * k + 1][rows]
        rows8[k] = jnp.concatenate([0.125 * c, 0.5 * r], axis=0)
        fields.append(rows8[k, pl.ds(0, 8, stride=2), :] + rows8[k, pl.ds(1, 8, stride=2), :])
    total = product(jnp.concatenate(fields, axis=1), move[...])
    for d in range(slots.shape[0]):
        slots[d] = total


def ascent_kernel(
    own, far_column, near_column, narrow, widen, grow, double, expand,
    xo, bo, casto, spano, heighto, diago, relaxo,
    xe, be, caste, spane, heighte, diage, relaxe,
    x1, b1, cast1, span1, height1, relax1,
    solution_out, residual_out, tiles, pairs, wide2, padded2, wide1, wide_own, wide_edge, results, sems,
):
    count = own.shape[0]
    rows = 4 * count
    part_lane = iota((rows, 128), 1) // 32
    index = lax.axis_index("cast")

    fields = []
    for part in range(2):
        for d in range(count):
            rows_d = slice(4 * part, 4 * part + 4)
            left, right = by_side("span", near_column[d, rows_d], far_column[d, rows_d])
            for s, block in enumerate((own[d, rows_d], right, left)):
                tiles[s, 4 * d : 4 * d + 4] = block
        own_tile, right, left = tiles[0], shift(tiles[1], 32, 1), shift(tiles[2], -32, 1)
        slabs = []
        for z in range(4):
            both = jnp.where(part_lane == (z + 1) % 4, right, left)
            slabs.append(shift(jnp.where(part_lane == z, own_tile, both), -32 * z, 1))
        fields.append(slabs)
    coeff2, source2 = fields
    level2 = whole_level(coeff2, source2)
    x2 = level2.sweep(level2.start())
    remains = level2.residual(x2)

    gathered = []
    for field in (coeff2, remains):
        for k in range(2):
            gathered.append(pair_rows(field[2 * k] + field[2 * k + 1], pairs))
    merged = product(jnp.concatenate(gathered, axis=0), narrow[...])
    half = rows // 2
    lane3 = iota((half, 128), 1)
    known = (lane3 < 32) | (lane3 >= 112)
    coeff3 = [jnp.where(known, 0.125 * merged[half * k : half * (k + 1)], 1.0) for k in range(2)]
    source3 = [0.5 * merged[half * (2 + k) : half * (3 + k)] for k in range(2)]
    level3 = whole_level(coeff3, source3)
    x3 = level3.solve(SWEEPS_COARSE - 1)

    spread = product(jnp.concatenate(x3, axis=0), widen[...])
    for k in range(2):
        wide2[k, pl.ds(0, half, stride=2), :] = spread[half * k : half * (k + 1)]
        wide2[k, pl.ds(1, half, stride=2), :] = spread[half * k : half * (k + 1)]
    x2 = [x2[z] + wide2[z // 2] for z in range(4)]
    x2 = level2.sweep(level2.sweep(x2))

    for z in range(4):
        padded2[z, 0:8] = jnp.zeros((8, 128), F32)
        padded2[z, 8 : 8 + rows] = x2[z]
        padded2[z, 8 + rows : 16 + rows] = jnp.zeros((8, 128), F32)
    local = [shift(padded2[z, pl.ds(4 * index + 6, 8), :], -2, 0) for z in range(4)]
    spread = product(jnp.concatenate(local, axis=0), grow[...])
    for z in range(4):
        for s in range(2):
            wide1[z, pl.ds(s, 8, stride=2), :] = spread[8 * z : 8 * z + 8]
    level1 = Level(cast1, span1, height1, None, relax1, b1, 8)
    x = [x1[z] + wide1[z // 2] for z in range(8)]
    x = level1.sweep(level1.sweep(x))

    spread = product(jnp.concatenate(x, axis=0), double[...])
    for z in range(8):
        for s in range(2):
            wide_own[z, pl.ds(s, KEPT1, stride=2), :] = spread[KEPT1 * z : KEPT1 * (z + 1)]
    sides = [jnp.concatenate([x[k], x[k + 4]], axis=1) for k in range(4)]
    spread = product(jnp.concatenate(sides, axis=0), expand[...])
    for k in range(4):
        for s in range(2):
            wide_edge[k, pl.ds(s, KEPT1, stride=2), :] = spread[KEPT1 * k : KEPT1 * (k + 1)]
    level_own = Level(casto, spano, heighto, diago, relaxo, bo, HZ)
    level_edge = Level(caste, spane, heighte, diage, relaxe, be, PACK, 2)

    def refined(wide, k):
        edge = jnp.where(iota((8, BS), 0) < 4, wide[k, BC : BC + 8], wide[k, BC + 8 :])
        return jnp.concatenate([wide[k, :BC], edge], axis=0)

    own_wide = [refined(wide_own, k) for k in range(8)]
    edge_wide = [refined(wide_edge, k) for k in range(4)]
    own_x = [xo[z] + own_wide[z // 2] for z in range(HZ)]
    edge_x = [xe[k] + edge_wide[k // 2] for k in range(PACK)]
    edge_x = level_edge.sweep(level_edge.sweep(edge_x))
    own_x = level_own.sweep(level_own.sweep(own_x))
    lane = iota((BC, BS), 1)
    rows = slice(0, BC)

    copies = []

    beside = lane % 64 < 16

    def joined(side):
        return jnp.where(beside, shift(side[rows], -32, 1), side[rows])

    def give(number, out, z, mid, side):
        value = shift(side, -16 - 64 * (z // PACK), 1)
        results[number, z] = jnp.where((lane < 8) | (lane >= 120), value, mid[rows])
        if z % 4 == 3:
            quarter = pl.ds(z - 3, 4)
            copy = pltpu.make_async_copy(results.at[number, quarter], out.at[quarter], sems.at[number, z // 4])
            copy.start()
            copies.append(copy)

    sides = [joined(value) for value in edge_x]
    for z in range(HZ):
        give(0, solution_out, z, own_x[z], sides[z % PACK])
    sides = [joined(value) for value in level_edge.residual(edge_x)]
    for z in range(HZ):
        give(1, residual_out, z, level_own.residual_at(own_x, z), sides[z % PACK])
    for copy in copies:
        copy.wait()


VMEM = pl.BlockSpec(memory_space=pltpu.VMEM)
HBM = pl.BlockSpec(memory_space=pltpu.HBM)
PARAMS = pltpu.CompilerParams(vmem_limit_bytes=16 * 1024 * 1024)
INTERPRET = False


def call(kernel, in_specs, outs, scratch=(), out_spec=VMEM):
    return pl.pallas_call(
        kernel,
        in_specs=in_specs,
        out_specs=[out_spec] * len(outs),
        out_shape=[jax.ShapeDtypeStruct(s, F32) if isinstance(s, tuple) else s for s in outs],
        scratch_shapes=[pltpu.VMEM(s, F32) if isinstance(s, tuple) else s for s in scratch],
        compiler_params=PARAMS,
        interpret=INTERPRET,
    )


def swap(value, axis, far):
    size = lax.axis_size(axis)
    partner = [(((i - 1) ^ 1) + 1) % size if far else i ^ 1 for i in range(size)]
    return lax.ppermute(value, axis, list(enumerate(partner)))


def shards(phase, viscosity_table, pressure_source):
    count = lax.axis_size("cast")
    packed = (2, 2, SENT, BS)
    own_state = [(HZ, KEPT, BS)] * 4 + [(HZ + 1, KEPT, BS)] + [(HZ, KEPT, BS)] * 2
    edge_state = [(PACK, KEPT, BS)] * 4 + [(PACK + 1, KEPT, BS)] + [(PACK, KEPT, BS)] * 2
    level1_state = [(8, KEPT1, BS)] * 4 + [(9, KEPT1, BS), (8, KEPT1, BS)]

    arguments = (pltpu.with_memory_space_constraint(a, pltpu.HBM) for a in (viscosity_table, phase, pressure_source))
    stage_scratch = [pltpu.SMEM((3,), F32), pltpu.VMEM((HZ, BC, BS), jnp.int32), pltpu.SemaphoreType.DMA((4,))]
    own, far_cast, near_cast = call(
        stage_kernel, [HBM] * 3, [(2, HZ, BC, BS), (CAST_ROWS, BS), (CAST_ROWS, BS)], stage_scratch
    )(*arguments)
    far_cast = swap(far_cast, "cast", True)
    near_cast = swap(near_cast, "cast", False)
    square = (BS, BS)
    tables = [square, square, (BS, 2 * BS), (BS, 4 * BS), (4 * BS, BS), square, square, square, square, (2 * BS, BS)]
    tables = [jax.ShapeDtypeStruct(t, BF16) for t in tables]
    near_own, far_own, own_merge, mid_merge, edge_merge, slot_merge, move, *spreads = call(
        prepare_kernel, [VMEM], [(2, 2, BC, BS)] * 2 + tables
    )(own)
    near_span, far_span = call(margin_kernel, [VMEM] * 4, [packed, packed])(near_own, far_own, far_cast, near_cast)
    near_span = swap(near_span, "span", False)
    far_span = swap(far_span, "span", True)
    *kept_own, merged, merged_mid, inner, inner4 = call(
        own_kernel,
        [VMEM] * 5,
        own_state + [(HZ, HALF, BS), (HZ, HALF - 8, BS), (2, PACK, ROWS, BS), (2, 4, SENT, BS)],
        [(HZ, ROWS, BS)],
    )(own, far_cast, near_cast, own_merge, mid_merge)
    (slots,) = call(
        edge_kernel, [VMEM] * 6, [(count, 8, BS)], [(4, SENT, BS), (4, 16, BS)]
    )(near_span, far_span, inner4, merged_mid, slot_merge, move)
    kept_edge = call(state_kernel, [VMEM] * 5, edge_state + level1_state, [(8, ROWS, BS)])(
        near_span, far_span, inner, merged, edge_merge
    )

    column = lax.all_to_all(slots, "cast", 0, 0)
    near_column = swap(column, "span", False)
    far_column = swap(column, "span", True)
    rows = 4 * count
    scratch = [
        (3, rows, BS),
        (rows, BS),
        (2, rows, BS),
        (4, rows + 16, BS),
        (4, KEPT1, BS),
        (8, 2 * KEPT1, BS),
        (4, 2 * KEPT1, BS),
        (2, HZ, BC, BS),
        pltpu.SemaphoreType.DMA((2, 4)),
    ]
    state = spreads + kept_own + list(kept_edge)
    return tuple(
        call(ascent_kernel, [VMEM] * (3 + len(state)), [(HZ, BC, BS)] * 2, scratch, HBM)(
            column, far_column, near_column, *state
        )
    )


def solution(mesh):
    blocks = P(None, "cast", "span")
    return jax.shard_map(
        shards,
        mesh=mesh,
        in_specs=(blocks, P(), blocks),
        out_specs=(blocks, blocks),
        check_vma=False,
    )
```

```python
import jax
import jax.numpy as jnp
from jax import lax
from jax.experimental import pallas as pl
from jax.experimental.pallas import tpu as pltpu
from jax.sharding import PartitionSpec as P

HZ, BC, BS = 16, 16, 128
HALO = 16
ROWS = BC + 2 * HALO
HALF = ROWS // 2
KEPT = BC + 8
KEPT1 = HALF - 8
SENT = BC + 16
REACH = (13, 12)
BASE = (0, REACH[0] * HZ)
CAST_ROWS = sum(REACH) * HZ
PACK = HZ // 2
SWEEPS_COARSE = 8
WEIGHT = 0.8
F32 = jnp.float32
BF16 = jnp.bfloat16


def shift(x, step, axis):
    if step == 0:
        return x
    return pltpu.roll(x, step % x.shape[axis], axis)


def iota(shape, axis):
    return lax.broadcasted_iota(jnp.int32, shape, axis)


def product(a, b):
    high = a.astype(BF16)
    low = (a - high.astype(F32)).astype(BF16)
    parts, twice = jnp.concatenate([high, low], axis=1), jnp.concatenate([b, b], axis=0)
    return jnp.dot(parts, twice, preferred_element_type=F32)


def harmonic(a, b):
    return 2.0 * a * b / (a + b)


def near(x, below, above, cast, span, low, high):
    return (
        (cast * shift(x, 1, 0) + shift(cast * x, -1, 0))
        + (low * below + high * above)
        + (span * shift(x, 1, 1) + shift(span * x, -1, 1))
    )


def diagonal_of(cast, span, low, high):
    return cast + shift(cast, -1, 0) + span + shift(span, -1, 1) + low + high


class Level:
    def __init__(self, cast, span, height, diag, relax, source, depth, packed=1):
        self.cast, self.span, self.height = cast, span, height
        self.diag, self.relax, self.source = diag, relax, source
        self.depth, self.packed = depth, packed

    def near(self, x, z):
        last = self.depth - 1
        below, above = x[max(z - 1, 0)], x[min(z + 1, last)]
        if self.packed > 1 and z == 0:
            below = shift(x[last], BS // self.packed, 1)
        if self.packed > 1 and z == last:
            above = shift(x[0], -(BS // self.packed), 1)
        return near(x[z], below, above, self.cast[z], self.span[z], self.height[z], self.height[z + 1])

    def start(self):
        return [self.relax[z] * self.source[z] for z in range(self.depth)]

    def sweep(self, x):
        return [
            (1.0 - WEIGHT) * x[z] + self.relax[z] * (self.near(x, z) + self.source[z])
            for z in range(self.depth)
        ]

    def solve(self, sweeps):
        part = [
            (
                relax * self.cast[z],
                relax * shift(self.cast[z], -1, 0),
                relax * self.span[z],
                relax * shift(self.span[z], -1, 1),
                relax * self.height[1],
            )
            for z, relax in enumerate(self.relax)
        ]
        first = x = self.start()
        for _ in range(sweeps):
            x = [
                ((1.0 - WEIGHT) * x[z] + first[z] + part[z][4] * x[1 - z])
                + (part[z][0] * shift(x[z], 1, 0) + part[z][1] * shift(x[z], -1, 0))
                + (part[z][2] * shift(x[z], 1, 1) + part[z][3] * shift(x[z], -1, 1))
                for z in range(2)
            ]
        return x

    def residual_at(self, x, z):
        return self.source[z] - self.diag[z] * x[z] + self.near(x, z)

    def residual(self, x):
        return [self.residual_at(x, z) for z in range(self.depth)]


def fine_level(visc, source, outside, packed):
    depth = len(visc)
    shape = visc[0].shape
    weight = jnp.where(outside, 0.0, WEIGHT)
    cast = [2.0 / (v + shift(v, 1, 0)) for v in visc]
    span = [2.0 / (v + shift(v, 1, 1)) for v in visc]
    inner = [2.0 / (a + b) for a, b in zip(visc[:-1], visc[1:])]
    if packed > 1:
        width = BS // packed
        bottom = jnp.where(iota(shape, 1) < width, 0.0, 2.0 / (visc[0] + shift(visc[-1], width, 1)))
        top = shift(bottom, -width, 1)
    else:
        bottom = top = jnp.zeros(shape, F32)
    height = [bottom] + inner + [top]
    diag = [diagonal_of(cast[z], span[z], height[z], height[z + 1]) for z in range(depth)]
    relax = [weight / d for d in diag]
    return Level(cast, span, height, diag, relax, source, depth, packed)


def kept_rows(value):
    edge = jnp.where(iota((8, BS), 0) < 4, value[HALO + BC : HALO + BC + 8], value[HALO - 8 : HALO])
    return jnp.concatenate([value[HALO : HALO + BC], edge], axis=0)


def kept_rows1(value):
    return jnp.concatenate([value[8:16], jnp.where(iota((8, BS), 0) < 4, value[16:], value[:8])], axis=0)


def keep(level, x, refs):
    for ref, values in zip(refs, (x, level.source, level.cast, level.span, level.height, level.diag, level.relax)):
        for z, value in enumerate(values):
            ref[z] = kept_rows(value)


def coarse_parts(visc, remains, scratch):
    parts = []
    count = len(visc) // 2
    half = visc[0].shape[0] // 2
    for a, values in enumerate(([1.0 / v for v in visc], remains)):
        for k in range(count):
            scratch[a * count + k] = values[2 * k] + values[2 * k + 1]
            ref = scratch.at[a * count + k]
            parts.append(ref[pl.ds(0, half, stride=2), :] + ref[pl.ds(1, half, stride=2), :])
    return jnp.concatenate(parts, axis=0)


def ends(value, first, last, edge):
    rows = value.shape[0]
    row = iota((rows, BS), 0)
    value = jnp.where(first & (row < edge), jnp.broadcast_to(value[edge : edge + 1], (rows, BS)), value)
    stop = rows - edge
    return jnp.where(last & (row >= stop), jnp.broadcast_to(value[stop - 1 : stop], (rows, BS)), value)


def beyond(rows, edge):
    row = iota((rows, BS), 0)
    index = lax.axis_index("cast")
    first, last = index == 0, index == lax.axis_size("cast") - 1
    return first, last, (first & (row < edge)) | (last & (row >= rows - edge))


def height_faces(coeff):
    flat = jnp.zeros_like(coeff[0])
    inner = [harmonic(a, b) for a, b in zip(coeff[:-1], coeff[1:])]
    return [flat] + inner + [flat]


def whole_level(coeff, source):
    shape = coeff[0].shape
    row = iota(shape, 0)
    height = height_faces(coeff)
    cast, span, diag, relax = [], [], [], []
    for z, c in enumerate(coeff):
        lower = jnp.where(row == 0, 0.0, harmonic(shift(c, 1, 0), c))
        ends = jnp.where((row == 0) | (row == shape[0] - 1), c, 0.0)
        side = harmonic(shift(c, 1, 1), c)
        total = diagonal_of(lower, side, height[z], height[z + 1]) + ends
        cast.append(lower)
        span.append(side)
        diag.append(total)
        relax.append(WEIGHT / total)
    return Level(cast, span, height, diag, relax, source, len(coeff))


def pair_rows(value, scratch):
    rows = value.shape[0]
    scratch[...] = value
    return scratch[pl.ds(0, rows // 2, stride=2), :] + scratch[pl.ds(1, rows // 2, stride=2), :]


def by_side(axis, near_pair, far_pair):
    even = lax.rem(lax.axis_index(axis), 2) == 0
    return jnp.where(even, far_pair, near_pair), jnp.where(even, near_pair, far_pair)


def beyond_rows(near_cast, far_cast, a, z):
    reach, base = REACH[a], BASE[a]
    start = base + reach * z

    stop = base + reach * HZ
    even = lax.rem(lax.axis_index("cast"), 2) == 0

    def window(first, one, other):
        at = min(max(first, base), stop - HALO)
        rows = slice(at, at + HALO)
        return shift(jnp.where(even, one[rows], other[rows]), at - first, 0)

    return window(start - (HALO - reach), far_cast, near_cast), window(start, near_cast, far_cast)


def extended(own, near_cast, far_cast, a, z):
    before, after = beyond_rows(near_cast, far_cast, a, z)
    return jnp.concatenate([before, own[a, z], after], axis=0)


def stage_kernel(table_in, phase_in, source_in, out, far_out, near_out, table, phase, sems):
    even = lax.rem(lax.axis_index("cast"), 2) == 0

    def put(a, z, value):
        reach = REACH[a]
        first, last = value, shift(value, reach - HALO, 0)
        rows = HALO if a == 0 or z < HZ - 1 else reach
        place = slice(BASE[a] + reach * z, BASE[a] + reach * z + rows)
        near_out[place] = jnp.where(even, last, first)[:rows]
        far_out[place] = jnp.where(even, first, last)[:rows]

    copies = [
        pltpu.make_async_copy(table_in, table, sems.at[0]),
        pltpu.make_async_copy(phase_in.at[pl.ds(0, 8)], phase.at[pl.ds(0, 8)], sems.at[1]),
        pltpu.make_async_copy(phase_in.at[pl.ds(8, 8)], phase.at[pl.ds(8, 8)], sems.at[2]),
        pltpu.make_async_copy(source_in, out.at[1], sems.at[3]),
    ]
    for copy in copies:
        copy.start()
    copies[0].wait()
    copies[1].wait()
    for z in range(HZ):
        if z == 8:
            copies[2].wait()
        p = phase[z]
        value = jnp.where(p == 0, table[0], jnp.where(p == 1, table[1], table[2]))
        out[0, z] = value
        put(0, z, value)
    copies[3].wait()
    for z in range(HZ):
        put(1, z, out[1, z])


def ones(where):
    return jnp.where(where, 1.0, 0.0).astype(BF16)


def prepare_kernel(own, near_own, far_own, own_merge, mid_merge, edge_merge, slot_merge, move, narrow, widen, grow, double, expand):
    lane = iota((BC, BS), 1)
    for a in range(2):
        for group in range(2):
            head = tail = None
            for start, z in places(group):
                h, t = shift(own[a, z], start, 1), shift(own[a, z], start + HALO, 1)
                inside = (lane >= start) & (lane < start + HALO)
                head = h if head is None else jnp.where(inside, h, head)
                tail = t if tail is None else jnp.where(inside, t, tail)
            far_own[a, group], near_own[a, group] = by_side("span", tail, head)
    i, j = iota((BS, BS), 0), iota((BS, BS), 1)
    own_merge[...] = ones((i // 2 == j) & (i >= 8) & (i < 120))
    mid_merge[...] = ones((i // 2 == j) & (i >= 4) & (i < 124))
    narrow[...] = ones(((i < 64) & (i // 2 == j)) | ((i >= 96) & (i // 2 + 64 == j)))
    widen[...] = ones(((j < 64) & (j // 2 == i)) | ((j >= 96) & (j // 2 + 64 == i)))
    grow[...] = ones(((j < 96) & (j // 2 == i)) | ((j >= 96) & (j // 2 + 64 == i)))
    double[...] = ones(j // 2 == i)
    i, j = iota((BS, 2 * BS), 0), iota((BS, 2 * BS), 1)
    m = i % 64
    target = jnp.where(m < 24, (m // 2 + 120) % BS, m // 2 + 40)
    edge_merge[...] = ones(((m < 24) | (m >= 40)) & (target == j % BS) & (i // 64 == j // BS))
    i, j = iota((BS, 4 * BS), 0), iota((BS, 4 * BS), 1)
    m = i % 32
    target = jnp.where(m < 12, (m // 2 + 124) % BS, m // 2 + 52)
    slot_merge[...] = ones(((m < 12) | (m >= 20)) & (target == j % BS) & (i // 32 == j // BS))
    i, j = iota((4 * BS, BS), 0), iota((4 * BS, BS), 1)
    move[...] = ones((i % BS < 64) & (i % BS // 2 + 32 * (i // BS) == j))
    i, j = iota((2 * BS, BS), 0), iota((2 * BS, BS), 1)
    m = j % 64
    origin = jnp.where(m < 32, (m // 2 + 120) % BS, m // 2 + 40)
    expand[...] = ones((origin == i % BS) & (i // BS == j // 64))


def places(group):
    return [(16 * sub + 32 * g, group * 2 + sub + 4 * g) for sub in range(2) for g in range(4)]


def margin_kernel(near_own, far_own, far_cast, near_cast, near_span, far_span):
    lane = iota((16, BS), 1)
    seg = lane % HALO
    for a in range(2):
        for group in range(2):
            head = tail = None
            for start, z in places(group):
                before, after = beyond_rows(near_cast, far_cast, a, z)
                inner = jnp.concatenate([before[8:], after[:8]], axis=0)
                far = jnp.concatenate([before[:8], after[8:]], axis=0)
                h = jnp.where(seg >= 12, shift(far, start + 12, 1), shift(inner, start, 1))
                t = jnp.where(seg < 4, shift(far, start + HALO - 12, 1), shift(inner, start + HALO, 1))
                inside = (lane >= start) & (lane < start + HALO)
                head = h if head is None else jnp.where(inside, h, head)
                tail = t if tail is None else jnp.where(inside, t, tail)
            sides = by_side("span", tail, head)
            for out, packed, value in ((far_span, far_own, sides[0]), (near_span, near_own, sides[1])):
                out[a, group, :8] = value[:8]
                out[a, group, 8:24] = packed[a, group]
                out[a, group, 24:] = value[8:]


def spread_rows(sent, step, more):
    moved = shift(sent, step, 1)
    return jnp.concatenate([shift(sent[:8], step + more, 1), moved, shift(sent[-8:], step + more, 1)], axis=0)


def own_kernel(own, far_cast, near_cast, own_merge, mid_merge, x, b, cast, span, height, diag, relax, merged, merged_mid, inner, inner4, scratch):
    first, last, outside = beyond(ROWS, HALO)
    visc, source = [], []
    for z in range(HZ):
        v, s = (extended(own, near_cast, far_cast, a, z) for a in range(2))
        visc.append(ends(v, first, last, HALO))
        source.append(s)
    lane = iota((ROWS, BS), 1)
    for a, field in enumerate((visc, source)):
        for k in range(PACK):
            low, high = field[k], field[k + PACK]
            inner[a, k] = jnp.where(
                lane < 32,
                shift(low, 16, 1),
                jnp.where(lane < 64, shift(low, 48, 1), jnp.where(lane < 96, shift(high, 80, 1), shift(high, 112, 1))),
            )
        quarter = lane[8 : ROWS - 8]
        for k in range(4):
            value = None
            for g in range(4):
                slab = field[k + 4 * g][8 : ROWS - 8]
                edges = jnp.where(quarter % 32 < 16, shift(slab, 32 * g + 8, 1), shift(slab, 32 * g - 104, 1))
                value = edges if value is None else jnp.where(quarter // 32 == g, edges, value)
            inner4[a, k] = value
    level = fine_level(visc, source, outside, 1)
    values = level.sweep(level.start())
    keep(level, values, (x, b, cast, span, height, diag, relax))
    parts = coarse_parts(visc, level.residual(values), scratch)
    total = product(parts, own_merge[...])
    for k in range(HZ):
        merged[k] = total[HALF * k : HALF * (k + 1)]
    total = product(parts, mid_merge[...])
    for k in range(HZ):
        merged_mid[k] = total[HALF * k + 4 : HALF * (k + 1) - 4]


def edge_levels(near_span, far_span, inner, merged, edge_merge, scratch, halo):
    rows = BC + 2 * halo
    first, last, outside = beyond(rows, halo)
    wide = halo == HALO
    packed = 2 if wide else 4
    lane = iota((rows, BS), 1) % (BS // packed)
    fields = []
    for a in range(2):
        slabs = []
        for k in range(HZ // packed):
            group, offset = k % 4 // 2, 16 * (k % 2) + 32 * (k // 4)
            left, right = by_side("span", near_span[a, group], far_span[a, group])
            if wide:
                l, r = spread_rows(left, -offset, 12), spread_rows(right, 48 - offset, -12)
                value = jnp.where(lane < 16, l, jnp.where(lane >= 48, r, inner[a, k]))
            else:
                l, r = shift(left, -offset - 8, 1), shift(right, 24 - offset, 1)
                value = jnp.where(lane < 8, l, jnp.where(lane >= 24, r, inner[a, k]))
            slabs.append(ends(value, first, last, halo) if a == 0 else value)
        fields.append(slabs)
    visc, source = fields
    level = fine_level(visc, source, outside, packed)
    values = level.sweep(level.start())
    fine = level, values
    parts = coarse_parts(visc, level.residual(values), scratch)
    total = product(parts, edge_merge[...])

    edge, half = halo // 2, rows // 2
    first, last, outside = beyond(half, edge)
    weight = jnp.where(outside, 0.0, WEIGHT)
    coarse = []
    for k in range(HZ):
        a, z = divmod(k, 8)
        side, pos = divmod(z, 4 if wide else 2)
        row = half * (HZ // packed // 2 * a + pos)
        coarse.append(merged[k] + total[row : row + half, BS * side : BS * (side + 1)])
    lane = iota((half, BS), 1)
    known = (lane < BS // 2 + edge) | (lane >= BS - edge)
    coeff = [jnp.where(known, 0.125 * ends(c, first, last, edge), 1.0) for c in coarse[:8]]
    source = [0.5 * c for c in coarse[8:]]
    height = height_faces(coeff)
    cast_faces = [harmonic(shift(c, 1, 0), c) for c in coeff]
    span_faces = [harmonic(shift(c, 1, 1), c) for c in coeff]
    diagonal = [diagonal_of(cast_faces[z], span_faces[z], height[z], height[z + 1]) for z in range(8)]
    level = Level(cast_faces, span_faces, height, diagonal, [weight / d for d in diagonal], source, 8)
    return fine, (level, level.sweep(level.start()), coeff)


def state_kernel(
    near_span, far_span, inner, merged, edge_merge, x, b, cast, span, height, diag, relax,
    x1, b1, cast1, span1, height1, relax1, scratch,
):
    fine, (level, values, _) = edge_levels(near_span, far_span, inner, merged, edge_merge, scratch, HALO)
    keep(*fine, (x, b, cast, span, height, diag, relax))
    kept = (x1, values), (b1, level.source), (cast1, level.cast), (span1, level.span), (height1, level.height), (relax1, level.relax)
    for ref, items in kept:
        for z, item in enumerate(items):
            ref[z] = kept_rows1(item)


def edge_kernel(near_span, far_span, inner, merged, edge_merge, move, slots, scratch, rows8):
    _, (level, values, coeff) = edge_levels(near_span, far_span, inner, merged, edge_merge, scratch, 8)
    remains = level.residual(values)
    edge = 4

    fields = []
    for k in range(4):
        rows = slice(edge, edge + 8)
        c = coeff[2 * k][rows] + coeff[2 * k + 1][rows]
        r = remains[2 * k][rows] + remains[2 * k + 1][rows]
        rows8[k] = jnp.concatenate([0.125 * c, 0.5 * r], axis=0)
        fields.append(rows8[k, pl.ds(0, 8, stride=2), :] + rows8[k, pl.ds(1, 8, stride=2), :])
    total = product(jnp.concatenate(fields, axis=1), move[...])
    for d in range(slots.shape[0]):
        slots[d] = total


def ascent_kernel(
    own, far_column, near_column, narrow, widen, grow, double, expand,
    xo, bo, casto, spano, heighto, diago, relaxo,
    xe, be, caste, spane, heighte, diage, relaxe,
    x1, b1, cast1, span1, height1, relax1,
    solution_out, residual_out, tiles, pairs, wide2, padded2, wide1, wide_own, wide_edge, results, sems,
):
    count = own.shape[0]
    rows = 4 * count
    part_lane = iota((rows, 128), 1) // 32
    index = lax.axis_index("cast")

    fields = []
    for part in range(2):
        for d in range(count):
            rows_d = slice(4 * part, 4 * part + 4)
            left, right = by_side("span", near_column[d, rows_d], far_column[d, rows_d])
            for s, block in enumerate((own[d, rows_d], right, left)):
                tiles[s, 4 * d : 4 * d + 4] = block
        own_tile, right, left = tiles[0], shift(tiles[1], 32, 1), shift(tiles[2], -32, 1)
        slabs = []
        for z in range(4):
            both = jnp.where(part_lane == (z + 1) % 4, right, left)
            slabs.append(shift(jnp.where(part_lane == z, own_tile, both), -32 * z, 1))
        fields.append(slabs)
    coeff2, source2 = fields
    level2 = whole_level(coeff2, source2)
    x2 = level2.sweep(level2.start())
    remains = level2.residual(x2)

    gathered = []
    for field in (coeff2, remains):
        for k in range(2):
            gathered.append(pair_rows(field[2 * k] + field[2 * k + 1], pairs))
    merged = product(jnp.concatenate(gathered, axis=0), narrow[...])
    half = rows // 2
    lane3 = iota((half, 128), 1)
    known = (lane3 < 32) | (lane3 >= 112)
    coeff3 = [jnp.where(known, 0.125 * merged[half * k : half * (k + 1)], 1.0) for k in range(2)]
    source3 = [0.5 * merged[half * (2 + k) : half * (3 + k)] for k in range(2)]
    level3 = whole_level(coeff3, source3)
    x3 = level3.solve(SWEEPS_COARSE - 1)

    spread = product(jnp.concatenate(x3, axis=0), widen[...])
    for k in range(2):
        wide2[k, pl.ds(0, half, stride=2), :] = spread[half * k : half * (k + 1)]
        wide2[k, pl.ds(1, half, stride=2), :] = spread[half * k : half * (k + 1)]
    x2 = [x2[z] + wide2[z // 2] for z in range(4)]
    x2 = level2.sweep(level2.sweep(x2))

    for z in range(4):
        padded2[z, 0:8] = jnp.zeros((8, 128), F32)
        padded2[z, 8 : 8 + rows] = x2[z]
        padded2[z, 8 + rows : 16 + rows] = jnp.zeros((8, 128), F32)
    local = [shift(padded2[z, pl.ds(4 * index + 6, 8), :], -2, 0) for z in range(4)]
    spread = product(jnp.concatenate(local, axis=0), grow[...])
    for z in range(4):
        for s in range(2):
            wide1[z, pl.ds(s, 8, stride=2), :] = spread[8 * z : 8 * z + 8]
    level1 = Level(cast1, span1, height1, None, relax1, b1, 8)
    x = [x1[z] + wide1[z // 2] for z in range(8)]
    x = level1.sweep(level1.sweep(x))

    spread = product(jnp.concatenate(x, axis=0), double[...])
    for z in range(8):
        for s in range(2):
            wide_own[z, pl.ds(s, KEPT1, stride=2), :] = spread[KEPT1 * z : KEPT1 * (z + 1)]
    sides = [jnp.concatenate([x[k], x[k + 4]], axis=1) for k in range(4)]
    spread = product(jnp.concatenate(sides, axis=0), expand[...])
    for k in range(4):
        for s in range(2):
            wide_edge[k, pl.ds(s, KEPT1, stride=2), :] = spread[KEPT1 * k : KEPT1 * (k + 1)]
    level_own = Level(casto, spano, heighto, diago, relaxo, bo, HZ)
    level_edge = Level(caste, spane, heighte, diage, relaxe, be, PACK, 2)

    def refined(wide, k):
        edge = jnp.where(iota((8, BS), 0) < 4, wide[k, BC : BC + 8], wide[k, BC + 8 :])
        return jnp.concatenate([wide[k, :BC], edge], axis=0)

    own_wide = [refined(wide_own, k) for k in range(8)]
    edge_wide = [refined(wide_edge, k) for k in range(4)]
    own_x = [xo[z] + own_wide[z // 2] for z in range(HZ)]
    edge_x = [xe[k] + edge_wide[k // 2] for k in range(PACK)]
    edge_x = level_edge.sweep(level_edge.sweep(edge_x))
    own_x = level_own.sweep(level_own.sweep(own_x))
    lane = iota((BC, BS), 1)
    rows = slice(0, BC)

    copies = []

    beside = lane % 64 < 16

    def joined(side):
        return jnp.where(beside, shift(side[rows], -32, 1), side[rows])

    def give(number, out, z, mid, side):
        value = shift(side, -16 - 64 * (z // PACK), 1)
        results[number, z] = jnp.where((lane < 8) | (lane >= 120), value, mid[rows])
        if z % 4 == 3:
            quarter = pl.ds(z - 3, 4)
            copy = pltpu.make_async_copy(results.at[number, quarter], out.at[quarter], sems.at[number, z // 4])
            copy.start()
            copies.append(copy)

    sides = [joined(value) for value in edge_x]
    for z in range(HZ):
        give(0, solution_out, z, own_x[z], sides[z % PACK])
    sides = [joined(value) for value in level_edge.residual(edge_x)]
    for z in range(HZ):
        give(1, residual_out, z, level_own.residual_at(own_x, z), sides[z % PACK])
    for copy in copies:
        copy.wait()


VMEM = pl.BlockSpec(memory_space=pltpu.VMEM)
HBM = pl.BlockSpec(memory_space=pltpu.HBM)
PARAMS = pltpu.CompilerParams(vmem_limit_bytes=16 * 1024 * 1024)
INTERPRET = False


def call(kernel, in_specs, outs, scratch=(), out_spec=VMEM):
    return pl.pallas_call(
        kernel,
        in_specs=in_specs,
        out_specs=[out_spec] * len(outs),
        out_shape=[jax.ShapeDtypeStruct(s, F32) if isinstance(s, tuple) else s for s in outs],
        scratch_shapes=[pltpu.VMEM(s, F32) if isinstance(s, tuple) else s for s in scratch],
        compiler_params=PARAMS,
        interpret=INTERPRET,
    )


def swap(value, axis, far):
    size = lax.axis_size(axis)
    partner = [(((i - 1) ^ 1) + 1) % size if far else i ^ 1 for i in range(size)]
    return lax.ppermute(value, axis, list(enumerate(partner)))


def shards(phase, viscosity_table, pressure_source):
    count = lax.axis_size("cast")
    packed = (2, 2, SENT, BS)
    own_state = [(HZ, KEPT, BS)] * 4 + [(HZ + 1, KEPT, BS)] + [(HZ, KEPT, BS)] * 2
    edge_state = [(PACK, KEPT, BS)] * 4 + [(PACK + 1, KEPT, BS)] + [(PACK, KEPT, BS)] * 2
    level1_state = [(8, KEPT1, BS)] * 4 + [(9, KEPT1, BS), (8, KEPT1, BS)]

    arguments = (pltpu.with_memory_space_constraint(a, pltpu.HBM) for a in (viscosity_table, phase, pressure_source))
    stage_scratch = [pltpu.SMEM((3,), F32), pltpu.VMEM((HZ, BC, BS), jnp.int32), pltpu.SemaphoreType.DMA((4,))]
    own, far_cast, near_cast = call(
        stage_kernel, [HBM] * 3, [(2, HZ, BC, BS), (CAST_ROWS, BS), (CAST_ROWS, BS)], stage_scratch
    )(*arguments)
    far_cast = swap(far_cast, "cast", True)
    near_cast = swap(near_cast, "cast", False)
    square = (BS, BS)
    tables = [square, square, (BS, 2 * BS), (BS, 4 * BS), (4 * BS, BS), square, square, square, square, (2 * BS, BS)]
    tables = [jax.ShapeDtypeStruct(t, BF16) for t in tables]
    near_own, far_own, own_merge, mid_merge, edge_merge, slot_merge, move, *spreads = call(
        prepare_kernel, [VMEM], [(2, 2, BC, BS)] * 2 + tables
    )(own)
    near_span, far_span = call(margin_kernel, [VMEM] * 4, [packed, packed])(near_own, far_own, far_cast, near_cast)
    near_span = swap(near_span, "span", False)
    far_span = swap(far_span, "span", True)
    *kept_own, merged, merged_mid, inner, inner4 = call(
        own_kernel,
        [VMEM] * 5,
        own_state + [(HZ, HALF, BS), (HZ, HALF - 8, BS), (2, PACK, ROWS, BS), (2, 4, SENT, BS)],
        [(HZ, ROWS, BS)],
    )(own, far_cast, near_cast, own_merge, mid_merge)
    (slots,) = call(
        edge_kernel, [VMEM] * 6, [(count, 8, BS)], [(4, SENT, BS), (4, 16, BS)]
    )(near_span, far_span, inner4, merged_mid, slot_merge, move)
    kept_edge = call(state_kernel, [VMEM] * 5, edge_state + level1_state, [(8, ROWS, BS)])(
        near_span, far_span, inner, merged, edge_merge
    )

    column = lax.all_to_all(slots, "cast", 0, 0)
    near_column = swap(column, "span", False)
    far_column = swap(column, "span", True)
    rows = 4 * count
    scratch = [
        (3, rows, BS),
        (rows, BS),
        (2, rows, BS),
        (4, rows + 16, BS),
        (4, KEPT1, BS),
        (8, 2 * KEPT1, BS),
        (4, 2 * KEPT1, BS),
        (2, HZ, BC, BS),
        pltpu.SemaphoreType.DMA((2, 4)),
    ]
    state = spreads + kept_own + list(kept_edge)
    return tuple(
        call(ascent_kernel, [VMEM] * (3 + len(state)), [(HZ, BC, BS)] * 2, scratch, HBM)(
            column, far_column, near_column, *state
        )
    )


def solution(mesh):
    blocks = P(None, "cast", "span")
    return jax.shard_map(
        shards,
        mesh=mesh,
        in_specs=(blocks, P(), blocks),
        out_specs=(blocks, blocks),
        check_vma=False,
    )
```
